32 devices in a mesh: group: 4 (over y, x), shard: 8 (over z, core).
Axes of the slice: x: 2, y: 2, z: 4, core: 2. Of those that a mesh axis runs over, the one named last changes fastest.
Arguments:
- entity: float32 [16384, 400], P(('group', 'shard')), may hold values from -6 to 6
- entity_state: float32 [16384], P(('group', 'shard')), may hold values from 0.1 to 10
- relation: float32 [1345, 400], replicated, may hold values from -6 to 6
- relation_state: float32 [1345], replicated, may hold values from 10 to 1000
- src_send: int32 [32, 8, 128], P(('group', 'shard')), may hold values from 0 to 511
- dst_send: int32 [32, 8, 128], P(('group', 'shard')), may hold values from 0 to 511
- edge_source: int32 [32768], P(('group', 'shard')), may hold values from 0 to 1023
- edge_relation: int32 [32768], P(('group', 'shard')), may hold values from 0 to 1344
- edge_target: int32 [32768], P(('group', 'shard')), may hold values from 0 to 1023
- neg_slots: int32 [64, 1000], P(('group', 'shard')), may hold values from 0 to 1023
- edge_count: int32 [32], P(('group', 'shard')), may hold values from 1 to 1024, 10922 in all
Outputs:
- entity_new: float32 [16384, 400], P(('group', 'shard'))
- relation_new: float32 [1345, 400], replicated
- edge_loss: float32 [32768], P(('group', 'shard'))
The draws below stay inside these ranges and needn't reach their ends.
Inputs may be any that keep to these rules, and one draw needn't show every extreme that they name: The live edges of a device are its first edge_count slots; some device has all 1024 live.
All inputs are finite; a program needn't handle non-finite values.
Results may differ from the reference program's by a relative error of at most 0.0003.
Values sent between devices are 32-bit elements; how exact they have to be, the bound alone decides.
No kernel may reach another device: no remote copies, remote signals or barrier semaphores. Data moves between devices by JAX's collectives and lax.ppermute only.
A program may use at most 128 MiB of HBM per device.

```python
import math
import jax
import jax.numpy as jnp
import numpy as np
from jax import lax

D = 400
NEG = 1000
RELS = 1345
SPAN = 512
ROWS_DEV = 512
EDGES_DEV = 1024
TABLE = 1024
BLOCK = 128
ENTITIES = 16384
EDGES = 32768
SPANS = 64
N_GROUP = 4
N_SHARD = 8
DEVICES = 32


def draw_entity(key, part):
    values = jnp.clip(0.5 * jax.random.normal(jax.random.fold_in(key, 13), (ENTITIES, D), jnp.float32), -3.0, 3.0)
    return values


def plant(entries, key, low, high):
    place = [jax.random.randint(jax.random.fold_in(key, axis), (), 0, length) for axis, length in enumerate(entries.shape)]
    longest = entries.shape.index(max(entries.shape))
    next_to = place[:longest] + [(place[longest] + 1) % entries.shape[longest]] + place[longest + 1:]
    return entries.at[tuple(place)].set(low).at[tuple(next_to)].set(high)


def steps_of(own_key, extent, cuts, smallest, high):
    def one(axis_at, shards_of):
        steps = jax.random.uniform(jax.random.fold_in(jax.random.fold_in(own_key, 6), axis_at), (shards_of,), jnp.float32, smallest / len(cuts), high / len(cuts))
        return jnp.repeat(jnp.exp(steps), extent[axis_at] // shards_of).reshape((-1,) + (1,) * (len(extent) - axis_at - 1))

    gain = one(*cuts[0])
    for cut in cuts[1:]:
        gain = gain * one(*cut)
    return gain


def length_profile(number_of, total, reach, skew):
    weights = [(1 << 20) // math.isqrt(grade ** skew) + 1 for grade in range(2, number_of + 1)]
    rest, counts = total - reach - (number_of - 1), [1] * (number_of - 1)
    while rest > 0:
        free = [i for i in range(number_of - 1) if counts[i] < reach]
        mass, left = sum([weights[i] for i in free]), rest
        for i in free:
            extra = min(reach - counts[i], max(1, left * weights[i] // mass), rest)
            counts[i] = counts[i] + extra
            rest = rest - extra
    return np.array([reach] + counts)


def uneven_parts(own_key, amount, total, reach, slope):
    if amount == 2:
        one = jax.random.randint(own_key, (), max(1, total - reach), min(reach, total - 1) + 1)
        return jnp.stack([one, total - one])
    tallies = jnp.asarray(length_profile(amount, total, reach, slope), jnp.int32)
    twos = (amount - 1) // 2
    giver, sink = tallies[1:1 + 2 * twos:2], tallies[2:2 + 2 * twos:2]
    slack = jnp.minimum(giver - 1, reach - sink)
    moved = jax.random.randint(jax.random.fold_in(own_key, 1), (twos,), 0, 1 << 20) % (slack + 1)
    tallies = tallies.at[1:1 + 2 * twos:2].set(giver - moved).at[2:2 + 2 * twos:2].set(sink + moved)
    return tallies[jax.random.permutation(jax.random.fold_in(own_key, 2), amount)]


def noise(own_key, shape, scale, limit, kind=jnp.bfloat16):
    return jnp.clip(scale * jax.random.normal(own_key, shape, jnp.float32), -limit, limit).astype(kind)


def setup_inputs(seed: int = 0) -> dict:
    arg_keys = jax.random.split(jax.random.key(seed), 12)
    entity = draw_entity(jax.random.fold_in(arg_keys[11], 71), 0)
    entity_state = jnp.clip(jnp.exp(math.log(10.0) - 4.6051702 * jax.random.uniform(arg_keys[1], (ENTITIES,), jnp.float32) ** steps_of(arg_keys[1], (ENTITIES,), ((0, 32),), -0.2, 0.2)), 0.1, 10.0)
    relation = noise(arg_keys[2], (RELS, D), 1.0, 6.0, jnp.float32)
    relation_state = jnp.clip(jnp.exp(jax.random.uniform(arg_keys[3], (RELS,), jnp.float32, math.log(10.0), math.log(1000.0))), 10.0, 1000.0)
    src_send = plant(jax.random.randint(arg_keys[4], (DEVICES, N_SHARD, BLOCK), 0, ROWS_DEV), jax.random.fold_in(arg_keys[4], 1), 0, ROWS_DEV - 1).astype(jnp.int32)
    dst_send = plant(jax.random.randint(arg_keys[5], (DEVICES, N_SHARD, BLOCK), 0, ROWS_DEV), jax.random.fold_in(arg_keys[5], 1), 0, ROWS_DEV - 1).astype(jnp.int32)
    edge_source = plant(jax.random.randint(arg_keys[6], (EDGES,), 0, TABLE), jax.random.fold_in(arg_keys[6], 1), 0, TABLE - 1).astype(jnp.int32)
    edge_relation = plant(jax.random.randint(arg_keys[7], (EDGES,), 0, RELS), jax.random.fold_in(arg_keys[7], 1), 0, RELS - 1).astype(jnp.int32)
    edge_target = plant(jax.random.randint(arg_keys[8], (EDGES,), 0, TABLE), jax.random.fold_in(arg_keys[8], 1), 0, TABLE - 1).astype(jnp.int32)
    neg_slots = plant(jax.random.randint(arg_keys[9], (SPANS, NEG), 0, TABLE), jax.random.fold_in(arg_keys[9], 1), 0, TABLE - 1).astype(jnp.int32)
    edge_count = uneven_parts(arg_keys[10], DEVICES, DEVICES * EDGES_DEV // 3, EDGES_DEV, 2).astype(jnp.int32)
    return dict(entity=entity, entity_state=entity_state, relation=relation, relation_state=relation_state, src_send=src_send, dst_send=dst_send, edge_source=edge_source, edge_relation=edge_relation, edge_target=edge_target, neg_slots=neg_slots, edge_count=edge_count)


learn_rate = 0.5

def complex_product(multiplier, multiplicand):
    half_width = multiplier.shape[1] // 2
    first_real, first_imag = (multiplier[:, :half_width], multiplier[:, half_width:])
    second_real, second_imag = (multiplicand[:, :half_width], multiplicand[:, half_width:])
    return jnp.concatenate([first_real * second_real - first_imag * second_imag, first_real * second_imag + first_imag * second_real], axis=1)

def conj_product(multiplier, multiplicand):
    half_width = multiplier.shape[1] // 2
    first_real, first_imag = (multiplier[:, :half_width], multiplier[:, half_width:])
    second_real, second_imag = (multiplicand[:, :half_width], multiplicand[:, half_width:])
    return jnp.concatenate([first_real * second_real + first_imag * second_imag, first_imag * second_real - first_real * second_imag], axis=1)

def span_terms(queries, tail_rows, negatives, live_mask):
    pos_score = lax.optimization_barrier(jnp.sum(queries * tail_rows, axis=1))
    neg_score = jnp.dot(queries, negatives.T, precision=lax.Precision.HIGHEST)
    score_peak = jnp.maximum(pos_score, lax.optimization_barrier(jnp.max(neg_score, axis=1)))
    exp_total = jnp.exp(pos_score - score_peak) + lax.optimization_barrier(jnp.sum(jnp.exp(neg_score - score_peak[:, None]), axis=1))
    log_total = score_peak + jnp.log(exp_total)
    edge_loss = (log_total - pos_score) * live_mask
    pos_grad = (jnp.exp(pos_score - log_total) - 1.0) * live_mask
    neg_grad = jnp.exp(neg_score - log_total[:, None]) * live_mask[:, None]
    neg_query = jnp.dot(neg_grad, negatives, precision=lax.Precision.HIGHEST)
    negative_grad = lax.dot_general(neg_grad, queries, (((0,), (0,)), ((), ())), precision=lax.Precision.HIGHEST)
    return (edge_loss, pos_grad, neg_query, negative_grad)

def adagrad(params, accumulator, gradient):
    new_state = accumulator + lax.optimization_barrier(jnp.mean(gradient * gradient, axis=1))
    return params - learn_rate * gradient / jnp.sqrt(new_state)[:, None]

def reference(entity, entity_state, relation, relation_state, src_send, dst_send, edge_source, edge_relation, edge_target, neg_slots, edge_count):
    devices = N_GROUP * N_SHARD
    spans = EDGES_DEV // SPAN
    owners = jnp.arange(N_SHARD, dtype=jnp.int32)

    def device_step(carried, device):
        entity_grad, relation_grad = carried
        group_id = device // N_SHARD
        shard_id = device % N_SHARD
        next_group = (group_id + 1) % N_GROUP
        source_owner = group_id * N_SHARD + owners
        target_owner = next_group * N_SHARD + owners
        source_global = (source_owner[:, None] * ROWS_DEV + src_send[source_owner, shard_id, :]).reshape(-1)
        target_global = (target_owner[:, None] * ROWS_DEV + dst_send[target_owner, shard_id, :]).reshape(-1)
        source_table = entity[source_global]
        target_table = entity[target_global]
        first_edge = device * EDGES_DEV
        slot_source = lax.dynamic_slice_in_dim(edge_source, first_edge, EDGES_DEV)
        slot_relation = lax.dynamic_slice_in_dim(edge_relation, first_edge, EDGES_DEV)
        slot_target = lax.dynamic_slice_in_dim(edge_target, first_edge, EDGES_DEV)
        slot_negative = lax.dynamic_slice_in_dim(neg_slots, device * spans, spans, 0)
        live_mask = (jnp.arange(EDGES_DEV, dtype=jnp.int32) < edge_count[device]).astype(jnp.float32)
        head_rows = source_table[slot_source]
        tail_rows = target_table[slot_target]
        rel_rows = relation[slot_relation]
        queries = complex_product(head_rows, rel_rows)

        def per_span(position):
            first_row = position * SPAN
            return span_terms(lax.dynamic_slice_in_dim(queries, first_row, SPAN), lax.dynamic_slice_in_dim(tail_rows, first_row, SPAN), target_table[slot_negative[position]], lax.dynamic_slice_in_dim(live_mask, first_row, SPAN))
        edge_loss, pos_grad, neg_query, negative_grad = lax.map(per_span, jnp.arange(spans, dtype=jnp.int32))
        feature_count = entity.shape[1]
        edge_loss = edge_loss.reshape(-1)
        pos_grad = pos_grad.reshape(-1)
        neg_query = neg_query.reshape(EDGES_DEV, feature_count)
        negative_grad = negative_grad.reshape(spans * NEG, feature_count)
        query_grad = pos_grad[:, None] * tail_rows + neg_query
        tail_grad = pos_grad[:, None] * queries
        entity_grad = entity_grad.at[source_global[slot_source]].add(conj_product(query_grad, rel_rows))
        entity_grad = entity_grad.at[target_global[slot_target]].add(tail_grad)
        entity_grad = entity_grad.at[target_global[slot_negative.reshape(-1)]].add(negative_grad)
        relation_grad = relation_grad.at[slot_relation].add(conj_product(query_grad, head_rows))
        return ((entity_grad, relation_grad), edge_loss)
    initial = (jnp.zeros(entity.shape, jnp.float32), jnp.zeros(relation.shape, jnp.float32))
    (entity_grad, relation_grad), losses = lax.scan(device_step, initial, jnp.arange(devices, dtype=jnp.int32))
    return (adagrad(entity, entity_state, entity_grad), adagrad(relation, relation_state, relation_grad), losses.reshape(-1))
```

```python
import functools

import jax
import jax.numpy as jnp
from jax import lax
from jax.experimental import pallas as pl
from jax.experimental.pallas import tpu as pltpu
from jax.sharding import PartitionSpec as P

SPAN = 512
LANES = 128
CHUNK = 256

learn_rate = 0.5

F32, BF16, I32 = jnp.float32, jnp.bfloat16, jnp.int32
WHOLE = pl.BlockSpec(memory_space=pltpu.VMEM)
VMEM_LIMIT = 60 << 20


def params():
    return pltpu.CompilerParams(vmem_limit_bytes=VMEM_LIMIT, dimension_semantics=("arbitrary",))


def cost(flops, moved):
    return pl.CostEstimate(flops=flops, bytes_accessed=moved, transcendentals=0)


def split2(x):
    hi = x.astype(BF16)
    return hi, (x - hi.astype(F32)).astype(BF16)


def split3(x):
    hi = x.astype(BF16)
    rest = x - hi.astype(F32)
    mid = rest.astype(BF16)
    return hi, mid, (rest - mid.astype(F32)).astype(BF16)


def dot(a, b):
    return jnp.dot(a, b, preferred_element_type=F32)


def dot_nt(a, b):
    return lax.dot_general(a, b, (((1,), (1,)), ((), ())), preferred_element_type=F32)


def one_hot(mask):
    return jnp.where(mask, 1.0, 0.0).astype(BF16)


def rows_hot(length, slots):
    return one_hot(lax.broadcasted_iota(I32, (length, slots.shape[1]), 0) == slots)


def columns_hot(slots, length):
    return one_hot(lax.broadcasted_iota(I32, (slots.shape[0], length), 1) == slots)


def complex_product(a, b):
    half = a.shape[0] // 2
    ar, ai, br, bi = a[:half], a[half:], b[:half], b[half:]
    return jnp.concatenate([ar * br - ai * bi, ar * bi + ai * br], axis=0)


def conj_product(a, b):
    half = a.shape[0] // 2
    ar, ai, br, bi = a[:half], a[half:], b[:half], b[half:]
    return jnp.concatenate([ar * br + ai * bi, ai * br - ar * bi], axis=0)


def pick_kernel(rows_ref, slots_ref, out_ref, pieces):
    block = out_ref.shape[2]

    @pl.when(pl.program_id(0) == 0)
    def _():
        pieces[0], pieces[1], pieces[2] = split3(rows_ref[...])

    hot = rows_hot(rows_ref.shape[1], slots_ref[...])
    picked = dot(pieces[0], hot) + dot(pieces[1], hot) + dot(pieces[2], hot)
    for i in range(CHUNK // block):
        out_ref[i] = picked[:, i * block:(i + 1) * block]


def pick_blocks(rows, slots, peers, block):
    features, length = rows.shape
    steps = peers * block // CHUNK
    return pl.pallas_call(
        pick_kernel,
        grid=(steps,),
        in_specs=[
            pl.BlockSpec((features, length), lambda i: (0, 0)),
            pl.BlockSpec((1, CHUNK), lambda i: (0, i)),
        ],
        out_specs=pl.BlockSpec((CHUNK // block, features, block), lambda i: (i, 0, 0)),
        out_shape=jax.ShapeDtypeStruct((peers, features, block), F32),
        scratch_shapes=[pltpu.VMEM((3, features, length), BF16)],
        compiler_params=params(),
        cost_estimate=cost(6 * features * length * peers * block, 8 * features * peers * block),
        name="pick",
    )(rows, slots)


def relation_kernel(rel_ref, edge_rel_ref, out_ref, pieces):
    count = rel_ref.shape[1]
    padded = pieces.shape[2]

    @pl.when(pl.program_id(0) == 0)
    def _():
        features = rel_ref.shape[0]
        tail = padded - count // LANES * LANES
        for piece, value in enumerate(split3(rel_ref[...])):
            pieces[piece, :, padded - tail:] = jnp.zeros((features, tail), BF16)
            pieces[piece, :, :count] = value

    hot = rows_hot(padded, edge_rel_ref[...])
    out_ref[...] = dot(pieces[0], hot) + dot(pieces[1], hot) + dot(pieces[2], hot)


def relation_rows(relation, edge_relation):
    features, count = relation.shape
    edges = edge_relation.shape[1]
    padded = pl.cdiv(count, LANES) * LANES
    return pl.pallas_call(
        relation_kernel,
        grid=(edges // CHUNK,),
        in_specs=[
            pl.BlockSpec((features, count), lambda i: (0, 0)),
            pl.BlockSpec((1, CHUNK), lambda i: (0, i)),
        ],
        out_specs=pl.BlockSpec((features, CHUNK), lambda i: (0, i)),
        out_shape=jax.ShapeDtypeStruct((features, edges), F32),
        scratch_shapes=[pltpu.VMEM((3, features, padded), BF16)],
        compiler_params=params(),
        cost_estimate=cost(6 * features * padded * edges, 8 * features * edges),
        name="relation_rows",
    )(relation, edge_relation)


def count_kernel(slots_ref, out_ref):
    table_rows = out_ref.shape[2]
    hits = lax.broadcasted_iota(I32, (slots_ref.shape[1], table_rows), 1) == slots_ref[0]
    out_ref[0] = jnp.sum(jnp.where(hits, 1.0, 0.0), axis=0, keepdims=True)


def slot_counts(neg_slots, table_rows):
    spans, negatives = neg_slots.shape
    return pl.pallas_call(
        count_kernel,
        grid=(spans,),
        in_specs=[pl.BlockSpec((1, negatives, 1), lambda i: (i, 0, 0))],
        out_specs=pl.BlockSpec((1, 1, table_rows), lambda i: (i, 0, 0)),
        out_shape=jax.ShapeDtypeStruct((spans, 1, table_rows), F32),
        compiler_params=params(),
        cost_estimate=cost(2 * spans * negatives * table_rows, 512 * spans * negatives),
        name="slot_counts",
    )(neg_slots[:, :, None])


def query_kernel(source_ref, edge_source_ref, rels_ref, heads_ref, columns_ref, rows_ref, pieces):
    peers, features, block = source_ref.shape

    @pl.when(pl.program_id(0) == 0)
    def _():
        for p in range(peers):
            for piece, value in enumerate(split3(source_ref[p])):
                pieces[piece, :, p * block:(p + 1) * block] = value

    hot = rows_hot(peers * block, edge_source_ref[...])
    heads = dot(pieces[0], hot) + dot(pieces[1], hot) + dot(pieces[2], hot)
    heads_ref[...] = heads
    queries = complex_product(heads, rels_ref[...])
    columns_ref[0], columns_ref[1] = split2(queries)
    rows_ref[0], rows_ref[1] = split2(queries.T)


def query_rows(source_blocks, edge_source, rels):
    peers, features, block = source_blocks.shape
    edges = edge_source.shape[1]
    return pl.pallas_call(
        query_kernel,
        grid=(edges // CHUNK,),
        in_specs=[
            pl.BlockSpec((peers, features, block), lambda i: (0, 0, 0)),
            pl.BlockSpec((1, CHUNK), lambda i: (0, i)),
            pl.BlockSpec((features, CHUNK), lambda i: (0, i)),
        ],
        out_specs=[
            pl.BlockSpec((features, CHUNK), lambda i: (0, i)),
            pl.BlockSpec((2, features, CHUNK), lambda i: (0, 0, i)),
            pl.BlockSpec((2, CHUNK, features), lambda i: (0, i, 0)),
        ],
        out_shape=[
            jax.ShapeDtypeStruct((features, edges), F32),
            jax.ShapeDtypeStruct((2, features, edges), BF16),
            jax.ShapeDtypeStruct((2, edges, features), BF16),
        ],
        scratch_shapes=[pltpu.VMEM((3, features, peers * block), BF16)],
        compiler_params=params(),
        cost_estimate=cost(6 * features * peers * block * edges, 20 * features * edges),
        name="query_rows",
    )(source_blocks, edge_source, rels)


def score_kernel(
    live_ref, target_ref, rows_ref, columns_ref, counts_ref, edge_target_ref,
    loss_ref, grad_ref, table_ref, table_grad_ref, total,
):
    peers, features, block = target_ref.shape
    step = pl.program_id(0)

    @pl.when(step == 0)
    def _():
        total[...] = jnp.zeros_like(total)
        for p in range(peers):
            for piece, value in enumerate(split2(target_ref[p])):
                table_ref[piece, :, p * block:(p + 1) * block] = value

    score = (
        dot(rows_ref[0], table_ref[0]) + dot(rows_ref[0], table_ref[1]) + dot(rows_ref[1], table_ref[0])
    )
    counts = counts_ref[0]
    own = lax.broadcasted_iota(I32, score.shape, 1) == edge_target_ref[...]
    pos = jnp.sum(jnp.where(own, score, 0.0), axis=1, keepdims=True)
    peak = jnp.max(jnp.where(counts > 0.0, score, -jnp.inf), axis=1, keepdims=True)
    peak = jnp.maximum(pos, peak)
    weight = counts * jnp.exp(jnp.minimum(score - peak, 0.0))
    pos_weight = jnp.exp(pos - peak)
    sum_all = pos_weight + jnp.sum(weight, axis=1, keepdims=True)
    edge = step * CHUNK + lax.broadcasted_iota(I32, (CHUNK, 1), 0)
    live = jnp.where(edge < live_ref[0], 1.0, 0.0)
    loss_ref[...] = (peak - pos + jnp.log(sum_all)) * live
    scale = live / sum_all
    pos_grad = pos_weight * scale - live
    grad = weight * scale + jnp.where(own, pos_grad, 0.0)
    hi, lo = split2(grad)
    grad_ref[0], grad_ref[1] = hi, lo
    total[...] += dot(columns_ref[0], hi) + dot(columns_ref[0], lo) + dot(columns_ref[1], hi)

    @pl.when(step == pl.num_programs(0) - 1)
    def _():
        for p in range(peers):
            table_grad_ref[p] = total[:, p * block:(p + 1) * block]


def score_spans(live, target_blocks, query_rows_, query_columns, counts, edge_target):
    peers, features, block = target_blocks.shape
    edges = edge_target.shape[0]
    table_rows = peers * block
    per_span = SPAN // CHUNK
    return pl.pallas_call(
        score_kernel,
        grid=(edges // CHUNK,),
        in_specs=[
            pl.BlockSpec(memory_space=pltpu.SMEM),
            pl.BlockSpec((peers, features, block), lambda i: (0, 0, 0)),
            pl.BlockSpec((2, CHUNK, features), lambda i: (0, i, 0)),
            pl.BlockSpec((2, features, CHUNK), lambda i: (0, 0, i)),
            pl.BlockSpec((1, 1, table_rows), lambda i: (i // per_span, 0, 0)),
            pl.BlockSpec((CHUNK, 1), lambda i: (i, 0)),
        ],
        out_specs=[
            pl.BlockSpec((CHUNK, 1), lambda i: (i, 0)),
            pl.BlockSpec((2, CHUNK, table_rows), lambda i: (0, i, 0)),
            pl.BlockSpec((2, features, table_rows), lambda i: (0, 0, 0)),
            pl.BlockSpec((peers, features, block), lambda i: (0, 0, 0)),
        ],
        out_shape=[
            jax.ShapeDtypeStruct((edges, 1), F32),
            jax.ShapeDtypeStruct((2, edges, table_rows), BF16),
            jax.ShapeDtypeStruct((2, features, table_rows), BF16),
            jax.ShapeDtypeStruct((peers, features, block), F32),
        ],
        scratch_shapes=[pltpu.VMEM((features, table_rows), F32)],
        compiler_params=params(),
        cost_estimate=cost(12 * features * table_rows * edges, 30 * features * edges),
        name="score_spans",
    )(live, target_blocks, query_rows_, query_columns, counts, edge_target)


def edge_grad_kernel(
    table_ref, grad_ref, heads_ref, rels_ref, edge_rel_ref, edge_source_ref,
    rel_grad_ref, source_grad_ref, rel_total, source_total,
):
    step = pl.program_id(0)
    parts, _, width = rel_grad_ref.shape
    peers, _, block = source_grad_ref.shape

    @pl.when(step == 0)
    def _():
        rel_total[...] = jnp.zeros_like(rel_total)
        source_total[...] = jnp.zeros_like(source_total)

    query_grad = (
        dot_nt(table_ref[0], grad_ref[0]) + dot_nt(table_ref[0], grad_ref[1]) + dot_nt(table_ref[1], grad_ref[0])
    )
    hi, lo = split2(conj_product(query_grad, heads_ref[...]))
    hot = columns_hot(edge_rel_ref[...], parts * width)
    rel_total[...] += dot(hi, hot) + dot(lo, hot)
    hi, lo = split2(conj_product(query_grad, rels_ref[...]))
    hot = columns_hot(edge_source_ref[...], peers * block)
    source_total[...] += dot(hi, hot) + dot(lo, hot)

    @pl.when(step == pl.num_programs(0) - 1)
    def _():
        for p in range(parts):
            rel_grad_ref[p] = rel_total[:, p * width:(p + 1) * width]
        for p in range(peers):
            source_grad_ref[p] = source_total[:, p * block:(p + 1) * block]


def edge_grads(table, grad, heads, rels, edge_relation, edge_source, parts, width, peers, block):
    _, features, table_rows = table.shape
    edges = heads.shape[1]
    return pl.pallas_call(
        edge_grad_kernel,
        grid=(edges // CHUNK,),
        in_specs=[
            pl.BlockSpec((2, features, table_rows), lambda i: (0, 0, 0)),
            pl.BlockSpec((2, CHUNK, table_rows), lambda i: (0, i, 0)),
            pl.BlockSpec((features, CHUNK), lambda i: (0, i)),
            pl.BlockSpec((features, CHUNK), lambda i: (0, i)),
            pl.BlockSpec((CHUNK, 1), lambda i: (i, 0)),
            pl.BlockSpec((CHUNK, 1), lambda i: (i, 0)),
        ],
        out_specs=[
            pl.BlockSpec((parts, features, width), lambda i: (0, 0, 0)),
            pl.BlockSpec((peers, features, block), lambda i: (0, 0, 0)),
        ],
        out_shape=[
            jax.ShapeDtypeStruct((parts, features, width), F32),
            jax.ShapeDtypeStruct((peers, features, block), F32),
        ],
        scratch_shapes=[
            pltpu.VMEM((features, parts * width), F32),
            pltpu.VMEM((features, peers * block), F32),
        ],
        compiler_params=params(),
        cost_estimate=cost(16 * features * table_rows * edges, 30 * features * edges),
        name="edge_grads",
    )(table, grad, heads, rels, edge_relation, edge_source)


def put_back(received_ref, slots_ref, rows):
    peers, _, block = received_ref.shape
    total = None
    for p in range(peers):
        hi, lo = split2(received_ref[p])
        hot = columns_hot(slots_ref[p * block:(p + 1) * block, :], rows)
        term = dot(hi, hot) + dot(lo, hot)
        total = term if total is None else total + term
    return total


def target_home_kernel(received_ref, slots_ref, out_ref):
    out_ref[...] = put_back(received_ref, slots_ref, out_ref.shape[1])


def target_home(received, slots, rows):
    features = received.shape[1]
    return pl.pallas_call(
        target_home_kernel,
        in_specs=[WHOLE, WHOLE],
        out_specs=WHOLE,
        out_shape=jax.ShapeDtypeStruct((features, rows), F32),
        compiler_params=pltpu.CompilerParams(vmem_limit_bytes=VMEM_LIMIT),
        cost_estimate=cost(4 * features * rows * slots.shape[0], 8 * features * slots.shape[0]),
        name="target_home",
    )(received, slots)


def adagrad(params_, state, gradient):
    new_state = state + jnp.mean(gradient * gradient, axis=0, keepdims=True)
    return params_ - learn_rate * gradient / jnp.sqrt(new_state)


def entity_kernel(received_ref, slots_ref, other_ref, entity_ref, state_ref, out_ref):
    gradient = other_ref[...] + put_back(received_ref, slots_ref, out_ref.shape[1])
    out_ref[...] = adagrad(entity_ref[...], state_ref[...], gradient)


def entity_update(received, slots, other, entity, state):
    features, rows = entity.shape
    return pl.pallas_call(
        entity_kernel,
        in_specs=[WHOLE] * 5,
        out_specs=WHOLE,
        out_shape=jax.ShapeDtypeStruct((features, rows), F32),
        compiler_params=pltpu.CompilerParams(vmem_limit_bytes=VMEM_LIMIT),
        cost_estimate=cost(4 * features * rows * slots.shape[0], 8 * features * slots.shape[0]),
        name="entity_update",
    )(received, slots, other, entity, state)


def swapped(value, axis, bit):
    count = lax.axis_size(axis)
    return lax.ppermute(value, axis, [(i, i ^ bit) for i in range(count)])


def passed_along(value, axis, by):
    count = lax.axis_size(axis)
    return lax.ppermute(value, axis, [(i, (i + by) % count) for i in range(count)])


def relation_sum(parts):
    groups, features, width = parts.shape
    half = features // 2
    shards = lax.axis_size("shard")
    chips = shards // 2
    core = lax.axis_index("shard") % 2
    lines = [[chip * 2 + c for chip in range(chips)] for c in range(2)]
    halves = parts.reshape(groups, 2, half, width)
    kept = lax.dynamic_index_in_dim(halves, core, 1, keepdims=False)
    sent = lax.dynamic_index_in_dim(halves, 1 - core, 1, keepdims=False)
    mine = kept + swapped(sent, "shard", 1)
    mine = jnp.sum(lax.all_to_all(mine, "group", 0, 0, tiled=True), axis=0)
    slices = mine.reshape(chips, half // chips, width)
    slices = lax.all_to_all(slices, "shard", 0, 0, axis_index_groups=lines, tiled=True)
    piece = jnp.sum(slices, axis=0)
    slices = lax.all_to_all(
        jnp.broadcast_to(piece[None], slices.shape), "shard", 0, 0, axis_index_groups=lines, tiled=True
    )
    mine = slices.reshape(half, width)
    mine = lax.all_to_all(
        jnp.broadcast_to(mine[None], (groups, half, width)), "group", 0, 0, tiled=True
    )
    other = swapped(mine, "shard", 1)
    low = jnp.where(core == 0, mine, other)
    high = jnp.where(core == 0, other, mine)
    return jnp.concatenate([low, high], axis=1).transpose(1, 0, 2).reshape(features, groups * width)


def on_device(
    entity, entity_state, relation, relation_state, src_send, dst_send,
    edge_source, edge_relation, edge_target, neg_slots, edge_count,
):
    rows, features = entity.shape
    relations = relation.shape[0]
    peers, block = src_send.shape[1:]
    edges = edge_source.shape[0]
    table_rows = peers * block
    groups = lax.axis_size("group")
    width = pl.cdiv(relations, groups * LANES) * LANES
    entity_t, relation_t = entity.T, relation.T

    exchange = functools.partial(
        lax.all_to_all, axis_name="shard", split_axis=0, concat_axis=0, tiled=True
    )
    source_blocks = exchange(pick_blocks(entity_t, src_send.reshape(1, -1), peers, block))
    shifted = passed_along(pick_blocks(entity_t, dst_send.reshape(1, -1), peers, block), "group", -1)
    target_blocks = exchange(shifted)
    rels = relation_rows(relation_t, edge_relation.reshape(1, -1))
    counts = slot_counts(neg_slots, table_rows)
    heads, query_columns, query_rows_ = query_rows(source_blocks, edge_source.reshape(1, -1), rels)
    loss, grad, table, table_grad = score_spans(
        edge_count, target_blocks, query_rows_, query_columns, counts, edge_target.reshape(-1, 1)
    )
    home = passed_along(exchange(table_grad), "group", 1)
    rel_parts, source_grad = edge_grads(
        table, grad, heads, rels, edge_relation.reshape(-1, 1), edge_source.reshape(-1, 1),
        groups, width, peers, block,
    )
    rel_total = relation_sum(rel_parts)[:, :relations]
    returned = exchange(source_grad)
    target_part = target_home(home, dst_send.reshape(-1, 1), rows)
    entity_new = entity_update(
        returned, src_send.reshape(-1, 1), target_part, entity_t, entity_state.reshape(1, -1)
    )
    relation_new = adagrad(relation_t, relation_state.reshape(1, -1), rel_total)
    return entity_new.T, relation_new.T, loss.reshape(-1)


def solution(mesh):
    both = ("group", "shard")
    return jax.shard_map(
        on_device,
        mesh=mesh,
        in_specs=(
            P(both, None), P(both), P(), P(), P(both, None, None), P(both, None, None),
            P(both), P(both), P(both), P(both, None), P(both),
        ),
        out_specs=(P(both, None), P(), P(both)),
        check_vma=False,
    )
```

```python
import functools

import jax
import jax.numpy as jnp
from jax import lax
from jax.experimental import pallas as pl
from jax.experimental.pallas import tpu as pltpu
from jax.sharding import PartitionSpec as P

SPAN = 512
LANES = 128
CHUNK = 256
WIDE = 512


learn_rate = 0.5

F32, BF16, I32 = jnp.float32, jnp.bfloat16, jnp.int32
VMEM = pl.BlockSpec(memory_space=pltpu.VMEM)
SMEM = pl.BlockSpec(memory_space=pltpu.SMEM)
VMEM_LIMIT = 60 << 20


def kernel_call(kernel, name, outs, flops, moved, **kw):
    semantics = ("arbitrary",) if "grid" in kw else None
    return pl.pallas_call(
        kernel,
        out_shape=outs,
        compiler_params=pltpu.CompilerParams(
            vmem_limit_bytes=VMEM_LIMIT, dimension_semantics=semantics
        ),
        cost_estimate=pl.CostEstimate(flops=flops, bytes_accessed=moved, transcendentals=0),
        name=name,
        **kw,
    )


def shape(dims, dtype=F32):
    return jax.ShapeDtypeStruct(dims, dtype)


def held(dims):
    return pl.BlockSpec(dims, lambda i: (0,) * len(dims))


def split2(x):
    hi = x.astype(BF16)
    return hi, (x - hi.astype(F32)).astype(BF16)


def split3(x):
    hi = x.astype(BF16)
    rest = x - hi.astype(F32)
    mid = rest.astype(BF16)
    return hi, mid, (rest - mid.astype(F32)).astype(BF16)


def dot(a, b):
    return jnp.dot(a, b, preferred_element_type=F32)


def dot_nt(a, b):
    return lax.dot_general(a, b, (((1,), (1,)), ((), ())), preferred_element_type=F32)


def one_hot(mask):
    return jnp.where(mask, 1.0, 0.0).astype(BF16)


def rows_hot(length, slots):
    return one_hot(lax.broadcasted_iota(I32, (length, slots.shape[1]), 0) == slots)


def columns_hot(slots, length):
    return one_hot(lax.broadcasted_iota(I32, (slots.shape[0], length), 1) == slots)


def complex_product(a, b):
    half = a.shape[0] // 2
    ar, ai, br, bi = a[:half], a[half:], b[:half], b[half:]
    return jnp.concatenate([ar * br - ai * bi, ar * bi + ai * br], axis=0)


def conj_product(a, b):
    half = a.shape[0] // 2
    ar, ai, br, bi = a[:half], a[half:], b[:half], b[half:]
    return jnp.concatenate([ar * br + ai * bi, ai * br - ar * bi], axis=0)


def hops(peers):
    chips = peers // 2
    ahead = [(k, b) for k in range(1, chips) for b in (0, 1)]
    return ahead + [(0, 1), (0, 0)]


def partner(me, hop, peers, sign):
    chips = peers // 2
    return (me // 2 + sign * hop[0]) % chips * 2 + (me % 2 + hop[1]) % 2


def places_of(me, owner, peers):
    chips = peers // 2
    k = (me // 2 - owner // 2) % chips
    b = (me + owner) % 2
    return (k - 1) % chips * 2 + jnp.where(k == 0, 1 - b, b)


def pick_kernel(order_ref, rows_ref, slots_ref, *outs):
    hi, mid, lo = split3(rows_ref[...])
    block = slots_ref.shape[1]
    together = max(1, CHUNK // block)
    for first in range(0, len(outs), together):
        group = outs[first:first + together]
        slots = [slots_ref[pl.ds(order_ref[first + i], 1), :] for i in range(len(group))]
        hot = rows_hot(rows_ref.shape[1], jnp.concatenate(slots, axis=1))
        picked = dot(hi, hot) + dot(mid, hot) + dot(lo, hot)
        for i, out in enumerate(group):
            out[...] = picked[:, i * block:(i + 1) * block]


def pick_blocks(order, rows, slots):
    features, length = rows.shape
    block = slots.shape[1]
    count = order.shape[0]
    return kernel_call(
        pick_kernel, "pick", [shape((features, block))] * count,
        6 * features * length * count * block, 8 * features * count * block,
        in_specs=[SMEM, VMEM, VMEM], out_specs=[VMEM] * count,
    )(order, rows, slots)


def relation_kernel(rel_ref, edge_rel_ref, out_ref, pieces):
    count = rel_ref.shape[1]
    padded = pieces.shape[2]

    @pl.when(pl.program_id(0) == 0)
    def _():
        features = rel_ref.shape[0]
        tail = padded - count // LANES * LANES
        for piece, value in enumerate(split3(rel_ref[...])):
            pieces[piece, :, padded - tail:] = jnp.zeros((features, tail), BF16)
            pieces[piece, :, :count] = value

    hot = rows_hot(padded, edge_rel_ref[...])
    out_ref[...] = dot(pieces[0], hot) + dot(pieces[1], hot) + dot(pieces[2], hot)


def relation_rows(relation, edge_relation):
    features, count = relation.shape
    edges = edge_relation.shape[1]
    padded = pl.cdiv(count, LANES) * LANES
    return kernel_call(
        relation_kernel, "relation_rows", shape((features, edges)),
        6 * features * padded * edges, 8 * features * edges,
        grid=(edges // CHUNK,),
        in_specs=[held((features, count)), pl.BlockSpec((1, CHUNK), lambda i: (0, i))],
        out_specs=pl.BlockSpec((features, CHUNK), lambda i: (0, i)),
        scratch_shapes=[pltpu.VMEM((3, features, padded), BF16)],
    )(relation, edge_relation)


def count_kernel(slots_ref, out_ref):
    table_rows = out_ref.shape[2]
    hits = lax.broadcasted_iota(I32, (slots_ref.shape[1], table_rows), 1) == slots_ref[0]
    out_ref[0] = jnp.sum(jnp.where(hits, 1.0, 0.0), axis=0, keepdims=True)


def slot_counts(neg_slots, table_rows):
    spans, negatives = neg_slots.shape
    return kernel_call(
        count_kernel, "slot_counts", shape((spans, 1, table_rows)),
        2 * spans * negatives * table_rows, 512 * spans * negatives,
        grid=(spans,),
        in_specs=[pl.BlockSpec((1, negatives, 1), lambda i: (i, 0, 0))],
        out_specs=pl.BlockSpec((1, 1, table_rows), lambda i: (i, 0, 0)),
    )(neg_slots[:, :, None])


def hot_kernel(order_ref, slots_ref, out_ref):
    peers, block, _ = slots_ref.shape
    for j in range(peers):
        out_ref[j * block:(j + 1) * block, :] = columns_hot(slots_ref[order_ref[j]], out_ref.shape[1])


def home_hots(order, slots, rows):
    peers, block = slots.shape
    return kernel_call(
        hot_kernel, "home_hots", shape((peers * block, rows), BF16),
        2 * peers * block * rows, 2 * peers * block * rows,
        in_specs=[SMEM, VMEM], out_specs=VMEM,
    )(order, slots[:, :, None])


def query_kernel(*refs):
    edge_source_ref, rels_ref, *blocks = refs[:-4]
    heads_ref, columns_ref, rows_ref, pieces = refs[-4:]
    block = blocks[0].shape[1]

    @pl.when(pl.program_id(0) == 0)
    def _():
        for p, ref in enumerate(blocks):
            for piece, value in enumerate(split3(ref[...])):
                pieces[piece, :, p * block:(p + 1) * block] = value

    hot = rows_hot(pieces.shape[2], edge_source_ref[...])
    heads = dot(pieces[0], hot) + dot(pieces[1], hot) + dot(pieces[2], hot)
    heads_ref[...] = heads
    queries = complex_product(heads, rels_ref[...])
    hi, lo = split2(queries)
    columns_ref[0], columns_ref[1] = hi, lo
    hi, lo = split2(queries.T)
    rows_ref[...] = jnp.concatenate([hi, hi, lo], axis=1)


def query_rows(blocks, edge_source, rels):
    peers = len(blocks)
    features, block = blocks[0].shape
    edges = edge_source.shape[1]
    return kernel_call(
        query_kernel, "query_rows",
        [shape((features, edges)), shape((2, features, edges), BF16), shape((edges, 3 * features), BF16)],
        6 * features * peers * block * edges, 20 * features * edges,
        grid=(edges // CHUNK,),
        in_specs=[
            pl.BlockSpec((1, CHUNK), lambda i: (0, i)),
            pl.BlockSpec((features, CHUNK), lambda i: (0, i)),
        ] + [held((features, block))] * peers,
        out_specs=[
            pl.BlockSpec((features, CHUNK), lambda i: (0, i)),
            pl.BlockSpec((2, features, CHUNK), lambda i: (0, 0, i)),
            pl.BlockSpec((CHUNK, 3 * features), lambda i: (i, 0)),
        ],
        scratch_shapes=[pltpu.VMEM((3, features, peers * block), BF16)],
    )(edge_source, rels, *blocks)


def score_kernel(peers, *refs):
    live_ref, rows_ref, columns_ref, counts_ref, edge_target_ref = refs[:5]
    blocks = refs[5:5 + peers]
    loss_ref, grad_ref, table_ref = refs[5 + peers:8 + peers]
    block_grads = refs[8 + peers:8 + 2 * peers]
    total, = refs[8 + 2 * peers:]
    features, block = blocks[0].shape
    step = pl.program_id(0)

    @pl.when(step == 0)
    def _():
        total[...] = jnp.zeros_like(total)
        for p, ref in enumerate(blocks):
            hi, lo = split2(ref[...])
            at = pl.ds(p * block, block)
            table_ref[:features, at] = hi
            table_ref[features:2 * features, at] = lo
            table_ref[2 * features:, at] = hi

    score = dot(rows_ref[...], table_ref[...])
    counts = counts_ref[0]
    own = lax.broadcasted_iota(I32, score.shape, 1) == edge_target_ref[...]
    pos = jnp.sum(jnp.where(own, score, 0.0), axis=1, keepdims=True)
    peak = jnp.max(jnp.where(counts > 0.0, score, -jnp.inf), axis=1, keepdims=True)
    peak = jnp.maximum(pos, peak)
    weight = counts * jnp.exp(jnp.minimum(score - peak, 0.0))
    pos_weight = jnp.exp(pos - peak)
    sum_all = pos_weight + jnp.sum(weight, axis=1, keepdims=True)
    edge = step * score.shape[0] + lax.broadcasted_iota(I32, pos.shape, 0)
    live = jnp.where(edge < live_ref[0], 1.0, 0.0)
    loss_ref[...] = (peak - pos + jnp.log(sum_all)) * live
    scale = live / sum_all
    pos_grad = pos_weight * scale - live
    grad = weight * scale + jnp.where(own, pos_grad, 0.0)
    hi, lo = split2(grad)
    grad_ref[0], grad_ref[1] = hi, lo
    total[...] += dot(columns_ref[0], hi) + dot(columns_ref[0], lo) + dot(columns_ref[1], hi)

    @pl.when(step == pl.num_programs(0) - 1)
    def _():
        for p, ref in enumerate(block_grads):
            ref[...] = total[:, p * block:(p + 1) * block]


def score_spans(live, blocks, rows, columns, counts, edge_target):
    peers = len(blocks)
    features, block = blocks[0].shape
    edges = edge_target.shape[0]
    table_rows = peers * block
    chunk = CHUNK
    per_span = SPAN // chunk
    return kernel_call(
        functools.partial(score_kernel, peers), "score_spans",
        [
            shape((edges, 1)),
            shape((2, edges, table_rows), BF16),
            shape((3 * features, table_rows), BF16),
        ] + [shape((features, block))] * peers,
        12 * features * table_rows * edges, 30 * features * edges,
        grid=(edges // chunk,),
        in_specs=[
            SMEM,
            pl.BlockSpec((chunk, 3 * features), lambda i: (i, 0)),
            pl.BlockSpec((2, features, chunk), lambda i: (0, 0, i)),
            pl.BlockSpec((1, 1, table_rows), lambda i: (i // per_span, 0, 0)),
            pl.BlockSpec((chunk, 1), lambda i: (i, 0)),
        ] + [held((features, block))] * peers,
        out_specs=[
            pl.BlockSpec((chunk, 1), lambda i: (i, 0)),
            pl.BlockSpec((2, chunk, table_rows), lambda i: (0, i, 0)),
            held((3 * features, table_rows)),
        ] + [held((features, block))] * peers,
        scratch_shapes=[pltpu.VMEM((features, table_rows), F32)],
    )(live, rows, columns, counts, edge_target, *blocks)


def relation_grad_kernel(
    me_ref, table_ref, grad_ref, heads_ref, rels_ref, edge_rel_ref, source_ref, *refs
):
    outs, total = refs[:-1], refs[-1]
    groups = len(outs) // 2
    half, width = outs[0].shape
    step = pl.program_id(0)

    @pl.when(step == 0)
    def _():
        total[...] = jnp.zeros_like(total)

    features = heads_ref.shape[0]
    hi, lo = table_ref[:features], table_ref[features:2 * features]
    query_grad = dot_nt(hi, grad_ref[0]) + dot_nt(hi, grad_ref[1]) + dot_nt(lo, grad_ref[0])
    source_ref[0], source_ref[1] = split2(conj_product(query_grad, rels_ref[...]))
    hi, lo = split2(conj_product(query_grad, heads_ref[...]))
    hot = columns_hot(edge_rel_ref[...], total.shape[1])
    total[...] += dot(hi, hot) + dot(lo, hot)

    @pl.when(step == pl.num_programs(0) - 1)
    def _():
        group, core = me_ref[0], me_ref[1]
        for j in range(groups):
            at = pl.ds(pl.multiple_of((group ^ j) * width, LANES), width)
            outs[j][...] = total[pl.ds(pl.multiple_of(core * half, 8), half), at]
            outs[groups + j][...] = total[pl.ds(pl.multiple_of((1 - core) * half, 8), half), at]


def relation_grads(me, table, grad, heads, rels, edge_relation, groups, width):
    features, edges = heads.shape
    table_rows = table.shape[1]
    chunk = CHUNK
    return kernel_call(
        relation_grad_kernel, "relation_grads",
        [shape((2, features, edges), BF16)] + [shape((features // 2, width))] * (2 * groups),
        10 * features * table_rows * edges, 30 * features * edges,
        grid=(edges // chunk,),
        in_specs=[
            SMEM,
            held((3 * features, table_rows)),
            pl.BlockSpec((2, chunk, table_rows), lambda i: (0, i, 0)),
            pl.BlockSpec((features, chunk), lambda i: (0, i)),
            pl.BlockSpec((features, chunk), lambda i: (0, i)),
            pl.BlockSpec((chunk, 1), lambda i: (i, 0)),
        ],
        out_specs=[pl.BlockSpec((2, features, chunk), lambda i: (0, 0, i))]
        + [held((features // 2, width))] * (2 * groups),
        scratch_shapes=[pltpu.VMEM((features, groups * width), F32)],
    )(me, table, grad, heads, rels, edge_relation)


def source_grad_kernel(rows_ref, edge_source_ref, *refs):
    outs, total = refs[:-1], refs[-1]
    block = outs[0].shape[1]
    step = pl.program_id(0)

    @pl.when(step == 0)
    def _():
        total[...] = jnp.zeros_like(total)

    hot = columns_hot(edge_source_ref[...], total.shape[1])
    total[...] += dot(rows_ref[0], hot) + dot(rows_ref[1], hot)

    @pl.when(step == pl.num_programs(0) - 1)
    def _():
        for p, ref in enumerate(outs):
            ref[...] = total[:, p * block:(p + 1) * block]


def source_grads(rows, edge_source, peers, block):
    _, features, edges = rows.shape
    return kernel_call(
        source_grad_kernel, "source_grads", [shape((features, block))] * peers,
        4 * features * peers * block * edges, 12 * features * edges,
        grid=(edges // CHUNK,),
        in_specs=[
            pl.BlockSpec((2, features, CHUNK), lambda i: (0, 0, i)),
            pl.BlockSpec((CHUNK, 1), lambda i: (i, 0)),
        ],
        out_specs=[held((features, block))] * peers,
        scratch_shapes=[pltpu.VMEM((features, peers * block), F32)],
    )(rows, edge_source)


def put_back(blocks, hot_ref):
    hi, lo = split2(jnp.concatenate([ref[...] for ref in blocks], axis=1))
    return dot(hi, hot_ref[...]) + dot(lo, hot_ref[...])


def target_home_kernel(hot_ref, *refs):
    refs[-1][...] = put_back(refs[:-1], hot_ref)


def target_home(hots, blocks):
    features = blocks[0].shape[0]
    rows = hots.shape[1]
    return kernel_call(
        target_home_kernel, "target_home", shape((features, rows)),
        4 * features * rows * hots.shape[0], 8 * features * hots.shape[0],
        in_specs=[VMEM] * (1 + len(blocks)), out_specs=VMEM,
    )(hots, *blocks)


def adagrad(params, state, gradient):
    new_state = state + jnp.mean(gradient * gradient, axis=0, keepdims=True)
    return params - learn_rate * gradient / jnp.sqrt(new_state)


def entity_kernel(other_ref, entity_ref, state_ref, hot_ref, *refs):
    gradient = other_ref[...] + put_back(refs[:-1], hot_ref)
    refs[-1][...] = adagrad(entity_ref[...], state_ref[...], gradient)


def entity_update(hots, blocks, other, entity, state):
    features, rows = entity.shape
    return kernel_call(
        entity_kernel, "entity_update", shape((features, rows)),
        4 * features * rows * hots.shape[0], 8 * features * hots.shape[0],
        in_specs=[VMEM] * (4 + len(blocks)), out_specs=VMEM,
    )(other, entity, state, hots, *blocks)


def cut_kernel(me_ref, *refs):
    chips = me_ref.shape[0]
    terms, outs, whole = refs[:-1 - chips], refs[-1 - chips:-1], refs[-1]
    rows, width = outs[0].shape
    have = terms[0].shape[0]
    total = terms[0][...]
    for term in terms[1:]:
        total = total + term[...]
    whole[:have, :] = total
    if have < chips * rows:
        whole[have:, :] = jnp.zeros((chips * rows - have, width), F32)
    for k, out in enumerate(outs):
        out[...] = whole[pl.ds(pl.multiple_of(me_ref[k] * rows, 8), rows), :]


def cut_pieces(order, terms):
    chips = order.shape[0]
    half, width = terms[0].shape
    rows = pl.cdiv(half, 8 * chips) * 8
    return kernel_call(
        cut_kernel, "cut_pieces", [shape((rows, width))] * chips,
        len(terms) * half * width, 4 * (len(terms) + 1) * half * width,
        in_specs=[SMEM] + [VMEM] * len(terms), out_specs=[VMEM] * chips,
        scratch_shapes=[pltpu.VMEM((chips * rows, width), F32)],
    )(order, *terms)


def join_kernel(me_ref, *refs):
    pieces, out_ref, whole = refs[:-2], refs[-2], refs[-1]
    rows = pieces[0].shape[0]
    for k, piece in enumerate(pieces):
        whole[pl.ds(pl.multiple_of(me_ref[k] * rows, 8), rows), :] = piece[...]
    out_ref[...] = whole[:out_ref.shape[0], :]


def join_pieces(order, pieces, half):
    rows, width = pieces[0].shape
    return kernel_call(
        join_kernel, "join_pieces", shape((half, width)),
        half * width, 8 * half * width,
        in_specs=[SMEM] + [VMEM] * len(pieces), out_specs=VMEM,
        scratch_shapes=[pltpu.VMEM((len(pieces) * rows, width), F32)],
    )(order, *pieces)


def relation_update_kernel(me_ref, relation_ref, state_ref, *refs):
    parts, out_ref, total = refs[:-2], refs[-2], refs[-1]
    groups = len(parts) // 2
    half, width = parts[0].shape
    group, core = me_ref[0], me_ref[1]
    for j in range(groups):
        at = pl.ds(pl.multiple_of((group ^ j) * width, LANES), width)
        total[pl.ds(pl.multiple_of(core * half, 8), half), at] = parts[j][...]
        total[pl.ds(pl.multiple_of((1 - core) * half, 8), half), at] = parts[groups + j][...]
    gradient = total[:, :out_ref.shape[1]]
    out_ref[...] = adagrad(relation_ref[...], state_ref[...], gradient)


def relation_update(me, relation, state, parts):
    features, count = relation.shape
    half, width = parts[0].shape
    groups = len(parts) // 2
    return kernel_call(
        relation_update_kernel, "relation_update", shape((features, count)),
        8 * features * count, 12 * features * count,
        in_specs=[SMEM] + [VMEM] * (2 + len(parts)), out_specs=VMEM,
        scratch_shapes=[pltpu.VMEM((features, groups * width), F32)],
    )(me, relation, state, *parts)


def sent_on(value, hop, peers):
    return lax.ppermute(value, "shard", [(i, partner(i, hop, peers, 1)) for i in range(peers)])


def sent_across(value, hop, peers, groups, by):
    pairs = [
        (g * peers + i, (g + by) % groups * peers + partner(i, hop, peers, 1))
        for g in range(groups)
        for i in range(peers)
    ]
    return lax.ppermute(value, ("group", "shard"), pairs)


def sent_group(value, bit, groups):
    return lax.ppermute(value, "group", [(g, g ^ bit) for g in range(groups)])


def relation_sum(kept, sent, peers, groups, chip):
    chips = peers // 2
    half = kept[0].shape[0]
    other_core = (0, 1)
    mine = [a + sent_on(b, other_core, peers) for a, b in zip(kept, sent)]
    terms = [mine[0]] + [sent_group(mine[j], j, groups) for j in range(1, groups)]
    ahead = (chip + jnp.arange(chips, dtype=I32)) % chips
    behind = (chip - jnp.arange(chips, dtype=I32)) % chips
    pieces = cut_pieces(ahead, terms)
    piece = pieces[0]
    for k in range(1, chips):
        piece = piece + sent_on(pieces[k], (k, 0), peers)
    pieces = [piece] + [sent_on(piece, (k, 0), peers) for k in range(1, chips)]
    block = join_pieces(behind, pieces, half)
    blocks = [block] + [sent_group(block, j, groups) for j in range(1, groups)]
    return blocks + [sent_on(b, other_core, peers) for b in blocks]


def on_device(
    entity, entity_state, relation, relation_state, src_send, dst_send,
    edge_source, edge_relation, edge_target, neg_slots, edge_count,
):
    rows, features = entity.shape
    relations = relation.shape[0]
    peers, block = src_send.shape[1:]
    groups = lax.axis_size("group")
    group = lax.axis_index("group").astype(I32)
    me = lax.axis_index("shard").astype(I32)
    width = pl.cdiv(relations, groups * LANES) * LANES
    entity_t, relation_t = entity.T, relation.T
    ways = hops(peers)
    order = jnp.stack([partner(me, hop, peers, 1) for hop in ways])
    here = jnp.stack([group, me % 2])

    def placed(slots):
        return places_of(me, slots // block, peers) * block + slots % block

    edge_source, edge_target = placed(edge_source), placed(edge_target)
    first = peers // 2
    sources = pick_blocks(order[:first], entity_t, src_send[0])
    sources += pick_blocks(order[first:], entity_t, src_send[0])
    sources = [
        sent_on(value, hop, peers) if hop != (0, 0) else value for value, hop in zip(sources, ways)
    ]
    targets = pick_blocks(order, entity_t, dst_send[0])
    targets = [sent_across(value, hop, peers, groups, -1) for value, hop in zip(targets, ways)]
    rels = relation_rows(relation_t, edge_relation.reshape(1, -1))
    counts = slot_counts(placed(neg_slots), peers * block)
    source_hots = home_hots(order, src_send[0], rows)
    target_hots = home_hots(order, dst_send[0], rows)
    heads, query_columns, query_lines = query_rows(sources, edge_source.reshape(1, -1), rels)
    loss, grad, table, *table_grads = score_spans(
        edge_count, targets, query_lines, query_columns, counts, edge_target.reshape(-1, 1)
    )
    back = [(-hop[0], hop[1]) for hop in ways]
    home = [sent_across(value, hop, peers, groups, 1) for value, hop in zip(table_grads, back)]
    source_lines, *halves = relation_grads(
        here, table, grad, heads, rels, edge_relation.reshape(-1, 1), groups, width
    )
    source_parts = source_grads(source_lines, edge_source.reshape(-1, 1), peers, block)
    returned = [
        sent_on(value, hop, peers) if hop != (0, 0) else value
        for value, hop in zip(source_parts, back)
    ]
    parts = relation_sum(halves[:groups], halves[groups:], peers, groups, me // 2)
    relation_new = relation_update(here, relation_t, relation_state.reshape(1, -1), parts)
    target_part = target_home(target_hots, home)
    entity_new = entity_update(
        source_hots, returned, target_part, entity_t, entity_state.reshape(1, -1)
    )
    return entity_new.T, relation_new.T, loss.reshape(-1)


def solution(mesh):
    both = ("group", "shard")
    return jax.shard_map(
        on_device,
        mesh=mesh,
        in_specs=(
            P(both, None), P(both), P(), P(), P(both, None, None), P(both, None, None),
            P(both), P(both), P(both), P(both, None), P(both),
        ),
        out_specs=(P(both, None), P(), P(both)),
        check_vma=False,
    )
```

```python
import functools

import jax
import jax.numpy as jnp
from jax import lax
from jax.experimental import pallas as pl
from jax.experimental.pallas import tpu as pltpu
from jax.sharding import PartitionSpec as P


SPAN = 512
LANES = 128
CHUNK = 256


learn_rate = 0.5

F32, BF16, I32 = jnp.float32, jnp.bfloat16, jnp.int32
VMEM = pl.BlockSpec(memory_space=pltpu.VMEM)
SMEM = pl.BlockSpec(memory_space=pltpu.SMEM)
VMEM_LIMIT = 60 << 20


def kernel_call(kernel, outs, flops, moved, **kw):
    semantics = ("arbitrary",) if "grid" in kw else None
    return pl.pallas_call(
        kernel,
        out_shape=outs,
        compiler_params=pltpu.CompilerParams(
            vmem_limit_bytes=VMEM_LIMIT, dimension_semantics=semantics
        ),
        cost_estimate=pl.CostEstimate(flops=flops, bytes_accessed=moved, transcendentals=0),
        **kw,
    )


def shape(dims, dtype=F32):
    return jax.ShapeDtypeStruct(dims, dtype)


def held(dims):
    return pl.BlockSpec(dims, lambda i: (0,) * len(dims))


def split2(x):
    hi = x.astype(BF16)
    return hi, (x - hi.astype(F32)).astype(BF16)


def split3(x):
    hi = x.astype(BF16)
    rest = x - hi.astype(F32)
    mid = rest.astype(BF16)
    return hi, mid, (rest - mid.astype(F32)).astype(BF16)


def dot(a, b):
    return jnp.dot(a, b, preferred_element_type=F32)


def dot_nt(a, b):
    return lax.dot_general(a, b, (((1,), (1,)), ((), ())), preferred_element_type=F32)


def one_hot(mask):
    return jnp.where(mask, 1.0, 0.0).astype(BF16)


def rows_hot(length, slots):
    return one_hot(lax.broadcasted_iota(I32, (length, slots.shape[1]), 0) == slots)


def columns_hot(slots, length):
    return one_hot(lax.broadcasted_iota(I32, (slots.shape[0], length), 1) == slots)


def complex_product(a, b):
    half = a.shape[0] // 2
    ar, ai, br, bi = a[:half], a[half:], b[:half], b[half:]
    return jnp.concatenate([ar * br - ai * bi, ar * bi + ai * br], axis=0)


def conj_product(a, b):
    half = a.shape[0] // 2
    ar, ai, br, bi = a[:half], a[half:], b[:half], b[half:]
    return jnp.concatenate([ar * br + ai * bi, ai * br - ar * bi], axis=0)


def hops(peers):
    chips = peers // 2
    ahead = [(k, b) for k in range(1, chips) for b in (0, 1)]
    return ahead + [(0, 1), (0, 0)]


def partner(me, hop, peers, sign):
    chips = peers // 2
    return (me // 2 + sign * hop[0]) % chips * 2 + (me % 2 + hop[1]) % 2


def places_of(me, owner, peers):
    chips = peers // 2
    k = (me // 2 - owner // 2) % chips
    b = (me + owner) % 2
    return (k - 1) % chips * 2 + jnp.where(k == 0, 1 - b, b)


def pick_kernel(order_ref, rows_ref, slots_ref, *outs):
    hi, mid, lo = split3(rows_ref[...])
    block = slots_ref.shape[1]
    together = max(1, CHUNK // block)
    for first in range(0, len(outs), together):
        group = outs[first:first + together]
        slots = [slots_ref[pl.ds(order_ref[first + i], 1), :] for i in range(len(group))]
        hot = rows_hot(rows_ref.shape[1], jnp.concatenate(slots, axis=1))
        picked = dot(hi, hot) + dot(mid, hot) + dot(lo, hot)
        for i, out in enumerate(group):
            out[...] = picked[:, i * block:(i + 1) * block]


def pick_blocks(order, rows, slots):
    features, length = rows.shape
    block = slots.shape[1]
    count = order.shape[0]
    return kernel_call(
        pick_kernel, [shape((features, block))] * count,
        6 * features * length * count * block, 8 * features * count * block,
        in_specs=[SMEM, VMEM, VMEM], out_specs=[VMEM] * count,
    )(order, rows, slots)


def relation_kernel(rel_ref, edge_rel_ref, out_ref, pieces):
    count = rel_ref.shape[1]
    padded = pieces.shape[2]

    @pl.when(pl.program_id(0) == 0)
    def _():
        features = rel_ref.shape[0]
        tail = padded - count // LANES * LANES
        for piece, value in enumerate(split3(rel_ref[...])):
            pieces[piece, :, padded - tail:] = jnp.zeros((features, tail), BF16)
            pieces[piece, :, :count] = value

    hot = rows_hot(padded, edge_rel_ref[...])
    out_ref[...] = dot(pieces[0], hot) + dot(pieces[1], hot) + dot(pieces[2], hot)


def relation_rows(relation, edge_relation):
    features, count = relation.shape
    edges = edge_relation.shape[1]
    padded = pl.cdiv(count, LANES) * LANES
    return kernel_call(
        relation_kernel, shape((features, edges)),
        6 * features * padded * edges, 8 * features * edges,
        grid=(edges // CHUNK,),
        in_specs=[held((features, count)), pl.BlockSpec((1, CHUNK), lambda i: (0, i))],
        out_specs=pl.BlockSpec((features, CHUNK), lambda i: (0, i)),
        scratch_shapes=[pltpu.VMEM((3, features, padded), BF16)],
    )(relation, edge_relation)


def count_kernel(slots_ref, out_ref):
    table_rows = out_ref.shape[2]
    hits = lax.broadcasted_iota(I32, (slots_ref.shape[1], table_rows), 1) == slots_ref[0]
    out_ref[0] = jnp.sum(jnp.where(hits, 1.0, 0.0), axis=0, keepdims=True)


def slot_counts(neg_slots, table_rows):
    spans, negatives = neg_slots.shape
    return kernel_call(
        count_kernel, shape((spans, 1, table_rows)),
        2 * spans * negatives * table_rows, 512 * spans * negatives,
        grid=(spans,),
        in_specs=[pl.BlockSpec((1, negatives, 1), lambda i: (i, 0, 0))],
        out_specs=pl.BlockSpec((1, 1, table_rows), lambda i: (i, 0, 0)),
    )(neg_slots[:, :, None])


def hot_kernel(order_ref, slots_ref, out_ref):
    peers, block, _ = slots_ref.shape
    for j in range(peers):
        out_ref[j * block:(j + 1) * block, :] = columns_hot(slots_ref[order_ref[j]], out_ref.shape[1])


def home_hots(order, slots, rows):
    peers, block = slots.shape
    return kernel_call(
        hot_kernel, shape((peers * block, rows), BF16),
        2 * peers * block * rows, 2 * peers * block * rows,
        in_specs=[SMEM, VMEM], out_specs=VMEM,
    )(order, slots[:, :, None])


def query_kernel(*refs):
    edge_source_ref, rels_ref, *blocks = refs[:-4]
    heads_ref, columns_ref, rows_ref, pieces = refs[-4:]
    block = blocks[0].shape[1]

    @pl.when(pl.program_id(0) == 0)
    def _():
        for p, ref in enumerate(blocks):
            for piece, value in enumerate(split3(ref[...])):
                pieces[piece, :, p * block:(p + 1) * block] = value

    hot = rows_hot(pieces.shape[2], edge_source_ref[...])
    heads = dot(pieces[0], hot) + dot(pieces[1], hot) + dot(pieces[2], hot)
    heads_ref[...] = heads
    queries = complex_product(heads, rels_ref[...])
    hi, lo = split2(queries)
    columns_ref[0], columns_ref[1] = hi, lo
    hi, lo = split2(queries.T)
    rows_ref[...] = jnp.concatenate([hi, hi, lo], axis=1)


def query_rows(blocks, edge_source, rels):
    peers = len(blocks)
    features, block = blocks[0].shape
    edges = edge_source.shape[1]
    return kernel_call(
        query_kernel,
        [shape((features, edges)), shape((2, features, edges), BF16), shape((edges, 3 * features), BF16)],
        6 * features * peers * block * edges, 20 * features * edges,
        grid=(edges // CHUNK,),
        in_specs=[
            pl.BlockSpec((1, CHUNK), lambda i: (0, i)),
            pl.BlockSpec((features, CHUNK), lambda i: (0, i)),
        ] + [held((features, block))] * peers,
        out_specs=[
            pl.BlockSpec((features, CHUNK), lambda i: (0, i)),
            pl.BlockSpec((2, features, CHUNK), lambda i: (0, 0, i)),
            pl.BlockSpec((CHUNK, 3 * features), lambda i: (i, 0)),
        ],
        scratch_shapes=[pltpu.VMEM((3, features, peers * block), BF16)],
    )(edge_source, rels, *blocks)


def score_kernel(peers, *refs):
    live_ref, rows_ref, columns_ref, counts_ref, edge_target_ref = refs[:5]
    blocks = refs[5:5 + peers]
    loss_ref, grad_ref, table_ref = refs[5 + peers:8 + peers]
    block_grads = refs[8 + peers:8 + 2 * peers]
    total, = refs[8 + 2 * peers:]
    features, block = blocks[0].shape
    step = pl.program_id(0)

    @pl.when(step == 0)
    def _():
        total[...] = jnp.zeros_like(total)
        for p, ref in enumerate(blocks):
            hi, lo = split2(ref[...])
            at = pl.ds(p * block, block)
            table_ref[:features, at] = hi
            table_ref[features:2 * features, at] = lo
            table_ref[2 * features:, at] = hi

    score = dot(rows_ref[...], table_ref[...])
    counts = counts_ref[0]
    own = lax.broadcasted_iota(I32, score.shape, 1) == edge_target_ref[...]
    pos = jnp.sum(jnp.where(own, score, 0.0), axis=1, keepdims=True)
    peak = jnp.max(jnp.where(counts > 0.0, score, -jnp.inf), axis=1, keepdims=True)
    peak = jnp.maximum(pos, peak)
    weight = counts * jnp.exp(jnp.minimum(score - peak, 0.0))
    pos_weight = jnp.exp(pos - peak)
    sum_all = pos_weight + jnp.sum(weight, axis=1, keepdims=True)
    edge = step * score.shape[0] + lax.broadcasted_iota(I32, pos.shape, 0)
    live = jnp.where(edge < live_ref[0], 1.0, 0.0)
    loss_ref[...] = (peak - pos + jnp.log(sum_all)) * live
    scale = live / sum_all
    pos_grad = pos_weight * scale - live
    grad = weight * scale + jnp.where(own, pos_grad, 0.0)
    hi, lo = split2(grad)
    grad_ref[0], grad_ref[1] = hi, lo
    total[...] += dot(columns_ref[0], hi) + dot(columns_ref[0], lo) + dot(columns_ref[1], hi)

    @pl.when(step == pl.num_programs(0) - 1)
    def _():
        for p, ref in enumerate(block_grads):
            ref[...] = total[:, p * block:(p + 1) * block]


def score_spans(live, blocks, rows, columns, counts, edge_target):
    peers = len(blocks)
    features, block = blocks[0].shape
    edges = edge_target.shape[0]
    table_rows = peers * block
    chunk = CHUNK
    per_span = SPAN // chunk
    return kernel_call(
        functools.partial(score_kernel, peers),
        [
            shape((edges, 1)),
            shape((2, edges, table_rows), BF16),
            shape((3 * features, table_rows), BF16),
        ] + [shape((features, block))] * peers,
        12 * features * table_rows * edges, 30 * features * edges,
        grid=(edges // chunk,),
        in_specs=[
            SMEM,
            pl.BlockSpec((chunk, 3 * features), lambda i: (i, 0)),
            pl.BlockSpec((2, features, chunk), lambda i: (0, 0, i)),
            pl.BlockSpec((1, 1, table_rows), lambda i: (i // per_span, 0, 0)),
            pl.BlockSpec((chunk, 1), lambda i: (i, 0)),
        ] + [held((features, block))] * peers,
        out_specs=[
            pl.BlockSpec((chunk, 1), lambda i: (i, 0)),
            pl.BlockSpec((2, chunk, table_rows), lambda i: (0, i, 0)),
            held((3 * features, table_rows)),
        ] + [held((features, block))] * peers,
        scratch_shapes=[pltpu.VMEM((features, table_rows), F32)],
    )(live, rows, columns, counts, edge_target, *blocks)


def relation_grad_kernel(
    me_ref, table_ref, grad_ref, heads_ref, rels_ref, edge_rel_ref, source_ref, *refs
):
    outs, total = refs[:-1], refs[-1]
    groups = len(outs) // 2
    half, width = outs[0].shape
    step = pl.program_id(0)

    @pl.when(step == 0)
    def _():
        total[...] = jnp.zeros_like(total)

    features = heads_ref.shape[0]
    hi, lo = table_ref[:features], table_ref[features:2 * features]
    query_grad = dot_nt(hi, grad_ref[0]) + dot_nt(hi, grad_ref[1]) + dot_nt(lo, grad_ref[0])
    source_ref[0], source_ref[1] = split2(conj_product(query_grad, rels_ref[...]))
    hi, lo = split2(conj_product(query_grad, heads_ref[...]))
    hot = columns_hot(edge_rel_ref[...], total.shape[1])
    total[...] += dot(hi, hot) + dot(lo, hot)

    @pl.when(step == pl.num_programs(0) - 1)
    def _():
        group, core = me_ref[0], me_ref[1]
        for j in range(groups):
            at = pl.ds(pl.multiple_of((group ^ j) * width, LANES), width)
            outs[j][...] = total[pl.ds(pl.multiple_of(core * half, 8), half), at]
            outs[groups + j][...] = total[pl.ds(pl.multiple_of((1 - core) * half, 8), half), at]


def relation_grads(me, table, grad, heads, rels, edge_relation, groups, width):
    features, edges = heads.shape
    table_rows = table.shape[1]
    chunk = CHUNK
    return kernel_call(
        relation_grad_kernel,
        [shape((2, features, edges), BF16)] + [shape((features // 2, width))] * (2 * groups),
        10 * features * table_rows * edges, 30 * features * edges,
        grid=(edges // chunk,),
        in_specs=[
            SMEM,
            held((3 * features, table_rows)),
            pl.BlockSpec((2, chunk, table_rows), lambda i: (0, i, 0)),
            pl.BlockSpec((features, chunk), lambda i: (0, i)),
            pl.BlockSpec((features, chunk), lambda i: (0, i)),
            pl.BlockSpec((chunk, 1), lambda i: (i, 0)),
        ],
        out_specs=[pl.BlockSpec((2, features, chunk), lambda i: (0, 0, i))]
        + [held((features // 2, width))] * (2 * groups),
        scratch_shapes=[pltpu.VMEM((features, groups * width), F32)],
    )(me, table, grad, heads, rels, edge_relation)


def source_grad_kernel(rows_ref, edge_source_ref, *refs):
    outs, total = refs[:-1], refs[-1]
    block = outs[0].shape[1]
    step = pl.program_id(0)

    @pl.when(step == 0)
    def _():
        total[...] = jnp.zeros_like(total)

    hot = columns_hot(edge_source_ref[...], total.shape[1])
    total[...] += dot(rows_ref[0], hot) + dot(rows_ref[1], hot)

    @pl.when(step == pl.num_programs(0) - 1)
    def _():
        for p, ref in enumerate(outs):
            ref[...] = total[:, p * block:(p + 1) * block]


def source_grads(rows, edge_source, peers, block):
    _, features, edges = rows.shape
    return kernel_call(
        source_grad_kernel, [shape((features, block))] * peers,
        4 * features * peers * block * edges, 12 * features * edges,
        grid=(edges // CHUNK,),
        in_specs=[
            pl.BlockSpec((2, features, CHUNK), lambda i: (0, 0, i)),
            pl.BlockSpec((CHUNK, 1), lambda i: (i, 0)),
        ],
        out_specs=[held((features, block))] * peers,
        scratch_shapes=[pltpu.VMEM((features, peers * block), F32)],
    )(rows, edge_source)


def put_back(blocks, hot_ref):
    hi, lo = split2(jnp.concatenate([ref[...] for ref in blocks], axis=1))
    return dot(hi, hot_ref[...]) + dot(lo, hot_ref[...])


def target_home_kernel(hot_ref, *refs):
    refs[-1][...] = put_back(refs[:-1], hot_ref)


def target_home(hots, blocks):
    features = blocks[0].shape[0]
    rows = hots.shape[1]
    return kernel_call(
        target_home_kernel, shape((features, rows)),
        4 * features * rows * hots.shape[0], 8 * features * hots.shape[0],
        in_specs=[VMEM] * (1 + len(blocks)), out_specs=VMEM,
    )(hots, *blocks)


def adagrad(params, state, gradient):
    new_state = state + jnp.mean(gradient * gradient, axis=0, keepdims=True)
    return params - learn_rate * gradient / jnp.sqrt(new_state)


def entity_kernel(other_ref, entity_ref, state_ref, hot_ref, *refs):
    gradient = other_ref[...] + put_back(refs[:-1], hot_ref)
    refs[-1][...] = adagrad(entity_ref[...], state_ref[...], gradient)


def entity_update(hots, blocks, other, entity, state):
    features, rows = entity.shape
    return kernel_call(
        entity_kernel, shape((features, rows)),
        4 * features * rows * hots.shape[0], 8 * features * hots.shape[0],
        in_specs=[VMEM] * (4 + len(blocks)), out_specs=VMEM,
    )(other, entity, state, hots, *blocks)


def cut_kernel(me_ref, *refs):
    chips = me_ref.shape[0]
    terms, outs, whole = refs[:-1 - chips], refs[-1 - chips:-1], refs[-1]
    rows, width = outs[0].shape
    have = terms[0].shape[0]
    total = terms[0][...]
    for term in terms[1:]:
        total = total + term[...]
    whole[:have, :] = total
    if have < chips * rows:
        whole[have:, :] = jnp.zeros((chips * rows - have, width), F32)
    for k, out in enumerate(outs):
        out[...] = whole[pl.ds(pl.multiple_of(me_ref[k] * rows, 8), rows), :]


def cut_pieces(order, terms):
    chips = order.shape[0]
    half, width = terms[0].shape
    rows = pl.cdiv(half, 8 * chips) * 8
    return kernel_call(
        cut_kernel, [shape((rows, width))] * chips,
        len(terms) * half * width, 4 * (len(terms) + 1) * half * width,
        in_specs=[SMEM] + [VMEM] * len(terms), out_specs=[VMEM] * chips,
        scratch_shapes=[pltpu.VMEM((chips * rows, width), F32)],
    )(order, *terms)


def sum_kernel(*refs):
    total = refs[0][...]
    for ref in refs[1:-1]:
        total = total + ref[...]
    refs[-1][...] = total


def sum_pieces(pieces):
    rows, width = pieces[0].shape
    return kernel_call(
        sum_kernel, shape((rows, width)),
        len(pieces) * rows * width, 4 * (len(pieces) + 1) * rows * width,
        in_specs=[VMEM] * len(pieces), out_specs=VMEM,
    )(*pieces)


def join_kernel(me_ref, *refs):
    pieces, out_ref, whole = refs[:-2], refs[-2], refs[-1]
    rows = pieces[0].shape[0]
    for k, piece in enumerate(pieces):
        whole[pl.ds(pl.multiple_of(me_ref[k] * rows, 8), rows), :] = piece[...]
    out_ref[...] = whole[:out_ref.shape[0], :]


def join_pieces(order, pieces, half):
    rows, width = pieces[0].shape
    return kernel_call(
        join_kernel, shape((half, width)),
        half * width, 8 * half * width,
        in_specs=[SMEM] + [VMEM] * len(pieces), out_specs=VMEM,
        scratch_shapes=[pltpu.VMEM((len(pieces) * rows, width), F32)],
    )(order, *pieces)


def relation_update_kernel(me_ref, relation_ref, state_ref, *refs):
    parts, out_ref, total = refs[:-2], refs[-2], refs[-1]
    groups = len(parts) // 2
    half, width = parts[0].shape
    group, core = me_ref[0], me_ref[1]
    for j in range(groups):
        at = pl.ds(pl.multiple_of((group ^ j) * width, LANES), width)
        total[pl.ds(pl.multiple_of(core * half, 8), half), at] = parts[j][...]
        total[pl.ds(pl.multiple_of((1 - core) * half, 8), half), at] = parts[groups + j][...]
    gradient = total[:, :out_ref.shape[1]]
    out_ref[...] = adagrad(relation_ref[...], state_ref[...], gradient)


def relation_update(me, relation, state, parts):
    features, count = relation.shape
    _, width = parts[0].shape
    groups = len(parts) // 2
    return kernel_call(
        relation_update_kernel, shape((features, count)),
        8 * features * count, 12 * features * count,
        in_specs=[SMEM] + [VMEM] * (2 + len(parts)), out_specs=VMEM,
        scratch_shapes=[pltpu.VMEM((features, groups * width), F32)],
    )(me, relation, state, *parts)


def sent_on(value, hop, peers):
    return lax.ppermute(value, "shard", [(i, partner(i, hop, peers, 1)) for i in range(peers)])


def sent_across(value, hop, peers, groups, by):
    pairs = [
        (g * peers + i, (g + by) % groups * peers + partner(i, hop, peers, 1))
        for g in range(groups)
        for i in range(peers)
    ]
    return lax.ppermute(value, ("group", "shard"), pairs)


def sent_group(value, bit, groups):
    return lax.ppermute(value, "group", [(g, g ^ bit) for g in range(groups)])


def relation_sum(kept, sent, peers, groups, chip):
    chips = peers // 2
    half = kept[0].shape[0]
    other_core = (0, 1)
    sent = [sent_on(b, other_core, peers) for b in sent]
    mine = [a + b for a, b in zip(kept, sent)]
    terms = [mine[0]] + [sent_group(mine[j], j, groups) for j in range(1, groups)]
    ahead = (chip + jnp.arange(chips, dtype=I32)) % chips
    behind = (chip - jnp.arange(chips, dtype=I32)) % chips
    pieces = cut_pieces(ahead, terms)
    pieces = [pieces[0]] + [sent_on(pieces[k], (k, 0), peers) for k in range(1, chips)]
    piece = sum_pieces(pieces)
    pieces = [piece] + [sent_on(piece, (k, 0), peers) for k in range(1, chips)]
    block = join_pieces(behind, pieces, half)
    blocks = [block] + [sent_group(block, j, groups) for j in range(1, groups)]
    return blocks + [sent_on(b, other_core, peers) for b in blocks]


def on_device(
    entity, entity_state, relation, relation_state, src_send, dst_send,
    edge_source, edge_relation, edge_target, neg_slots, edge_count,
):
    rows, _ = entity.shape
    relations = relation.shape[0]
    peers, block = src_send.shape[1:]
    groups = lax.axis_size("group")
    group = lax.axis_index("group").astype(I32)
    me = lax.axis_index("shard").astype(I32)
    width = pl.cdiv(relations, groups * LANES) * LANES
    entity_t, relation_t = entity.T, relation.T
    ways = hops(peers)
    order = jnp.stack([partner(me, hop, peers, 1) for hop in ways])
    here = jnp.stack([group, me % 2])

    def placed(slots):
        return places_of(me, slots // block, peers) * block + slots % block

    edge_source, edge_target = placed(edge_source), placed(edge_target)
    first = peers // 2
    sources = pick_blocks(order[:first], entity_t, src_send[0])
    sources += pick_blocks(order[first:], entity_t, src_send[0])
    sources = [
        sent_on(value, hop, peers) if hop != (0, 0) else value
        for value, hop in zip(sources, ways)
    ]
    targets = pick_blocks(order, entity_t, dst_send[0])
    targets = [sent_across(value, hop, peers, groups, -1) for value, hop in zip(targets, ways)]
    rels = relation_rows(relation_t, edge_relation.reshape(1, -1))
    counts = slot_counts(placed(neg_slots), peers * block)
    source_hots = home_hots(order, src_send[0], rows)
    target_hots = home_hots(order, dst_send[0], rows)
    heads, query_columns, query_lines = query_rows(sources, edge_source.reshape(1, -1), rels)
    loss, grad, table, *table_grads = score_spans(
        edge_count, targets, query_lines, query_columns, counts, edge_target.reshape(-1, 1)
    )
    back = [(-hop[0], hop[1]) for hop in ways]
    home = [sent_across(value, hop, peers, groups, 1) for value, hop in zip(table_grads, back)]
    source_lines, *halves = relation_grads(
        here, table, grad, heads, rels, edge_relation.reshape(-1, 1), groups, width
    )
    source_parts = source_grads(source_lines, edge_source.reshape(-1, 1), peers, block)
    returned = []
    for value, hop, way in zip(source_parts, back, ways):
        returned.append(sent_on(value, hop, peers) if way != (0, 0) else value)
    parts = relation_sum(halves[:groups], halves[groups:], peers, groups, me // 2)
    relation_new = relation_update(here, relation_t, relation_state.reshape(1, -1), parts)
    target_part = target_home(target_hots, home)
    entity_new = entity_update(
        source_hots, returned, target_part, entity_t, entity_state.reshape(1, -1)
    )
    return entity_new.T, relation_new.T, loss.reshape(-1)


def solution(mesh):
    both = ("group", "shard")
    return jax.shard_map(
        on_device,
        mesh=mesh,
        in_specs=(
            P(both, None), P(both), P(), P(), P(both, None, None), P(both, None, None),
            P(both), P(both), P(both), P(both, None), P(both),
        ),
        out_specs=(P(both, None), P(), P(both)),
        check_vma=False,
    )
```

```python
import functools
import math

import jax
import jax.numpy as jnp
from jax import lax
from jax.experimental import pallas as pl
from jax.experimental.pallas import tpu as pltpu
from jax.sharding import PartitionSpec as P


SPAN = 512
LANES = 128
CHUNK = 256
WIDE = 512


learn_rate = 0.5

F32, BF16, I32 = jnp.float32, jnp.bfloat16, jnp.int32
VMEM = pl.BlockSpec(memory_space=pltpu.VMEM)
SMEM = pl.BlockSpec(memory_space=pltpu.SMEM)
VMEM_LIMIT = 60 << 20


def kernel_call(kernel, outs, flops, moved, **kw):
    semantics = ("arbitrary",) if "grid" in kw else None
    return pl.pallas_call(
        kernel,
        out_shape=outs,
        compiler_params=pltpu.CompilerParams(
            vmem_limit_bytes=VMEM_LIMIT, dimension_semantics=semantics
        ),
        cost_estimate=pl.CostEstimate(flops=flops, bytes_accessed=moved, transcendentals=0),
        **kw,
    )


def shape(dims, dtype=F32):
    return jax.ShapeDtypeStruct(dims, dtype)


def held(dims):
    return pl.BlockSpec(dims, lambda i: (0,) * len(dims))


def split2(x):
    hi = x.astype(BF16)
    return hi, (x - hi.astype(F32)).astype(BF16)


def split3(x):
    hi = x.astype(BF16)
    rest = x - hi.astype(F32)
    mid = rest.astype(BF16)
    return hi, mid, (rest - mid.astype(F32)).astype(BF16)


def dot(a, b):
    return jnp.dot(a, b, preferred_element_type=F32)


def dot_nt(a, b):
    return lax.dot_general(a, b, (((1,), (1,)), ((), ())), preferred_element_type=F32)


def one_hot(mask):
    return jnp.where(mask, 1.0, 0.0).astype(BF16)


def rows_hot(length, slots):
    return one_hot(lax.broadcasted_iota(I32, (length, slots.shape[1]), 0) == slots)


def columns_hot(slots, length):
    return one_hot(lax.broadcasted_iota(I32, (slots.shape[0], length), 1) == slots)


def complex_product(a, b):
    half = a.shape[0] // 2
    ar, ai, br, bi = a[:half], a[half:], b[:half], b[half:]
    return jnp.concatenate([ar * br - ai * bi, ar * bi + ai * br], axis=0)


def conj_product(a, b):
    half = a.shape[0] // 2
    ar, ai, br, bi = a[:half], a[half:], b[:half], b[half:]
    return jnp.concatenate([ar * br + ai * bi, ai * br - ar * bi], axis=0)


def hops(peers):
    chips = peers // 2
    ahead = [(k, b) for k in range(1, chips) for b in (0, 1)]
    return ahead + [(0, 1), (0, 0)]


def partner(me, hop, peers, sign):
    chips = peers // 2
    return (me // 2 + sign * hop[0]) % chips * 2 + (me % 2 + hop[1]) % 2


def places_of(me, owner, peers):
    chips = peers // 2
    k = (me // 2 - owner // 2) % chips
    b = (me + owner) % 2
    return (k - 1) % chips * 2 + jnp.where(k == 0, 1 - b, b)


def pick_kernel(order_ref, rows_ref, slots_ref, *outs):
    hi, mid, lo = split3(rows_ref[...])
    block = slots_ref.shape[1]
    together = max(1, CHUNK // block)
    for first in range(0, len(outs), together):
        group = outs[first:first + together]
        slots = [slots_ref[pl.ds(order_ref[first + i], 1), :] for i in range(len(group))]
        hot = rows_hot(rows_ref.shape[1], jnp.concatenate(slots, axis=1))
        picked = dot(hi, hot) + dot(mid, hot) + dot(lo, hot)
        for i, out in enumerate(group):
            out[...] = picked[:, i * block:(i + 1) * block]


def pick_blocks(order, rows, slots):
    features, length = rows.shape
    block = slots.shape[1]
    count = order.shape[0]
    return kernel_call(
        pick_kernel, [shape((features, block))] * count,
        6 * features * length * count * block, 8 * features * count * block,
        in_specs=[SMEM, VMEM, VMEM], out_specs=[VMEM] * count,
    )(order, rows, slots)


def relation_kernel(rel_ref, edge_rel_ref, out_ref, pieces):
    count = rel_ref.shape[1]
    padded = pieces.shape[2]

    @pl.when(pl.program_id(0) == 0)
    def _():
        features = rel_ref.shape[0]
        tail = padded - count // LANES * LANES
        for piece, value in enumerate(split3(rel_ref[...])):
            pieces[piece, :, padded - tail:] = jnp.zeros((features, tail), BF16)
            pieces[piece, :, :count] = value

    hot = rows_hot(padded, edge_rel_ref[...])
    out_ref[...] = dot(pieces[0], hot) + dot(pieces[1], hot) + dot(pieces[2], hot)


def relation_rows(relation, edge_relation):
    features, count = relation.shape
    edges = edge_relation.shape[1]
    padded = pl.cdiv(count, LANES) * LANES
    return kernel_call(
        relation_kernel, shape((features, edges)),
        6 * features * padded * edges, 8 * features * edges,
        grid=(edges // CHUNK,),
        in_specs=[held((features, count)), pl.BlockSpec((1, CHUNK), lambda i: (0, i))],
        out_specs=pl.BlockSpec((features, CHUNK), lambda i: (0, i)),
        scratch_shapes=[pltpu.VMEM((3, features, padded), BF16)],
    )(relation, edge_relation)


def count_kernel(slots_ref, out_ref):
    table_rows = out_ref.shape[2]
    hits = lax.broadcasted_iota(I32, (slots_ref.shape[1], table_rows), 1) == slots_ref[0]
    out_ref[0] = jnp.sum(jnp.where(hits, 1.0, 0.0), axis=0, keepdims=True)


def slot_counts(neg_slots, table_rows):
    spans, negatives = neg_slots.shape
    return kernel_call(
        count_kernel, shape((spans, 1, table_rows)),
        2 * spans * negatives * table_rows, 512 * spans * negatives,
        grid=(spans,),
        in_specs=[pl.BlockSpec((1, negatives, 1), lambda i: (i, 0, 0))],
        out_specs=pl.BlockSpec((1, 1, table_rows), lambda i: (i, 0, 0)),
    )(neg_slots[:, :, None])


def hot_kernel(order_ref, slots_ref, out_ref):
    peers, block, _ = slots_ref.shape
    for j in range(peers):
        out_ref[j * block:(j + 1) * block, :] = columns_hot(slots_ref[order_ref[j]], out_ref.shape[1])


def home_hots(order, slots, rows):
    peers, block = slots.shape
    return kernel_call(
        hot_kernel, shape((peers * block, rows), BF16),
        2 * peers * block * rows, 2 * peers * block * rows,
        in_specs=[SMEM, VMEM], out_specs=VMEM,
    )(order, slots[:, :, None])


def query_kernel(*refs):
    edge_source_ref, rels_ref, *blocks = refs[:-4]
    heads_ref, columns_ref, rows_ref, pieces = refs[-4:]
    block = blocks[0].shape[1]

    @pl.when(pl.program_id(0) == 0)
    def _():
        for p, ref in enumerate(blocks):
            for piece, value in enumerate(split3(ref[...])):
                pieces[piece, :, p * block:(p + 1) * block] = value

    hot = rows_hot(pieces.shape[2], edge_source_ref[...])
    heads = dot(pieces[0], hot) + dot(pieces[1], hot) + dot(pieces[2], hot)
    heads_ref[...] = heads
    queries = complex_product(heads, rels_ref[...])
    hi, lo = split2(queries)
    columns_ref[0], columns_ref[1] = hi, lo
    hi, lo = split2(queries.T)
    rows_ref[...] = jnp.concatenate([hi, hi, lo], axis=1)


def query_rows(blocks, edge_source, rels):
    peers = len(blocks)
    features, block = blocks[0].shape
    edges = edge_source.shape[1]
    return kernel_call(
        query_kernel,
        [shape((features, edges)), shape((2, features, edges), BF16), shape((edges, 3 * features), BF16)],
        6 * features * peers * block * edges, 20 * features * edges,
        grid=(edges // CHUNK,),
        in_specs=[
            pl.BlockSpec((1, CHUNK), lambda i: (0, i)),
            pl.BlockSpec((features, CHUNK), lambda i: (0, i)),
        ] + [held((features, block))] * peers,
        out_specs=[
            pl.BlockSpec((features, CHUNK), lambda i: (0, i)),
            pl.BlockSpec((2, features, CHUNK), lambda i: (0, 0, i)),
            pl.BlockSpec((CHUNK, 3 * features), lambda i: (i, 0)),
        ],
        scratch_shapes=[pltpu.VMEM((3, features, peers * block), BF16)],
    )(edge_source, rels, *blocks)


def softmax_step(step, live, score, counts, edge_target, loss_ref, grad_ref):
    own = lax.broadcasted_iota(I32, score.shape, 1) == edge_target
    pos = jnp.sum(jnp.where(own, score, 0.0), axis=1, keepdims=True)
    peak = jnp.max(jnp.where(counts > 0.0, score, -jnp.inf), axis=1, keepdims=True)
    peak = jnp.maximum(pos, peak)
    weight = counts * jnp.exp(jnp.minimum(score - peak, 0.0))
    pos_weight = jnp.exp(pos - peak)
    sum_all = pos_weight + jnp.sum(weight, axis=1, keepdims=True)
    edge = step * score.shape[0] + lax.broadcasted_iota(I32, pos.shape, 0)
    is_live = jnp.where(edge < live, 1.0, 0.0)
    loss_ref[...] = (peak - pos + jnp.log(sum_all)) * is_live
    scale = is_live / sum_all
    pos_grad = pos_weight * scale - is_live
    grad = weight * scale + jnp.where(own, pos_grad, 0.0)
    grad_ref[0], grad_ref[1] = split2(grad)


def score_kernel(peers, *refs):
    live_ref, rows_ref, counts_ref, edge_target_ref = refs[:4]
    blocks = refs[4:4 + peers]
    loss_ref, grad_ref, table_ref, scores = refs[4 + peers:]
    features, block = blocks[0].shape
    step = pl.program_id(0)
    last = pl.num_programs(0) - 1

    @pl.when(step == 0)
    def _():
        for p, ref in enumerate(blocks):
            hi, lo = split2(ref[...])
            at = pl.ds(p * block, block)
            table_ref[:features, at] = hi
            table_ref[features:2 * features, at] = lo
            table_ref[2 * features:, at] = hi

    def multiply():
        scores[step % 2] = dot(rows_ref[...], table_ref[...])

    def finish():
        softmax_step(
            step - 1, live_ref[0], scores[(step + 1) % 2], counts_ref[0], edge_target_ref[...],
            loss_ref, grad_ref,
        )

    @pl.when(step == 0)
    def _():
        multiply()

    @pl.when((step > 0) & (step < last))
    def _():
        multiply()
        finish()

    @pl.when(step == last)
    def _():
        finish()


def score_spans(live, blocks, rows, counts, edge_target):
    peers = len(blocks)
    features, block = blocks[0].shape
    edges = edge_target.shape[0]
    table_rows = peers * block
    chunk = CHUNK
    per_span = SPAN // chunk
    steps = edges // chunk

    def now(i):
        return jnp.minimum(i, steps - 1)

    def before(i):
        return jnp.maximum(i - 1, 0)

    return kernel_call(
        functools.partial(score_kernel, peers),
        [
            shape((edges, 1)),
            shape((2, edges, table_rows), BF16),
            shape((3 * features, table_rows), BF16),
        ],
        6 * features * table_rows * edges, 30 * features * edges,
        grid=(steps + 1,),
        in_specs=[
            SMEM,
            pl.BlockSpec((chunk, 3 * features), lambda i: (now(i), 0)),
            pl.BlockSpec((1, 1, table_rows), lambda i: (before(i) // per_span, 0, 0)),
            pl.BlockSpec((chunk, 1), lambda i: (before(i), 0)),
        ] + [held((features, block))] * peers,
        out_specs=[
            pl.BlockSpec((chunk, 1), lambda i: (before(i), 0)),
            pl.BlockSpec((2, chunk, table_rows), lambda i: (0, before(i), 0)),
            held((3 * features, table_rows)),
        ],
        scratch_shapes=[pltpu.VMEM((2, chunk, table_rows), F32)],
    )(live, rows, counts, edge_target, *blocks)


def table_grad_kernel(columns_ref, grad_ref, *outs):
    step = pl.program_id(0)
    block = outs[0].shape[1]
    result = (
        dot(columns_ref[0], grad_ref[0])
        + dot(columns_ref[0], grad_ref[1])
        + dot(columns_ref[1], grad_ref[0])
    )
    for pair in range(len(outs) // 2):
        @pl.when(step == pair)
        def _():
            outs[2 * pair][...] = result[:, :block]
            outs[2 * pair + 1][...] = result[:, block:]


def table_grads(columns, grad, block, first, count):
    _, features, edges = columns.shape
    return kernel_call(
        table_grad_kernel, [shape((features, block))] * count,
        6 * features * count * block * edges, 4 * edges * (features + count * block),
        grid=(count // 2,),
        in_specs=[
            held((2, features, edges)),
            pl.BlockSpec((2, edges, 2 * block), lambda i: (0, 0, first // 2 + i)),
        ],
        out_specs=[held((features, block))] * count,
    )(columns, grad)


def relation_grad_kernel(
    steps, me_ref, table_ref, grad_ref, heads_ref, rels_ref, edge_rel_ref, source_ref, *refs
):
    outs, lines, total = refs[:-2], refs[-2], refs[-1]
    groups = len(outs) // 2
    half, width = outs[0].shape
    step = pl.program_id(0)
    features, chunk = heads_ref.shape
    tile = total.shape[2]

    @pl.when(step < steps)
    def _():
        hi, lo = table_ref[:features], table_ref[features:2 * features]
        query_grad = dot_nt(hi, grad_ref[0]) + dot_nt(hi, grad_ref[1]) + dot_nt(lo, grad_ref[0])
        source_ref[0], source_ref[1] = split2(conj_product(query_grad, rels_ref[...]))
        lines[step] = jnp.concatenate(split2(conj_product(query_grad, heads_ref[...])), axis=1)

    @pl.when(step >= steps)
    def _():
        part = None
        for i in range(steps):
            slots = edge_rel_ref[i * chunk:(i + 1) * chunk, :] - (step - steps) * tile
            hot = columns_hot(slots, tile)
            term = dot(lines[i, :, :chunk], hot) + dot(lines[i, :, chunk:], hot)
            part = term if part is None else part + term
        total[step - steps] = part

    @pl.when(step == pl.num_programs(0) - 1)
    def _():
        group, core = me_ref[0], me_ref[1]
        for j in range(groups):
            for at in range(0, width, LANES):
                start = (group ^ j) * width + at
                rows = total.at[start // tile, :, pl.ds(pl.multiple_of(start % tile, LANES), LANES)]
                outs[j][:, at:at + LANES] = rows[pl.ds(pl.multiple_of(core * half, 8), half), :]
                outs[groups + j][:, at:at + LANES] = rows[
                    pl.ds(pl.multiple_of((1 - core) * half, 8), half), :
                ]


def relation_grads(me, table, grad, heads, rels, edge_relation, groups, width):
    features, edges = heads.shape
    table_rows = table.shape[1]
    chunk = CHUNK
    steps = edges // chunk
    tile = math.gcd(groups * width, WIDE)
    tiles = groups * width // tile

    def now(i):
        return jnp.minimum(i, steps - 1)

    return kernel_call(
        functools.partial(relation_grad_kernel, steps),
        [shape((2, features, edges), BF16)] + [shape((features // 2, width))] * (2 * groups),
        10 * features * table_rows * edges, 30 * features * edges,
        grid=(steps + tiles,),
        in_specs=[
            SMEM,
            held((3 * features, table_rows)),
            pl.BlockSpec((2, chunk, table_rows), lambda i: (0, now(i), 0)),
            pl.BlockSpec((features, chunk), lambda i: (0, now(i))),
            pl.BlockSpec((features, chunk), lambda i: (0, now(i))),
            held((edges, 1)),
        ],
        out_specs=[pl.BlockSpec((2, features, chunk), lambda i: (0, 0, now(i)))]
        + [held((features // 2, width))] * (2 * groups),
        scratch_shapes=[
            pltpu.VMEM((steps, features, 2 * chunk), BF16),
            pltpu.VMEM((tiles, features, tile), F32),
        ],
    )(me, table, grad, heads, rels, edge_relation)


def source_grad_kernel(rows_ref, edge_source_ref, *refs):
    outs, total = refs[:-1], refs[-1]
    block = outs[0].shape[1]
    step = pl.program_id(0)

    @pl.when(step == 0)
    def _():
        total[...] = jnp.zeros_like(total)

    hot = columns_hot(edge_source_ref[...], total.shape[1])
    total[...] += dot(rows_ref[0], hot) + dot(rows_ref[1], hot)

    @pl.when(step == pl.num_programs(0) - 1)
    def _():
        for p, ref in enumerate(outs):
            ref[...] = total[:, p * block:(p + 1) * block]


def source_grads(rows, edge_source, peers, block):
    _, features, edges = rows.shape
    return kernel_call(
        source_grad_kernel, [shape((features, block))] * peers,
        4 * features * peers * block * edges, 12 * features * edges,
        grid=(edges // CHUNK,),
        in_specs=[
            pl.BlockSpec((2, features, CHUNK), lambda i: (0, 0, i)),
            pl.BlockSpec((CHUNK, 1), lambda i: (i, 0)),
        ],
        out_specs=[held((features, block))] * peers,
        scratch_shapes=[pltpu.VMEM((features, peers * block), F32)],
    )(rows, edge_source)


def put_back(blocks, hot_ref):
    hi, lo = split2(jnp.concatenate([ref[...] for ref in blocks], axis=1))
    return dot(hi, hot_ref[...]) + dot(lo, hot_ref[...])


def target_home_kernel(hot_ref, *refs):
    refs[-1][...] = put_back(refs[:-1], hot_ref)


def target_home(hots, blocks):
    features = blocks[0].shape[0]
    rows = hots.shape[1]
    return kernel_call(
        target_home_kernel, shape((features, rows)),
        4 * features * rows * hots.shape[0], 8 * features * hots.shape[0],
        in_specs=[VMEM] * (1 + len(blocks)), out_specs=VMEM,
    )(hots, *blocks)


def adagrad(params, state, gradient):
    new_state = state + jnp.mean(gradient * gradient, axis=0, keepdims=True)
    return params - learn_rate * gradient / jnp.sqrt(new_state)


def entity_kernel(other_ref, entity_ref, state_ref, hot_ref, *refs):
    gradient = other_ref[...] + put_back(refs[:-1], hot_ref)
    refs[-1][...] = adagrad(entity_ref[...], state_ref[...], gradient)


def entity_update(hots, blocks, other, entity, state):
    features, rows = entity.shape
    return kernel_call(
        entity_kernel, shape((features, rows)),
        4 * features * rows * hots.shape[0], 8 * features * hots.shape[0],
        in_specs=[VMEM] * (4 + len(blocks)), out_specs=VMEM,
    )(other, entity, state, hots, *blocks)


def cut_kernel(me_ref, *refs):
    chips = me_ref.shape[0]
    terms, outs, whole = refs[:-1 - chips], refs[-1 - chips:-1], refs[-1]
    rows, width = outs[0].shape
    have = terms[0].shape[0]
    total = terms[0][...]
    for term in terms[1:]:
        total = total + term[...]
    whole[:have, :] = total
    if have < chips * rows:
        whole[have:, :] = jnp.zeros((chips * rows - have, width), F32)
    for k, out in enumerate(outs):
        out[...] = whole[pl.ds(pl.multiple_of(me_ref[k] * rows, 8), rows), :]


def cut_pieces(order, terms):
    chips = order.shape[0]
    half, width = terms[0].shape
    rows = pl.cdiv(half, 8 * chips) * 8
    return kernel_call(
        cut_kernel, [shape((rows, width))] * chips,
        len(terms) * half * width, 4 * (len(terms) + 1) * half * width,
        in_specs=[SMEM] + [VMEM] * len(terms), out_specs=[VMEM] * chips,
        scratch_shapes=[pltpu.VMEM((chips * rows, width), F32)],
    )(order, *terms)


def sum_kernel(*refs):
    total = refs[0][...]
    for ref in refs[1:-1]:
        total = total + ref[...]
    refs[-1][...] = total


def sum_pieces(pieces):
    rows, width = pieces[0].shape
    return kernel_call(
        sum_kernel, shape((rows, width)),
        len(pieces) * rows * width, 4 * (len(pieces) + 1) * rows * width,
        in_specs=[VMEM] * len(pieces), out_specs=VMEM,
    )(*pieces)


def join_kernel(me_ref, *refs):
    pieces, out_ref, whole = refs[:-2], refs[-2], refs[-1]
    rows = pieces[0].shape[0]
    for k, piece in enumerate(pieces):
        whole[pl.ds(pl.multiple_of(me_ref[k] * rows, 8), rows), :] = piece[...]
    out_ref[...] = whole[:out_ref.shape[0], :]


def join_pieces(order, pieces, half):
    rows, width = pieces[0].shape
    return kernel_call(
        join_kernel, shape((half, width)),
        half * width, 8 * half * width,
        in_specs=[SMEM] + [VMEM] * len(pieces), out_specs=VMEM,
        scratch_shapes=[pltpu.VMEM((len(pieces) * rows, width), F32)],
    )(order, *pieces)


def relation_update_kernel(me_ref, relation_ref, state_ref, *refs):
    parts, out_ref, total = refs[:-2], refs[-2], refs[-1]
    groups = len(parts) // 2
    half, width = parts[0].shape
    group, core = me_ref[0], me_ref[1]
    for j in range(groups):
        at = pl.ds(pl.multiple_of((group ^ j) * width, LANES), width)
        total[pl.ds(pl.multiple_of(core * half, 8), half), at] = parts[j][...]
        total[pl.ds(pl.multiple_of((1 - core) * half, 8), half), at] = parts[groups + j][...]
    gradient = total[:, :out_ref.shape[1]]
    out_ref[...] = adagrad(relation_ref[...], state_ref[...], gradient)


def relation_update(me, relation, state, parts):
    features, count = relation.shape
    _, width = parts[0].shape
    groups = len(parts) // 2
    return kernel_call(
        relation_update_kernel, shape((features, count)),
        8 * features * count, 12 * features * count,
        in_specs=[SMEM] + [VMEM] * (2 + len(parts)), out_specs=VMEM,
        scratch_shapes=[pltpu.VMEM((features, groups * width), F32)],
    )(me, relation, state, *parts)


def sent_on(value, hop, peers):
    return lax.ppermute(value, "shard", [(i, partner(i, hop, peers, 1)) for i in range(peers)])


def sent_across(value, hop, peers, groups, by):
    pairs = [
        (g * peers + i, (g + by) % groups * peers + partner(i, hop, peers, 1))
        for g in range(groups)
        for i in range(peers)
    ]
    return lax.ppermute(value, ("group", "shard"), pairs)


def sent_group(value, bit, groups):
    return lax.ppermute(value, "group", [(g, g ^ bit) for g in range(groups)])


def relation_sum(kept, sent, peers, groups, chip):
    chips = peers // 2
    half = kept[0].shape[0]
    other_core = (0, 1)
    sent = [sent_on(b, other_core, peers) for b in sent]
    mine = [a + b for a, b in zip(kept, sent)]
    terms = [mine[0]] + [sent_group(mine[j], j, groups) for j in range(1, groups)]
    ahead = (chip + jnp.arange(chips, dtype=I32)) % chips
    behind = (chip - jnp.arange(chips, dtype=I32)) % chips
    pieces = cut_pieces(ahead, terms)
    pieces = [pieces[0]] + [sent_on(pieces[k], (k, 0), peers) for k in range(1, chips)]
    piece = sum_pieces(pieces)
    pieces = [piece] + [sent_on(piece, (k, 0), peers) for k in range(1, chips)]
    block = join_pieces(behind, pieces, half)
    blocks = [block] + [sent_group(block, j, groups) for j in range(1, groups)]
    return blocks + [sent_on(b, other_core, peers) for b in blocks]


def on_device(
    entity, entity_state, relation, relation_state, src_send, dst_send,
    edge_source, edge_relation, edge_target, neg_slots, edge_count,
):
    rows, _ = entity.shape
    relations = relation.shape[0]
    peers, block = src_send.shape[1:]
    groups = lax.axis_size("group")
    group = lax.axis_index("group").astype(I32)
    me = lax.axis_index("shard").astype(I32)
    width = pl.cdiv(relations, groups * LANES) * LANES
    entity_t, relation_t = entity.T, relation.T
    ways = hops(peers)
    order = jnp.stack([partner(me, hop, peers, 1) for hop in ways])
    here = jnp.stack([group, me % 2])

    def placed(slots):
        return places_of(me, slots // block, peers) * block + slots % block

    edge_source, edge_target = placed(edge_source), placed(edge_target)
    first = peers // 2
    sources = pick_blocks(order[:first], entity_t, src_send[0])
    sources += pick_blocks(order[first:], entity_t, src_send[0])
    sources = [
        sent_on(value, hop, peers) if hop != (0, 0) else value
        for value, hop in zip(sources, ways)
    ]
    targets = pick_blocks(order, entity_t, dst_send[0])
    targets = [sent_across(value, hop, peers, groups, -1) for value, hop in zip(targets, ways)]
    rels = relation_rows(relation_t, edge_relation.reshape(1, -1))
    counts = slot_counts(placed(neg_slots), peers * block)
    source_hots = home_hots(order, src_send[0], rows)
    target_hots = home_hots(order, dst_send[0], rows)
    heads, query_columns, query_lines = query_rows(sources, edge_source.reshape(1, -1), rels)
    loss, grad, table = score_spans(
        edge_count, targets, query_lines, counts, edge_target.reshape(-1, 1)
    )
    table_parts = table_grads(query_columns, grad, block, 0, 2)
    table_parts += table_grads(query_columns, grad, block, 2, peers - 2)
    back = [(-hop[0], hop[1]) for hop in ways]
    home = [
        sent_across(value, hop, peers, groups, 1)
        for value, hop in zip(table_parts[:2], back[:2])
    ]
    home += [
        sent_across(value, hop, peers, groups, 1)
        for value, hop in zip(table_parts[2:], back[2:])
    ]
    source_lines, *halves = relation_grads(
        here, table, grad, heads, rels, edge_relation.reshape(-1, 1), groups, width
    )
    source_parts = source_grads(source_lines, edge_source.reshape(-1, 1), peers, block)
    returned = []
    for value, hop, way in zip(source_parts, back, ways):
        returned.append(sent_on(value, hop, peers) if way != (0, 0) else value)
    parts = relation_sum(halves[:groups], halves[groups:], peers, groups, me // 2)
    relation_new = relation_update(here, relation_t, relation_state.reshape(1, -1), parts)
    target_part = target_home(target_hots, home)
    entity_new = entity_update(
        source_hots, returned, target_part, entity_t, entity_state.reshape(1, -1)
    )
    return entity_new.T, relation_new.T, loss.reshape(-1)


def solution(mesh):
    both = ("group", "shard")
    return jax.shard_map(
        on_device,
        mesh=mesh,
        in_specs=(
            P(both, None), P(both), P(), P(), P(both, None, None), P(both, None, None),
            P(both), P(both), P(both), P(both, None), P(both),
        ),
        out_specs=(P(both, None), P(), P(both)),
        check_vma=False,
    )
```

```python
import functools
import math

import jax
import jax.numpy as jnp
from jax import lax
from jax.experimental import pallas as pl
from jax.experimental.pallas import tpu as pltpu
from jax.sharding import PartitionSpec as P


SPAN = 512
LANES = 128
CHUNK = 256
WIDE = 512


learn_rate = 0.5

F32, BF16, I32 = jnp.float32, jnp.bfloat16, jnp.int32
VMEM = pl.BlockSpec(memory_space=pltpu.VMEM)
SMEM = pl.BlockSpec(memory_space=pltpu.SMEM)
VMEM_LIMIT = 60 << 20


def kernel_call(kernel, outs, flops, moved, **kw):
    semantics = ("arbitrary",) if "grid" in kw else None
    return pl.pallas_call(
        kernel,
        out_shape=outs,
        compiler_params=pltpu.CompilerParams(
            vmem_limit_bytes=VMEM_LIMIT, dimension_semantics=semantics
        ),
        cost_estimate=pl.CostEstimate(flops=flops, bytes_accessed=moved, transcendentals=0),
        **kw,
    )


def shape(dims, dtype=F32):
    return jax.ShapeDtypeStruct(dims, dtype)


def held(dims):
    return pl.BlockSpec(dims, lambda i: (0,) * len(dims))


def split2(x):
    hi = x.astype(BF16)
    return hi, (x - hi.astype(F32)).astype(BF16)


def split3(x):
    hi = x.astype(BF16)
    rest = x - hi.astype(F32)
    mid = rest.astype(BF16)
    return hi, mid, (rest - mid.astype(F32)).astype(BF16)


def dot(a, b):
    return jnp.dot(a, b, preferred_element_type=F32)


def dot_nt(a, b):
    return lax.dot_general(a, b, (((1,), (1,)), ((), ())), preferred_element_type=F32)


def one_hot(mask):
    return jnp.where(mask, 1.0, 0.0).astype(BF16)


def rows_hot(length, slots):
    return one_hot(lax.broadcasted_iota(I32, (length, slots.shape[1]), 0) == slots)


def columns_hot(slots, length):
    return one_hot(lax.broadcasted_iota(I32, (slots.shape[0], length), 1) == slots)


def complex_product(a, b):
    half = a.shape[0] // 2
    ar, ai, br, bi = a[:half], a[half:], b[:half], b[half:]
    return jnp.concatenate([ar * br - ai * bi, ar * bi + ai * br], axis=0)


def conj_product(a, b):
    half = a.shape[0] // 2
    ar, ai, br, bi = a[:half], a[half:], b[:half], b[half:]
    return jnp.concatenate([ar * br + ai * bi, ai * br - ar * bi], axis=0)


def hops(peers):
    chips = peers // 2
    ahead = [(k, b) for k in range(1, chips) for b in (0, 1)]
    return ahead + [(0, 1), (0, 0)]


def partner(me, hop, peers, sign):
    chips = peers // 2
    return (me // 2 + sign * hop[0]) % chips * 2 + (me % 2 + hop[1]) % 2


def places_of(me, owner, peers):
    chips = peers // 2
    k = (me // 2 - owner // 2) % chips
    b = (me + owner) % 2
    return (k - 1) % chips * 2 + jnp.where(k == 0, 1 - b, b)


def pick_kernel(order_ref, rows_ref, slots_ref, *outs):
    hi, mid, lo = split3(rows_ref[...])
    block = slots_ref.shape[1]
    together = max(1, CHUNK // block)
    for first in range(0, len(outs), together):
        group = outs[first:first + together]
        slots = [slots_ref[pl.ds(order_ref[first + i], 1), :] for i in range(len(group))]
        hot = rows_hot(rows_ref.shape[1], jnp.concatenate(slots, axis=1))
        picked = dot(hi, hot) + dot(mid, hot) + dot(lo, hot)
        for i, out in enumerate(group):
            out[...] = picked[:, i * block:(i + 1) * block]


def pick_blocks(order, rows, slots):
    features, length = rows.shape
    block = slots.shape[1]
    count = order.shape[0]
    return kernel_call(
        pick_kernel, [shape((features, block))] * count,
        6 * features * length * count * block, 8 * features * count * block,
        in_specs=[SMEM, VMEM, VMEM], out_specs=[VMEM] * count,
    )(order, rows, slots)


def relation_kernel(rel_ref, edge_rel_ref, out_ref, pieces):
    count = rel_ref.shape[1]
    padded = pieces.shape[2]

    @pl.when(pl.program_id(0) == 0)
    def _():
        features = rel_ref.shape[0]
        tail = padded - count // LANES * LANES
        for piece, value in enumerate(split3(rel_ref[...])):
            pieces[piece, :, padded - tail:] = jnp.zeros((features, tail), BF16)
            pieces[piece, :, :count] = value

    hot = rows_hot(padded, edge_rel_ref[...])
    out_ref[...] = dot(pieces[0], hot) + dot(pieces[1], hot) + dot(pieces[2], hot)


def relation_rows(relation, edge_relation):
    features, count = relation.shape
    edges = edge_relation.shape[1]
    padded = pl.cdiv(count, LANES) * LANES
    return kernel_call(
        relation_kernel, shape((features, edges)),
        6 * features * padded * edges, 8 * features * edges,
        grid=(edges // CHUNK,),
        in_specs=[held((features, count)), pl.BlockSpec((1, CHUNK), lambda i: (0, i))],
        out_specs=pl.BlockSpec((features, CHUNK), lambda i: (0, i)),
        scratch_shapes=[pltpu.VMEM((3, features, padded), BF16)],
    )(relation, edge_relation)


def count_kernel(slots_ref, out_ref):
    table_rows = out_ref.shape[2]
    hits = lax.broadcasted_iota(I32, (slots_ref.shape[1], table_rows), 1) == slots_ref[0]
    counts = jnp.sum(jnp.where(hits, 1.0, 0.0), axis=0, keepdims=True)
    out_ref[0] = jnp.where(counts > 0.0, jnp.log(jnp.maximum(counts, 1.0)), -jnp.inf)


def slot_counts(neg_slots, table_rows):
    spans, negatives = neg_slots.shape
    return kernel_call(
        count_kernel, shape((spans, 1, table_rows)),
        2 * spans * negatives * table_rows, 512 * spans * negatives,
        grid=(spans,),
        in_specs=[pl.BlockSpec((1, negatives, 1), lambda i: (i, 0, 0))],
        out_specs=pl.BlockSpec((1, 1, table_rows), lambda i: (i, 0, 0)),
    )(neg_slots[:, :, None])


def hot_kernel(order_ref, slots_ref, out_ref):
    peers, block, _ = slots_ref.shape
    for j in range(peers):
        out_ref[j * block:(j + 1) * block, :] = columns_hot(slots_ref[order_ref[j]], out_ref.shape[1])


def home_hots(order, slots, rows):
    peers, block = slots.shape
    return kernel_call(
        hot_kernel, shape((peers * block, rows), BF16),
        2 * peers * block * rows, 2 * peers * block * rows,
        in_specs=[SMEM, VMEM], out_specs=VMEM,
    )(order, slots[:, :, None])


def query_kernel(*refs):
    edge_source_ref, rels_ref, *blocks = refs[:-4]
    heads_ref, columns_ref, rows_ref, pieces = refs[-4:]
    block = blocks[0].shape[1]

    @pl.when(pl.program_id(0) == 0)
    def _():
        for p, ref in enumerate(blocks):
            for piece, value in enumerate(split3(ref[...])):
                pieces[piece, :, p * block:(p + 1) * block] = value

    hot = rows_hot(pieces.shape[2], edge_source_ref[...])
    heads = dot(pieces[0], hot) + dot(pieces[1], hot) + dot(pieces[2], hot)
    heads_ref[...] = heads
    queries = complex_product(heads, rels_ref[...])
    hi, lo = split2(queries)
    columns_ref[0], columns_ref[1] = hi, lo
    hi, lo = split2(queries.T)
    rows_ref[...] = jnp.concatenate([hi, hi, lo], axis=1)


def query_rows(blocks, edge_source, rels):
    peers = len(blocks)
    features, block = blocks[0].shape
    edges = edge_source.shape[1]
    return kernel_call(
        query_kernel,
        [shape((features, edges)), shape((2, features, edges), BF16), shape((edges, 3 * features), BF16)],
        6 * features * peers * block * edges, 20 * features * edges,
        grid=(edges // CHUNK,),
        in_specs=[
            pl.BlockSpec((1, CHUNK), lambda i: (0, i)),
            pl.BlockSpec((features, CHUNK), lambda i: (0, i)),
        ] + [held((features, block))] * peers,
        out_specs=[
            pl.BlockSpec((features, CHUNK), lambda i: (0, i)),
            pl.BlockSpec((2, features, CHUNK), lambda i: (0, 0, i)),
            pl.BlockSpec((CHUNK, 3 * features), lambda i: (i, 0)),
        ],
        scratch_shapes=[pltpu.VMEM((3, features, peers * block), BF16)],
    )(edge_source, rels, *blocks)


def softmax_step(step, live, score, log_counts, edge_target, loss_ref, grad_ref):
    own = lax.broadcasted_iota(I32, score.shape, 1) == edge_target
    pos = jnp.sum(jnp.where(own, score, 0.0), axis=1, keepdims=True)
    score = score + log_counts
    peak = jnp.maximum(pos, jnp.max(score, axis=1, keepdims=True))
    weight = jnp.exp(score - peak)
    pos_weight = jnp.exp(pos - peak)
    sum_all = pos_weight + jnp.sum(weight, axis=1, keepdims=True)
    edge = step * score.shape[0] + lax.broadcasted_iota(I32, pos.shape, 0)
    is_live = jnp.where(edge < live, 1.0, 0.0)
    loss_ref[...] = (peak - pos + jnp.log(sum_all)) * is_live
    scale = is_live / sum_all
    pos_grad = pos_weight * scale - is_live
    grad = weight * scale + jnp.where(own, pos_grad, 0.0)
    grad_ref[0], grad_ref[1] = split2(grad)


def score_kernel(peers, *refs):
    live_ref, rows_ref, counts_ref, edge_target_ref = refs[:4]
    blocks = refs[4:4 + peers]
    loss_ref, grad_ref, table_ref, scores = refs[4 + peers:]
    features, block = blocks[0].shape
    step = pl.program_id(0)
    last = pl.num_programs(0) - 1

    @pl.when(step == 0)
    def _():
        for p, ref in enumerate(blocks):
            hi, lo = split2(ref[...])
            at = pl.ds(p * block, block)
            table_ref[:features, at] = hi
            table_ref[features:2 * features, at] = lo
            table_ref[2 * features:, at] = hi

    def multiply():
        scores[step % 2] = dot(rows_ref[...], table_ref[...])

    def finish():
        softmax_step(
            step - 1, live_ref[0], scores[(step + 1) % 2], counts_ref[0], edge_target_ref[...],
            loss_ref, grad_ref,
        )

    @pl.when(step == 0)
    def _():
        multiply()

    @pl.when((step > 0) & (step < last))
    def _():
        multiply()
        finish()

    @pl.when(step == last)
    def _():
        finish()


def score_spans(live, blocks, rows, counts, edge_target):
    peers = len(blocks)
    features, block = blocks[0].shape
    edges = edge_target.shape[0]
    table_rows = peers * block
    chunk = CHUNK
    per_span = SPAN // chunk
    steps = edges // chunk

    def now(i):
        return jnp.minimum(i, steps - 1)

    def before(i):
        return jnp.maximum(i - 1, 0)

    return kernel_call(
        functools.partial(score_kernel, peers),
        [
            shape((edges, 1)),
            shape((2, edges, table_rows), BF16),
            shape((3 * features, table_rows), BF16),
        ],
        6 * features * table_rows * edges, 30 * features * edges,
        grid=(steps + 1,),
        in_specs=[
            SMEM,
            pl.BlockSpec((chunk, 3 * features), lambda i: (now(i), 0)),
            pl.BlockSpec((1, 1, table_rows), lambda i: (before(i) // per_span, 0, 0)),
            pl.BlockSpec((chunk, 1), lambda i: (before(i), 0)),
        ] + [held((features, block))] * peers,
        out_specs=[
            pl.BlockSpec((chunk, 1), lambda i: (before(i), 0)),
            pl.BlockSpec((2, chunk, table_rows), lambda i: (0, before(i), 0)),
            held((3 * features, table_rows)),
        ],
        scratch_shapes=[pltpu.VMEM((2, chunk, table_rows), F32)],
    )(live, rows, counts, edge_target, *blocks)


def table_grad_kernel(columns_ref, grad_ref, *outs):
    step = pl.program_id(0)
    block = outs[0].shape[1]
    result = (
        dot(columns_ref[0], grad_ref[0])
        + dot(columns_ref[0], grad_ref[1])
        + dot(columns_ref[1], grad_ref[0])
    )
    for pair in range(len(outs) // 2):
        @pl.when(step == pair)
        def _():
            outs[2 * pair][...] = result[:, :block]
            outs[2 * pair + 1][...] = result[:, block:]


def table_grads(columns, grad, block, first, count):
    _, features, edges = columns.shape
    return kernel_call(
        table_grad_kernel, [shape((features, block))] * count,
        6 * features * count * block * edges, 4 * edges * (features + count * block),
        grid=(count // 2,),
        in_specs=[
            held((2, features, edges)),
            pl.BlockSpec((2, edges, 2 * block), lambda i: (0, 0, first // 2 + i)),
        ],
        out_specs=[held((features, block))] * count,
    )(columns, grad)


def relation_grad_kernel(
    steps, me_ref, table_ref, grad_ref, heads_ref, rels_ref, edge_rel_ref, source_ref, *refs
):
    outs, lines, total = refs[:-2], refs[-2], refs[-1]
    groups = len(outs) // 2
    half, width = outs[0].shape
    step = pl.program_id(0)
    features, chunk = heads_ref.shape
    tile = total.shape[2]

    @pl.when(step < steps)
    def _():
        hi, lo = table_ref[:features], table_ref[features:2 * features]
        query_grad = dot_nt(hi, grad_ref[0]) + dot_nt(hi, grad_ref[1]) + dot_nt(lo, grad_ref[0])
        source_ref[0], source_ref[1] = split2(conj_product(query_grad, rels_ref[...]))
        lines[step] = jnp.concatenate(split2(conj_product(query_grad, heads_ref[...])), axis=1)

    @pl.when(step >= steps)
    def _():
        part = None
        for i in range(steps):
            slots = edge_rel_ref[i * chunk:(i + 1) * chunk, :] - (step - steps) * tile
            hot = columns_hot(slots, tile)
            term = dot(lines[i, :, :chunk], hot) + dot(lines[i, :, chunk:], hot)
            part = term if part is None else part + term
        total[step - steps] = part

    @pl.when(step == pl.num_programs(0) - 1)
    def _():
        group, core = me_ref[0], me_ref[1]
        for j in range(groups):
            for at in range(0, width, LANES):
                start = (group ^ j) * width + at
                rows = total.at[start // tile, :, pl.ds(pl.multiple_of(start % tile, LANES), LANES)]
                outs[j][:, at:at + LANES] = rows[pl.ds(pl.multiple_of(core * half, 8), half), :]
                outs[groups + j][:, at:at + LANES] = rows[
                    pl.ds(pl.multiple_of((1 - core) * half, 8), half), :
                ]


def relation_grads(me, table, grad, heads, rels, edge_relation, groups, width):
    features, edges = heads.shape
    table_rows = table.shape[1]
    chunk = CHUNK
    steps = edges // chunk
    tile = math.gcd(groups * width, WIDE)
    tiles = groups * width // tile

    def now(i):
        return jnp.minimum(i, steps - 1)

    return kernel_call(
        functools.partial(relation_grad_kernel, steps),
        [shape((2, features, edges), BF16)] + [shape((features // 2, width))] * (2 * groups),
        10 * features * table_rows * edges, 30 * features * edges,
        grid=(steps + tiles,),
        in_specs=[
            SMEM,
            held((3 * features, table_rows)),
            pl.BlockSpec((2, chunk, table_rows), lambda i: (0, now(i), 0)),
            pl.BlockSpec((features, chunk), lambda i: (0, now(i))),
            pl.BlockSpec((features, chunk), lambda i: (0, now(i))),
            held((edges, 1)),
        ],
        out_specs=[pl.BlockSpec((2, features, chunk), lambda i: (0, 0, now(i)))]
        + [held((features // 2, width))] * (2 * groups),
        scratch_shapes=[
            pltpu.VMEM((steps, features, 2 * chunk), BF16),
            pltpu.VMEM((tiles, features, tile), F32),
        ],
    )(me, table, grad, heads, rels, edge_relation)


def source_grad_kernel(rows_ref, edge_source_ref, *refs):
    outs, total = refs[:-1], refs[-1]
    block = outs[0].shape[1]
    step = pl.program_id(0)

    @pl.when(step == 0)
    def _():
        total[...] = jnp.zeros_like(total)

    hot = columns_hot(edge_source_ref[...], total.shape[1])
    total[...] += dot(rows_ref[0], hot) + dot(rows_ref[1], hot)

    @pl.when(step == pl.num_programs(0) - 1)
    def _():
        for p, ref in enumerate(outs):
            ref[...] = total[:, p * block:(p + 1) * block]


def source_grads(rows, edge_source, peers, block):
    _, features, edges = rows.shape
    return kernel_call(
        source_grad_kernel, [shape((features, block))] * peers,
        4 * features * peers * block * edges, 12 * features * edges,
        grid=(edges // CHUNK,),
        in_specs=[
            pl.BlockSpec((2, features, CHUNK), lambda i: (0, 0, i)),
            pl.BlockSpec((CHUNK, 1), lambda i: (i, 0)),
        ],
        out_specs=[held((features, block))] * peers,
        scratch_shapes=[pltpu.VMEM((features, peers * block), F32)],
    )(rows, edge_source)


def put_back(blocks, hot_ref):
    hi, lo = split2(jnp.concatenate([ref[...] for ref in blocks], axis=1))
    return dot(hi, hot_ref[...]) + dot(lo, hot_ref[...])


def target_home_kernel(hot_ref, *refs):
    refs[-1][...] = put_back(refs[:-1], hot_ref)


def target_home(hots, blocks):
    features = blocks[0].shape[0]
    rows = hots.shape[1]
    return kernel_call(
        target_home_kernel, shape((features, rows)),
        4 * features * rows * hots.shape[0], 8 * features * hots.shape[0],
        in_specs=[VMEM] * (1 + len(blocks)), out_specs=VMEM,
    )(hots, *blocks)


def adagrad(params, state, gradient):
    new_state = state + jnp.mean(gradient * gradient, axis=0, keepdims=True)
    return params - learn_rate * gradient / jnp.sqrt(new_state)


def entity_kernel(other_ref, entity_ref, state_ref, hot_ref, *refs):
    gradient = other_ref[...] + put_back(refs[:-1], hot_ref)
    refs[-1][...] = adagrad(entity_ref[...], state_ref[...], gradient)


def entity_update(hots, blocks, other, entity, state):
    features, rows = entity.shape
    return kernel_call(
        entity_kernel, shape((features, rows)),
        4 * features * rows * hots.shape[0], 8 * features * hots.shape[0],
        in_specs=[VMEM] * (4 + len(blocks)), out_specs=VMEM,
    )(other, entity, state, hots, *blocks)


def cut_kernel(me_ref, *refs):
    chips = me_ref.shape[0]
    terms, outs, whole = refs[:-1 - chips], refs[-1 - chips:-1], refs[-1]
    rows, width = outs[0].shape
    have = terms[0].shape[0]
    total = terms[0][...]
    for term in terms[1:]:
        total = total + term[...]
    whole[:have, :] = total
    if have < chips * rows:
        whole[have:, :] = jnp.zeros((chips * rows - have, width), F32)
    for k, out in enumerate(outs):
        out[...] = whole[pl.ds(pl.multiple_of(me_ref[k] * rows, 8), rows), :]


def cut_pieces(order, terms):
    chips = order.shape[0]
    half, width = terms[0].shape
    rows = pl.cdiv(half, 8 * chips) * 8
    return kernel_call(
        cut_kernel, [shape((rows, width))] * chips,
        len(terms) * half * width, 4 * (len(terms) + 1) * half * width,
        in_specs=[SMEM] + [VMEM] * len(terms), out_specs=[VMEM] * chips,
        scratch_shapes=[pltpu.VMEM((chips * rows, width), F32)],
    )(order, *terms)


def sum_kernel(*refs):
    total = refs[0][...]
    for ref in refs[1:-1]:
        total = total + ref[...]
    refs[-1][...] = total


def sum_pieces(pieces):
    rows, width = pieces[0].shape
    return kernel_call(
        sum_kernel, shape((rows, width)),
        len(pieces) * rows * width, 4 * (len(pieces) + 1) * rows * width,
        in_specs=[VMEM] * len(pieces), out_specs=VMEM,
    )(*pieces)


def join_kernel(me_ref, *refs):
    pieces, out_ref, whole = refs[:-2], refs[-2], refs[-1]
    rows = pieces[0].shape[0]
    for k, piece in enumerate(pieces):
        whole[pl.ds(pl.multiple_of(me_ref[k] * rows, 8), rows), :] = piece[...]
    out_ref[...] = whole[:out_ref.shape[0], :]


def join_pieces(order, pieces, half):
    rows, width = pieces[0].shape
    return kernel_call(
        join_kernel, shape((half, width)),
        half * width, 8 * half * width,
        in_specs=[SMEM] + [VMEM] * len(pieces), out_specs=VMEM,
        scratch_shapes=[pltpu.VMEM((len(pieces) * rows, width), F32)],
    )(order, *pieces)


def relation_update_kernel(me_ref, relation_ref, state_ref, *refs):
    parts, out_ref, total = refs[:-2], refs[-2], refs[-1]
    groups = len(parts) // 2
    half, width = parts[0].shape
    group, core = me_ref[0], me_ref[1]
    for j in range(groups):
        at = pl.ds(pl.multiple_of((group ^ j) * width, LANES), width)
        total[pl.ds(pl.multiple_of(core * half, 8), half), at] = parts[j][...]
        total[pl.ds(pl.multiple_of((1 - core) * half, 8), half), at] = parts[groups + j][...]
    gradient = total[:, :out_ref.shape[1]]
    out_ref[...] = adagrad(relation_ref[...], state_ref[...], gradient)


def relation_update(me, relation, state, parts):
    features, count = relation.shape
    _, width = parts[0].shape
    groups = len(parts) // 2
    return kernel_call(
        relation_update_kernel, shape((features, count)),
        8 * features * count, 12 * features * count,
        in_specs=[SMEM] + [VMEM] * (2 + len(parts)), out_specs=VMEM,
        scratch_shapes=[pltpu.VMEM((features, groups * width), F32)],
    )(me, relation, state, *parts)


def sent_on(value, hop, peers):
    return lax.ppermute(value, "shard", [(i, partner(i, hop, peers, 1)) for i in range(peers)])


def sent_across(value, hop, peers, groups, by):
    pairs = [
        (g * peers + i, (g + by) % groups * peers + partner(i, hop, peers, 1))
        for g in range(groups)
        for i in range(peers)
    ]
    return lax.ppermute(value, ("group", "shard"), pairs)


def sent_group(value, bit, groups):
    return lax.ppermute(value, "group", [(g, g ^ bit) for g in range(groups)])


def relation_sum(kept, sent, peers, groups, chip):
    chips = peers // 2
    half = kept[0].shape[0]
    other_core = (0, 1)
    sent = [sent_on(b, other_core, peers) for b in sent]
    mine = [a + b for a, b in zip(kept, sent)]
    terms = [mine[0]] + [sent_group(mine[j], j, groups) for j in range(1, groups)]
    ahead = (chip + jnp.arange(chips, dtype=I32)) % chips
    behind = (chip - jnp.arange(chips, dtype=I32)) % chips
    pieces = cut_pieces(ahead, terms)
    pieces = [pieces[0]] + [sent_on(pieces[k], (k, 0), peers) for k in range(1, chips)]
    piece = sum_pieces(pieces)
    pieces = [piece] + [sent_on(piece, (k, 0), peers) for k in range(1, chips)]
    block = join_pieces(behind, pieces, half)
    blocks = [block] + [sent_group(block, j, groups) for j in range(1, groups)]
    return blocks + [sent_on(b, other_core, peers) for b in blocks]


def on_device(
    entity, entity_state, relation, relation_state, src_send, dst_send,
    edge_source, edge_relation, edge_target, neg_slots, edge_count,
):
    rows, _ = entity.shape
    relations = relation.shape[0]
    peers, block = src_send.shape[1:]
    groups = lax.axis_size("group")
    group = lax.axis_index("group").astype(I32)
    me = lax.axis_index("shard").astype(I32)
    width = pl.cdiv(relations, groups * LANES) * LANES
    entity_t, relation_t = entity.T, relation.T
    ways = hops(peers)
    order = jnp.stack([partner(me, hop, peers, 1) for hop in ways])
    here = jnp.stack([group, me % 2])

    def placed(slots):
        return places_of(me, slots // block, peers) * block + slots % block

    edge_source, edge_target = placed(edge_source), placed(edge_target)
    first = peers // 2
    sources = pick_blocks(order[:first], entity_t, src_send[0])
    sources += pick_blocks(order[first:], entity_t, src_send[0])
    sources = [
        sent_on(value, hop, peers) if hop != (0, 0) else value
        for value, hop in zip(sources, ways)
    ]
    targets = pick_blocks(order, entity_t, dst_send[0])
    targets = [sent_across(value, hop, peers, groups, -1) for value, hop in zip(targets, ways)]
    rels = relation_rows(relation_t, edge_relation.reshape(1, -1))
    counts = slot_counts(placed(neg_slots), peers * block)
    source_hots = home_hots(order, src_send[0], rows)
    target_hots = home_hots(order, dst_send[0], rows)
    heads, query_columns, query_lines = query_rows(sources, edge_source.reshape(1, -1), rels)
    loss, grad, table = score_spans(
        edge_count, targets, query_lines, counts, edge_target.reshape(-1, 1)
    )
    table_parts = table_grads(query_columns, grad, block, 0, first)
    table_parts += table_grads(query_columns, grad, block, first, peers - first)
    back = [(-hop[0], hop[1]) for hop in ways]
    home = [
        sent_across(value, hop, peers, groups, 1)
        for value, hop in zip(table_parts[:first], back[:first])
    ]
    home += [
        sent_across(value, hop, peers, groups, 1)
        for value, hop in zip(table_parts[first:], back[first:])
    ]
    source_lines, *halves = relation_grads(
        here, table, grad, heads, rels, edge_relation.reshape(-1, 1), groups, width
    )
    source_parts = source_grads(source_lines, edge_source.reshape(-1, 1), peers, block)
    returned = []
    for value, hop, way in zip(source_parts, back, ways):
        returned.append(sent_on(value, hop, peers) if way != (0, 0) else value)
    parts = relation_sum(halves[:groups], halves[groups:], peers, groups, me // 2)
    relation_new = relation_update(here, relation_t, relation_state.reshape(1, -1), parts)
    target_part = target_home(target_hots, home)
    entity_new = entity_update(
        source_hots, returned, target_part, entity_t, entity_state.reshape(1, -1)
    )
    return entity_new.T, relation_new.T, loss.reshape(-1)


def solution(mesh):
    both = ("group", "shard")
    return jax.shard_map(
        on_device,
        mesh=mesh,
        in_specs=(
            P(both, None), P(both), P(), P(), P(both, None, None), P(both, None, None),
            P(both), P(both), P(both), P(both, None), P(both),
        ),
        out_specs=(P(both, None), P(), P(both)),
        check_vma=False,
    )
```

```python
import functools
import math

import jax
import jax.numpy as jnp
from jax import lax
from jax.experimental import pallas as pl
from jax.experimental.pallas import tpu as pltpu
from jax.sharding import PartitionSpec as P


SPAN = 512
LANES = 128
CHUNK = 256
WIDE = 512


learn_rate = 0.5

F32, BF16, I32 = jnp.float32, jnp.bfloat16, jnp.int32
VMEM = pl.BlockSpec(memory_space=pltpu.VMEM)
SMEM = pl.BlockSpec(memory_space=pltpu.SMEM)
VMEM_LIMIT = 32 << 20


def kernel_call(kernel, outs, flops, moved, **kw):
    semantics = ("arbitrary",) if "grid" in kw else None
    return pl.pallas_call(
        kernel,
        out_shape=outs,
        compiler_params=pltpu.CompilerParams(
            vmem_limit_bytes=VMEM_LIMIT, dimension_semantics=semantics
        ),
        cost_estimate=pl.CostEstimate(flops=flops, bytes_accessed=moved, transcendentals=0),
        **kw,
    )


def shape(dims, dtype=F32):
    return jax.ShapeDtypeStruct(dims, dtype)


def held(dims):
    return pl.BlockSpec(dims, lambda i: (0,) * len(dims))


def split2(x):
    hi = x.astype(BF16)
    return hi, (x - hi.astype(F32)).astype(BF16)


def split3(x):
    hi = x.astype(BF16)
    rest = x - hi.astype(F32)
    mid = rest.astype(BF16)
    return hi, mid, (rest - mid.astype(F32)).astype(BF16)


def dot(a, b):
    return jnp.dot(a, b, preferred_element_type=F32)


def dot_nt(a, b):
    return lax.dot_general(a, b, (((1,), (1,)), ((), ())), preferred_element_type=F32)


def one_hot(mask):
    return jnp.where(mask, 1.0, 0.0).astype(BF16)


def rows_hot(length, slots):
    return one_hot(lax.broadcasted_iota(I32, (length, slots.shape[1]), 0) == slots)


def columns_hot(slots, length):
    return one_hot(lax.broadcasted_iota(I32, (slots.shape[0], length), 1) == slots)


def complex_product(a, b):
    half = a.shape[0] // 2
    ar, ai, br, bi = a[:half], a[half:], b[:half], b[half:]
    return jnp.concatenate([ar * br - ai * bi, ar * bi + ai * br], axis=0)


def conj_product(a, b):
    half = a.shape[0] // 2
    ar, ai, br, bi = a[:half], a[half:], b[:half], b[half:]
    return jnp.concatenate([ar * br + ai * bi, ai * br - ar * bi], axis=0)


def hops(peers):
    chips = peers // 2
    ahead = [(k, b) for k in range(1, chips) for b in (0, 1)]
    return ahead + [(0, 1), (0, 0)]


def partner(me, hop, peers, sign):
    chips = peers // 2
    return (me // 2 + sign * hop[0]) % chips * 2 + (me % 2 + hop[1]) % 2


def places_of(me, owner, peers):
    chips = peers // 2
    k = (me // 2 - owner // 2) % chips
    b = (me + owner) % 2
    return (k - 1) % chips * 2 + jnp.where(k == 0, 1 - b, b)


def pick_kernel(order_ref, rows_ref, slots_ref, *outs):
    hi, mid, lo = split3(rows_ref[...])
    block = slots_ref.shape[1]
    together = max(1, CHUNK // block)
    for first in range(0, len(outs), together):
        group = outs[first:first + together]
        slots = [slots_ref[pl.ds(order_ref[first + i], 1), :] for i in range(len(group))]
        hot = rows_hot(rows_ref.shape[1], jnp.concatenate(slots, axis=1))
        picked = dot(hi, hot) + dot(mid, hot) + dot(lo, hot)
        for i, out in enumerate(group):
            out[...] = picked[:, i * block:(i + 1) * block]


def pick_blocks(order, rows, slots):
    features, length = rows.shape
    block = slots.shape[1]
    count = order.shape[0]
    return kernel_call(
        pick_kernel, [shape((features, block))] * count,
        6 * features * length * count * block, 8 * features * count * block,
        in_specs=[SMEM, VMEM, VMEM], out_specs=[VMEM] * count,
    )(order, rows, slots)


def relation_kernel(rel_ref, edge_rel_ref, out_ref, pieces):
    count = rel_ref.shape[1]
    padded = pieces.shape[2]

    @pl.when(pl.program_id(0) == 0)
    def _():
        features = rel_ref.shape[0]
        tail = padded - count // LANES * LANES
        for piece, value in enumerate(split3(rel_ref[...])):
            pieces[piece, :, padded - tail:] = jnp.zeros((features, tail), BF16)
            pieces[piece, :, :count] = value

    hot = rows_hot(padded, edge_rel_ref[...])
    out_ref[...] = dot(pieces[0], hot) + dot(pieces[1], hot) + dot(pieces[2], hot)


def relation_rows(relation, edge_relation):
    features, count = relation.shape
    edges = edge_relation.shape[1]
    padded = pl.cdiv(count, LANES) * LANES
    return kernel_call(
        relation_kernel, shape((features, edges)),
        6 * features * padded * edges, 8 * features * edges,
        grid=(edges // CHUNK,),
        in_specs=[held((features, count)), pl.BlockSpec((1, CHUNK), lambda i: (0, i))],
        out_specs=pl.BlockSpec((features, CHUNK), lambda i: (0, i)),
        scratch_shapes=[pltpu.VMEM((3, features, padded), BF16)],
    )(relation, edge_relation)


def count_kernel(slots_ref, out_ref):
    table_rows = out_ref.shape[2]
    hits = lax.broadcasted_iota(I32, (slots_ref.shape[1], table_rows), 1) == slots_ref[0]
    counts = jnp.sum(jnp.where(hits, 1.0, 0.0), axis=0, keepdims=True)
    out_ref[0] = jnp.where(counts > 0.0, jnp.log(jnp.maximum(counts, 1.0)), -jnp.inf)


def slot_counts(neg_slots, table_rows):
    spans, negatives = neg_slots.shape
    return kernel_call(
        count_kernel, shape((spans, 1, table_rows)),
        2 * spans * negatives * table_rows, 512 * spans * negatives,
        grid=(spans,),
        in_specs=[pl.BlockSpec((1, negatives, 1), lambda i: (i, 0, 0))],
        out_specs=pl.BlockSpec((1, 1, table_rows), lambda i: (i, 0, 0)),
    )(neg_slots[:, :, None])


def hot_kernel(order_ref, slots_ref, out_ref):
    peers, block, _ = slots_ref.shape
    for j in range(peers):
        out_ref[j * block:(j + 1) * block, :] = columns_hot(slots_ref[order_ref[j]], out_ref.shape[1])


def home_hots(order, slots, rows):
    peers, block = slots.shape
    return kernel_call(
        hot_kernel, shape((peers * block, rows), BF16),
        2 * peers * block * rows, 2 * peers * block * rows,
        in_specs=[SMEM, VMEM], out_specs=VMEM,
    )(order, slots[:, :, None])


def query_kernel(*refs):
    edge_source_ref, rels_ref, *blocks = refs[:-4]
    heads_ref, columns_ref, rows_ref, pieces = refs[-4:]
    block = blocks[0].shape[1]

    @pl.when(pl.program_id(0) == 0)
    def _():
        for p, ref in enumerate(blocks):
            for piece, value in enumerate(split3(ref[...])):
                pieces[piece, :, p * block:(p + 1) * block] = value

    hot = rows_hot(pieces.shape[2], edge_source_ref[...])
    heads = dot(pieces[0], hot) + dot(pieces[1], hot) + dot(pieces[2], hot)
    heads_ref[...] = heads
    queries = complex_product(heads, rels_ref[...])
    hi, lo = split2(queries)
    columns_ref[0], columns_ref[1] = hi, lo
    hi, lo = split2(queries.T)
    rows_ref[...] = jnp.concatenate([hi, hi, lo], axis=1)


def query_rows(blocks, edge_source, rels):
    peers = len(blocks)
    features, block = blocks[0].shape
    edges = edge_source.shape[1]
    return kernel_call(
        query_kernel,
        [shape((features, edges)), shape((2, features, edges), BF16), shape((edges, 3 * features), BF16)],
        6 * features * peers * block * edges, 20 * features * edges,
        grid=(edges // CHUNK,),
        in_specs=[
            pl.BlockSpec((1, CHUNK), lambda i: (0, i)),
            pl.BlockSpec((features, CHUNK), lambda i: (0, i)),
        ] + [held((features, block))] * peers,
        out_specs=[
            pl.BlockSpec((features, CHUNK), lambda i: (0, i)),
            pl.BlockSpec((2, features, CHUNK), lambda i: (0, 0, i)),
            pl.BlockSpec((CHUNK, 3 * features), lambda i: (i, 0)),
        ],
        scratch_shapes=[pltpu.VMEM((3, features, peers * block), BF16)],
    )(edge_source, rels, *blocks)


def softmax_step(step, live, score, log_counts, edge_target, loss_ref, grad_ref):
    own = lax.broadcasted_iota(I32, score.shape, 1) == edge_target
    pos = jnp.sum(jnp.where(own, score, 0.0), axis=1, keepdims=True)
    score = score + log_counts
    peak = jnp.maximum(pos, jnp.max(score, axis=1, keepdims=True))
    weight = jnp.exp(score - peak)
    pos_weight = jnp.exp(pos - peak)
    sum_all = pos_weight + jnp.sum(weight, axis=1, keepdims=True)
    edge = step * score.shape[0] + lax.broadcasted_iota(I32, pos.shape, 0)
    is_live = jnp.where(edge < live, 1.0, 0.0)
    loss_ref[...] = (peak - pos + jnp.log(sum_all)) * is_live
    scale = is_live / sum_all
    pos_grad = pos_weight * scale - is_live
    grad = weight * scale + jnp.where(own, pos_grad, 0.0)
    grad_ref[0], grad_ref[1] = split2(grad)


def score_kernel(peers, *refs):
    live_ref, rows_ref, counts_ref, edge_target_ref = refs[:4]
    blocks = refs[4:4 + peers]
    loss_ref, grad_ref, table_ref, scores = refs[4 + peers:]
    features, block = blocks[0].shape
    step = pl.program_id(0)
    last = pl.num_programs(0) - 1

    @pl.when(step == 0)
    def _():
        for p, ref in enumerate(blocks):
            hi, lo = split2(ref[...])
            at = pl.ds(p * block, block)
            table_ref[:features, at] = hi
            table_ref[features:2 * features, at] = lo
            table_ref[2 * features:, at] = hi

    def multiply():
        scores[step % 2] = dot(rows_ref[...], table_ref[...])

    def finish():
        softmax_step(
            step - 1, live_ref[0], scores[(step + 1) % 2], counts_ref[0], edge_target_ref[...],
            loss_ref, grad_ref,
        )

    @pl.when(step == 0)
    def _():
        multiply()

    @pl.when((step > 0) & (step < last))
    def _():
        multiply()
        finish()

    @pl.when(step == last)
    def _():
        finish()


def score_spans(live, blocks, rows, counts, edge_target):
    peers = len(blocks)
    features, block = blocks[0].shape
    edges = edge_target.shape[0]
    table_rows = peers * block
    chunk = CHUNK
    per_span = SPAN // chunk
    steps = edges // chunk

    def now(i):
        return jnp.minimum(i, steps - 1)

    def before(i):
        return jnp.maximum(i - 1, 0)

    return kernel_call(
        functools.partial(score_kernel, peers),
        [
            shape((edges, 1)),
            shape((2, edges, table_rows), BF16),
            shape((3 * features, table_rows), BF16),
        ],
        6 * features * table_rows * edges, 30 * features * edges,
        grid=(steps + 1,),
        in_specs=[
            SMEM,
            pl.BlockSpec((chunk, 3 * features), lambda i: (now(i), 0)),
            pl.BlockSpec((1, 1, table_rows), lambda i: (before(i) // per_span, 0, 0)),
            pl.BlockSpec((chunk, 1), lambda i: (before(i), 0)),
        ] + [held((features, block))] * peers,
        out_specs=[
            pl.BlockSpec((chunk, 1), lambda i: (before(i), 0)),
            pl.BlockSpec((2, chunk, table_rows), lambda i: (0, before(i), 0)),
            held((3 * features, table_rows)),
        ],
        scratch_shapes=[pltpu.VMEM((2, chunk, table_rows), F32)],
    )(live, rows, counts, edge_target, *blocks)


def table_grad_kernel(columns_ref, grad_ref, *outs):
    step = pl.program_id(0)
    block = outs[0].shape[1]
    result = (
        dot(columns_ref[0], grad_ref[0])
        + dot(columns_ref[0], grad_ref[1])
        + dot(columns_ref[1], grad_ref[0])
    )
    for pair in range(len(outs) // 2):
        @pl.when(step == pair)
        def _():
            outs[2 * pair][...] = result[:, :block]
            outs[2 * pair + 1][...] = result[:, block:]


def table_grads(columns, grad, block, first, count):
    _, features, edges = columns.shape
    return kernel_call(
        table_grad_kernel, [shape((features, block))] * count,
        6 * features * count * block * edges, 4 * edges * (features + count * block),
        grid=(count // 2,),
        in_specs=[
            held((2, features, edges)),
            pl.BlockSpec((2, edges, 2 * block), lambda i: (0, 0, first // 2 + i)),
        ],
        out_specs=[held((features, block))] * count,
    )(columns, grad)


def relation_grad_kernel(
    steps, me_ref, table_ref, grad_ref, heads_ref, rels_ref, edge_rel_ref, source_ref, *refs
):
    outs, lines, total = refs[:-2], refs[-2], refs[-1]
    groups = len(outs) // 2
    half, width = outs[0].shape
    step = pl.program_id(0)
    features, chunk = heads_ref.shape
    tile = total.shape[2]

    @pl.when(step < steps)
    def _():
        hi, lo = table_ref[:features], table_ref[features:2 * features]
        query_grad = dot_nt(hi, grad_ref[0]) + dot_nt(hi, grad_ref[1]) + dot_nt(lo, grad_ref[0])
        source_ref[0], source_ref[1] = split2(conj_product(query_grad, rels_ref[...]))
        lines[step] = jnp.concatenate(split2(conj_product(query_grad, heads_ref[...])), axis=1)

    @pl.when(step >= steps)
    def _():
        part = None
        for i in range(steps):
            slots = edge_rel_ref[i * chunk:(i + 1) * chunk, :] - (step - steps) * tile
            hot = columns_hot(slots, tile)
            term = dot(lines[i, :, :chunk], hot) + dot(lines[i, :, chunk:], hot)
            part = term if part is None else part + term
        total[step - steps] = part

    @pl.when(step == pl.num_programs(0) - 1)
    def _():
        group, core = me_ref[0], me_ref[1]
        for j in range(groups):
            for at in range(0, width, LANES):
                start = (group ^ j) * width + at
                rows = total.at[start // tile, :, pl.ds(pl.multiple_of(start % tile, LANES), LANES)]
                outs[j][:, at:at + LANES] = rows[pl.ds(pl.multiple_of(core * half, 8), half), :]
                outs[groups + j][:, at:at + LANES] = rows[
                    pl.ds(pl.multiple_of((1 - core) * half, 8), half), :
                ]


def relation_grads(me, table, grad, heads, rels, edge_relation, groups, width):
    features, edges = heads.shape
    table_rows = table.shape[1]
    chunk = CHUNK
    steps = edges // chunk
    tile = math.gcd(groups * width, WIDE)
    tiles = groups * width // tile

    def now(i):
        return jnp.minimum(i, steps - 1)

    return kernel_call(
        functools.partial(relation_grad_kernel, steps),
        [shape((2, features, edges), BF16)] + [shape((features // 2, width))] * (2 * groups),
        10 * features * table_rows * edges, 30 * features * edges,
        grid=(steps + tiles,),
        in_specs=[
            SMEM,
            held((3 * features, table_rows)),
            pl.BlockSpec((2, chunk, table_rows), lambda i: (0, now(i), 0)),
            pl.BlockSpec((features, chunk), lambda i: (0, now(i))),
            pl.BlockSpec((features, chunk), lambda i: (0, now(i))),
            held((edges, 1)),
        ],
        out_specs=[pl.BlockSpec((2, features, chunk), lambda i: (0, 0, now(i)))]
        + [held((features // 2, width))] * (2 * groups),
        scratch_shapes=[
            pltpu.VMEM((steps, features, 2 * chunk), BF16),
            pltpu.VMEM((tiles, features, tile), F32),
        ],
    )(me, table, grad, heads, rels, edge_relation)


def source_grad_kernel(first, rows_ref, edge_source_ref, *outs):
    step = pl.program_id(0)
    block = outs[0].shape[1]
    hot = columns_hot(edge_source_ref[...] - (first * block + step * 2 * block), 2 * block)
    result = dot(rows_ref[0], hot) + dot(rows_ref[1], hot)
    for pair in range(len(outs) // 2):
        @pl.when(step == pair)
        def _():
            outs[2 * pair][...] = result[:, :block]
            outs[2 * pair + 1][...] = result[:, block:]


def source_grads(rows, edge_source, block, first, count):
    _, features, edges = rows.shape
    return kernel_call(
        functools.partial(source_grad_kernel, first), [shape((features, block))] * count,
        4 * features * count * block * edges, 4 * features * (edges + count * block),
        grid=(count // 2,),
        in_specs=[held((2, features, edges)), held((edges, 1))],
        out_specs=[held((features, block))] * count,
    )(rows, edge_source)


def put_back(blocks, hot_ref):
    hi, lo = split2(jnp.concatenate([ref[...] for ref in blocks], axis=1))
    return dot(hi, hot_ref[...]) + dot(lo, hot_ref[...])


def target_home_kernel(hot_ref, *refs):
    refs[-1][...] = put_back(refs[:-1], hot_ref)


def target_home(hots, blocks):
    features = blocks[0].shape[0]
    rows = hots.shape[1]
    return kernel_call(
        target_home_kernel, shape((features, rows)),
        4 * features * rows * hots.shape[0], 8 * features * hots.shape[0],
        in_specs=[VMEM] * (1 + len(blocks)), out_specs=VMEM,
    )(hots, *blocks)


def adagrad(params, state, gradient):
    new_state = state + jnp.mean(gradient * gradient, axis=0, keepdims=True)
    return params - gradient * (learn_rate / jnp.sqrt(new_state))


def entity_kernel(other_ref, entity_ref, state_ref, hot_ref, *refs):
    gradient = other_ref[...] + put_back(refs[:-1], hot_ref)
    refs[-1][...] = adagrad(entity_ref[...], state_ref[...], gradient)


def entity_update(hots, blocks, other, entity, state):
    features, rows = entity.shape
    return kernel_call(
        entity_kernel, shape((features, rows)),
        4 * features * rows * hots.shape[0], 8 * features * hots.shape[0],
        in_specs=[VMEM] * (4 + len(blocks)), out_specs=VMEM,
    )(other, entity, state, hots, *blocks)


def cut_kernel(me_ref, *refs):
    chips = me_ref.shape[0]
    terms, outs, whole = refs[:-1 - chips], refs[-1 - chips:-1], refs[-1]
    rows, width = outs[0].shape
    have = terms[0].shape[0]
    total = terms[0][...]
    for term in terms[1:]:
        total = total + term[...]
    whole[:have, :] = total
    if have < chips * rows:
        whole[have:, :] = jnp.zeros((chips * rows - have, width), F32)
    for k, out in enumerate(outs):
        out[...] = whole[pl.ds(pl.multiple_of(me_ref[k] * rows, 8), rows), :]


def cut_pieces(order, terms):
    chips = order.shape[0]
    half, width = terms[0].shape
    rows = pl.cdiv(half, 8 * chips) * 8
    return kernel_call(
        cut_kernel, [shape((rows, width))] * chips,
        len(terms) * half * width, 4 * (len(terms) + 1) * half * width,
        in_specs=[SMEM] + [VMEM] * len(terms), out_specs=[VMEM] * chips,
        scratch_shapes=[pltpu.VMEM((chips * rows, width), F32)],
    )(order, *terms)


def sum_kernel(*refs):
    total = refs[0][...]
    for ref in refs[1:-1]:
        total = total + ref[...]
    refs[-1][...] = total


def sum_pieces(pieces):
    rows, width = pieces[0].shape
    return kernel_call(
        sum_kernel, shape((rows, width)),
        len(pieces) * rows * width, 4 * (len(pieces) + 1) * rows * width,
        in_specs=[VMEM] * len(pieces), out_specs=VMEM,
    )(*pieces)


def join_kernel(me_ref, *refs):
    pieces, out_ref, whole = refs[:-2], refs[-2], refs[-1]
    rows = pieces[0].shape[0]
    for k, piece in enumerate(pieces):
        whole[pl.ds(pl.multiple_of(me_ref[k] * rows, 8), rows), :] = piece[...]
    out_ref[...] = whole[:out_ref.shape[0], :]


def join_pieces(order, pieces, half):
    rows, width = pieces[0].shape
    return kernel_call(
        join_kernel, shape((half, width)),
        half * width, 8 * half * width,
        in_specs=[SMEM] + [VMEM] * len(pieces), out_specs=VMEM,
        scratch_shapes=[pltpu.VMEM((len(pieces) * rows, width), F32)],
    )(order, *pieces)


def relation_update_kernel(me_ref, relation_ref, state_ref, *refs):
    parts, out_ref, total = refs[:-2], refs[-2], refs[-1]
    groups = len(parts) // 2
    half, width = parts[0].shape
    group, core = me_ref[0], me_ref[1]
    for j in range(groups):
        at = pl.ds(pl.multiple_of((group ^ j) * width, LANES), width)
        total[pl.ds(pl.multiple_of(core * half, 8), half), at] = parts[j][...]
        total[pl.ds(pl.multiple_of((1 - core) * half, 8), half), at] = parts[groups + j][...]
    gradient = total[:, :out_ref.shape[1]]
    out_ref[...] = adagrad(relation_ref[...], state_ref[...], gradient)


def relation_update(me, relation, state, parts):
    features, count = relation.shape
    _, width = parts[0].shape
    groups = len(parts) // 2
    return kernel_call(
        relation_update_kernel, shape((features, count)),
        8 * features * count, 12 * features * count,
        in_specs=[SMEM] + [VMEM] * (2 + len(parts)), out_specs=VMEM,
        scratch_shapes=[pltpu.VMEM((features, groups * width), F32)],
    )(me, relation, state, *parts)


def sent_on(value, hop, peers):
    return lax.ppermute(value, "shard", [(i, partner(i, hop, peers, 1)) for i in range(peers)])


def sent_across(value, hop, peers, groups, by):
    pairs = [
        (g * peers + i, (g + by) % groups * peers + partner(i, hop, peers, 1))
        for g in range(groups)
        for i in range(peers)
    ]
    return lax.ppermute(value, ("group", "shard"), pairs)


def sent_group(value, bit, groups):
    return lax.ppermute(value, "group", [(g, g ^ bit) for g in range(groups)])


def relation_sum(kept, sent, peers, groups, chip):
    chips = peers // 2
    half = kept[0].shape[0]
    other_core = (0, 1)
    sent = [sent_on(b, other_core, peers) for b in sent]
    mine = [a + b for a, b in zip(kept, sent)]
    terms = [mine[0]] + [sent_group(mine[j], j, groups) for j in range(1, groups)]
    ahead = (chip + jnp.arange(chips, dtype=I32)) % chips
    behind = (chip - jnp.arange(chips, dtype=I32)) % chips
    pieces = cut_pieces(ahead, terms)
    pieces = [pieces[0]] + [sent_on(pieces[k], (k, 0), peers) for k in range(1, chips)]
    piece = sum_pieces(pieces)
    pieces = [piece] + [sent_on(piece, (k, 0), peers) for k in range(1, chips)]
    block = join_pieces(behind, pieces, half)
    blocks = [block] + [sent_group(block, j, groups) for j in range(1, groups)]
    return blocks + [sent_on(b, other_core, peers) for b in blocks]


def on_device(
    entity, entity_state, relation, relation_state, src_send, dst_send,
    edge_source, edge_relation, edge_target, neg_slots, edge_count,
):
    rows, _ = entity.shape
    relations = relation.shape[0]
    peers, block = src_send.shape[1:]
    groups = lax.axis_size("group")
    group = lax.axis_index("group").astype(I32)
    me = lax.axis_index("shard").astype(I32)
    width = pl.cdiv(relations, groups * LANES) * LANES
    entity_t, relation_t = entity.T, relation.T
    ways = hops(peers)
    order = jnp.stack([partner(me, hop, peers, 1) for hop in ways])
    here = jnp.stack([group, me % 2])

    def placed(slots):
        return places_of(me, slots // block, peers) * block + slots % block

    edge_source, edge_target = placed(edge_source), placed(edge_target)
    sources = pick_blocks(order[:2], entity_t, src_send[0])
    sources += pick_blocks(order[2:], entity_t, src_send[0])
    sources = [
        sent_on(value, hop, peers) if hop != (0, 0) else value
        for value, hop in zip(sources, ways)
    ]
    targets = pick_blocks(order, entity_t, dst_send[0])
    targets = [sent_across(value, hop, peers, groups, -1) for value, hop in zip(targets, ways)]
    rels = relation_rows(relation_t, edge_relation.reshape(1, -1))
    counts = slot_counts(placed(neg_slots), peers * block)
    source_hots = home_hots(order, src_send[0], rows)
    target_hots = home_hots(order, dst_send[0], rows)
    heads, query_columns, query_lines = query_rows(sources, edge_source.reshape(1, -1), rels)
    loss, grad, table = score_spans(
        edge_count, targets, query_lines, counts, edge_target.reshape(-1, 1)
    )
    table_parts = table_grads(query_columns, grad, block, 0, 2)
    table_parts += table_grads(query_columns, grad, block, 2, peers - 2)
    back = [(-hop[0], hop[1]) for hop in ways]
    home = [
        sent_across(value, hop, peers, groups, 1)
        for value, hop in zip(table_parts[:2], back[:2])
    ]
    home += [
        sent_across(value, hop, peers, groups, 1)
        for value, hop in zip(table_parts[2:], back[2:])
    ]
    source_lines, *halves = relation_grads(
        here, table, grad, heads, rels, edge_relation.reshape(-1, 1), groups, width
    )
    edge_source = edge_source.reshape(-1, 1)
    source_parts = source_grads(source_lines, edge_source, block, 0, 2)
    source_parts += source_grads(source_lines, edge_source, block, 2, peers - 2)
    returned = []
    for value, hop, way in zip(source_parts, back, ways):
        returned.append(sent_on(value, hop, peers) if way != (0, 0) else value)
    parts = relation_sum(halves[:groups], halves[groups:], peers, groups, me // 2)
    relation_new = relation_update(here, relation_t, relation_state.reshape(1, -1), parts)
    target_part = target_home(target_hots, home)
    entity_new = entity_update(
        source_hots, returned, target_part, entity_t, entity_state.reshape(1, -1)
    )
    return entity_new.T, relation_new.T, loss.reshape(-1)


def solution(mesh):
    both = ("group", "shard")
    return jax.shard_map(
        on_device,
        mesh=mesh,
        in_specs=(
            P(both, None), P(both), P(), P(), P(both, None, None), P(both, None, None),
            P(both), P(both), P(both), P(both, None), P(both),
        ),
        out_specs=(P(both, None), P(), P(both)),
        check_vma=False,
    )
```

```python
import functools
import math

import jax
import jax.numpy as jnp
from jax import lax
from jax.experimental import pallas as pl
from jax.experimental.pallas import tpu as pltpu
from jax.sharding import PartitionSpec as P


SPAN = 512
LANES = 128
CHUNK = 256
WIDE = 512


learn_rate = 0.5

F32, BF16, I32 = jnp.float32, jnp.bfloat16, jnp.int32
VMEM = pl.BlockSpec(memory_space=pltpu.VMEM)
SMEM = pl.BlockSpec(memory_space=pltpu.SMEM)
VMEM_LIMIT = 24 << 20


def kernel_call(kernel, outs, flops, moved, **kw):
    semantics = ("arbitrary",) if "grid" in kw else None
    return pl.pallas_call(
        kernel,
        out_shape=outs,
        compiler_params=pltpu.CompilerParams(
            vmem_limit_bytes=VMEM_LIMIT, dimension_semantics=semantics
        ),
        cost_estimate=pl.CostEstimate(flops=flops, bytes_accessed=moved, transcendentals=0),
        **kw,
    )


def shape(dims, dtype=F32):
    return jax.ShapeDtypeStruct(dims, dtype)


def held(dims):
    return pl.BlockSpec(dims, lambda i: (0,) * len(dims))


def split2(x):
    hi = x.astype(BF16)
    return hi, (x - hi.astype(F32)).astype(BF16)


def split3(x):
    hi = x.astype(BF16)
    rest = x - hi.astype(F32)
    mid = rest.astype(BF16)
    return hi, mid, (rest - mid.astype(F32)).astype(BF16)


def dot(a, b):
    return jnp.dot(a, b, preferred_element_type=F32)


def dot_nt(a, b):
    return lax.dot_general(a, b, (((1,), (1,)), ((), ())), preferred_element_type=F32)


def one_hot(mask):
    return jnp.where(mask, 1.0, 0.0).astype(BF16)


def rows_hot(length, slots):
    return one_hot(lax.broadcasted_iota(I32, (length, slots.shape[1]), 0) == slots)


def columns_hot(slots, length):
    return one_hot(lax.broadcasted_iota(I32, (slots.shape[0], length), 1) == slots)


def complex_product(a, b):
    half = a.shape[0] // 2
    ar, ai, br, bi = a[:half], a[half:], b[:half], b[half:]
    return jnp.concatenate([ar * br - ai * bi, ar * bi + ai * br], axis=0)


def conj_product(a, b):
    half = a.shape[0] // 2
    ar, ai, br, bi = a[:half], a[half:], b[:half], b[half:]
    return jnp.concatenate([ar * br + ai * bi, ai * br - ar * bi], axis=0)


def hops(peers):
    chips = peers // 2
    ahead = [(k, b) for k in range(1, chips) for b in (0, 1)]
    return ahead + [(0, 1), (0, 0)]


def partner(me, hop, peers, sign):
    chips = peers // 2
    return (me // 2 + sign * hop[0]) % chips * 2 + (me % 2 + hop[1]) % 2


def places_of(me, owner, peers):
    chips = peers // 2
    k = (me // 2 - owner // 2) % chips
    b = (me + owner) % 2
    return (k - 1) % chips * 2 + jnp.where(k == 0, 1 - b, b)


def pick_kernel(order_ref, rows_ref, slots_ref, *outs):
    hi, mid, lo = split3(rows_ref[...])
    block = slots_ref.shape[1]
    together = max(1, CHUNK // block)
    for first in range(0, len(outs), together):
        group = outs[first:first + together]
        slots = [slots_ref[pl.ds(order_ref[first + i], 1), :] for i in range(len(group))]
        hot = rows_hot(rows_ref.shape[1], jnp.concatenate(slots, axis=1))
        picked = dot(hi, hot) + dot(mid, hot) + dot(lo, hot)
        for i, out in enumerate(group):
            out[...] = picked[:, i * block:(i + 1) * block]


def pick_blocks(order, rows, slots):
    features, length = rows.shape
    block = slots.shape[1]
    count = order.shape[0]
    return kernel_call(
        pick_kernel, [shape((features, block))] * count,
        6 * features * length * count * block, 8 * features * count * block,
        in_specs=[SMEM, VMEM, VMEM], out_specs=[VMEM] * count,
    )(order, rows, slots)


def relation_kernel(rel_ref, edge_rel_ref, out_ref, pieces):
    count = rel_ref.shape[1]
    padded = pieces.shape[2]

    @pl.when(pl.program_id(0) == 0)
    def _():
        features = rel_ref.shape[0]
        tail = padded - count // LANES * LANES
        for piece, value in enumerate(split3(rel_ref[...])):
            pieces[piece, :, padded - tail:] = jnp.zeros((features, tail), BF16)
            pieces[piece, :, :count] = value

    hot = rows_hot(padded, edge_rel_ref[...])
    out_ref[...] = dot(pieces[0], hot) + dot(pieces[1], hot) + dot(pieces[2], hot)


def relation_rows(relation, edge_relation):
    features, count = relation.shape
    edges = edge_relation.shape[1]
    padded = pl.cdiv(count, LANES) * LANES
    return kernel_call(
        relation_kernel, shape((features, edges)),
        6 * features * padded * edges, 8 * features * edges,
        grid=(edges // CHUNK,),
        in_specs=[held((features, count)), pl.BlockSpec((1, CHUNK), lambda i: (0, i))],
        out_specs=pl.BlockSpec((features, CHUNK), lambda i: (0, i)),
        scratch_shapes=[pltpu.VMEM((3, features, padded), BF16)],
    )(relation, edge_relation)


def count_kernel(slots_ref, out_ref):
    table_rows = out_ref.shape[2]
    hits = lax.broadcasted_iota(I32, (slots_ref.shape[1], table_rows), 1) == slots_ref[0]
    counts = jnp.sum(jnp.where(hits, 1.0, 0.0), axis=0, keepdims=True)
    out_ref[0] = jnp.where(counts > 0.0, jnp.log(jnp.maximum(counts, 1.0)), -jnp.inf)


def slot_counts(neg_slots, table_rows):
    spans, negatives = neg_slots.shape
    return kernel_call(
        count_kernel, shape((spans, 1, table_rows)),
        2 * spans * negatives * table_rows, 512 * spans * negatives,
        grid=(spans,),
        in_specs=[pl.BlockSpec((1, negatives, 1), lambda i: (i, 0, 0))],
        out_specs=pl.BlockSpec((1, 1, table_rows), lambda i: (i, 0, 0)),
    )(neg_slots[:, :, None])


def hot_kernel(order_ref, slots_ref, out_ref):
    peers, block, _ = slots_ref.shape
    for j in range(peers):
        out_ref[j * block:(j + 1) * block, :] = columns_hot(slots_ref[order_ref[j]], out_ref.shape[1])


def home_hots(order, slots, rows):
    peers, block = slots.shape
    return kernel_call(
        hot_kernel, shape((peers * block, rows), BF16),
        2 * peers * block * rows, 2 * peers * block * rows,
        in_specs=[SMEM, VMEM], out_specs=VMEM,
    )(order, slots[:, :, None])


def query_kernel(*refs):
    edge_source_ref, rels_ref, *blocks = refs[:-4]
    heads_ref, columns_ref, rows_ref, pieces = refs[-4:]
    block = blocks[0].shape[1]

    @pl.when(pl.program_id(0) == 0)
    def _():
        for p, ref in enumerate(blocks):
            for piece, value in enumerate(split3(ref[...])):
                pieces[piece, :, p * block:(p + 1) * block] = value

    hot = rows_hot(pieces.shape[2], edge_source_ref[...])
    heads = dot(pieces[0], hot) + dot(pieces[1], hot) + dot(pieces[2], hot)
    heads_ref[...] = heads
    queries = complex_product(heads, rels_ref[...])
    hi, lo = split2(queries)
    columns_ref[0], columns_ref[1] = hi, lo
    hi, lo = split2(queries.T)
    rows_ref[...] = jnp.concatenate([hi, hi, lo], axis=1)


def query_rows(blocks, edge_source, rels):
    peers = len(blocks)
    features, block = blocks[0].shape
    edges = edge_source.shape[1]
    return kernel_call(
        query_kernel,
        [shape((features, edges)), shape((2, features, edges), BF16), shape((edges, 3 * features), BF16)],
        6 * features * peers * block * edges, 20 * features * edges,
        grid=(edges // CHUNK,),
        in_specs=[
            pl.BlockSpec((1, CHUNK), lambda i: (0, i)),
            pl.BlockSpec((features, CHUNK), lambda i: (0, i)),
        ] + [held((features, block))] * peers,
        out_specs=[
            pl.BlockSpec((features, CHUNK), lambda i: (0, i)),
            pl.BlockSpec((2, features, CHUNK), lambda i: (0, 0, i)),
            pl.BlockSpec((CHUNK, 3 * features), lambda i: (i, 0)),
        ],
        scratch_shapes=[pltpu.VMEM((3, features, peers * block), BF16)],
    )(edge_source, rels, *blocks)


def softmax_step(step, live, score, log_counts, edge_target, loss_ref, grad_ref):
    own = lax.broadcasted_iota(I32, score.shape, 1) == edge_target
    pos = jnp.sum(jnp.where(own, score, 0.0), axis=1, keepdims=True)
    score = score + log_counts
    peak = jnp.maximum(pos, jnp.max(score, axis=1, keepdims=True))
    weight = jnp.exp(score - peak)
    pos_weight = jnp.exp(pos - peak)
    sum_all = pos_weight + jnp.sum(weight, axis=1, keepdims=True)
    edge = step * score.shape[0] + lax.broadcasted_iota(I32, pos.shape, 0)
    is_live = jnp.where(edge < live, 1.0, 0.0)
    loss_ref[...] = (peak - pos + jnp.log(sum_all)) * is_live
    scale = is_live / sum_all
    pos_grad = pos_weight * scale - is_live
    grad = weight * scale + jnp.where(own, pos_grad, 0.0)
    grad_ref[0], grad_ref[1] = split2(grad)


def score_kernel(peers, *refs):
    live_ref, rows_ref, counts_ref, edge_target_ref = refs[:4]
    blocks = refs[4:4 + peers]
    loss_ref, grad_ref, table_ref, scores = refs[4 + peers:]
    features, block = blocks[0].shape
    step = pl.program_id(0)
    last = pl.num_programs(0) - 1

    @pl.when(step == 0)
    def _():
        for p, ref in enumerate(blocks):
            hi, lo = split2(ref[...])
            at = pl.ds(p * block, block)
            table_ref[:features, at] = hi
            table_ref[features:2 * features, at] = lo
            table_ref[2 * features:, at] = hi

    def multiply():
        scores[step % 2] = dot(rows_ref[...], table_ref[...])

    def finish():
        softmax_step(
            step - 1, live_ref[0], scores[(step + 1) % 2], counts_ref[0], edge_target_ref[...],
            loss_ref, grad_ref,
        )

    @pl.when(step == 0)
    def _():
        multiply()

    @pl.when((step > 0) & (step < last))
    def _():
        multiply()
        finish()

    @pl.when(step == last)
    def _():
        finish()


def score_spans(live, blocks, rows, counts, edge_target):
    peers = len(blocks)
    features, block = blocks[0].shape
    edges = edge_target.shape[0]
    table_rows = peers * block
    chunk = CHUNK
    per_span = SPAN // chunk
    steps = edges // chunk

    def now(i):
        return jnp.minimum(i, steps - 1)

    def before(i):
        return jnp.maximum(i - 1, 0)

    return kernel_call(
        functools.partial(score_kernel, peers),
        [
            shape((edges, 1)),
            shape((2, edges, table_rows), BF16),
            shape((3 * features, table_rows), BF16),
        ],
        6 * features * table_rows * edges, 30 * features * edges,
        grid=(steps + 1,),
        in_specs=[
            SMEM,
            pl.BlockSpec((chunk, 3 * features), lambda i: (now(i), 0)),
            pl.BlockSpec((1, 1, table_rows), lambda i: (before(i) // per_span, 0, 0)),
            pl.BlockSpec((chunk, 1), lambda i: (before(i), 0)),
        ] + [held((features, block))] * peers,
        out_specs=[
            pl.BlockSpec((chunk, 1), lambda i: (before(i), 0)),
            pl.BlockSpec((2, chunk, table_rows), lambda i: (0, before(i), 0)),
            held((3 * features, table_rows)),
        ],
        scratch_shapes=[pltpu.VMEM((2, chunk, table_rows), F32)],
    )(live, rows, counts, edge_target, *blocks)


def table_grad_kernel(columns_ref, grad_ref, *outs):
    step = pl.program_id(0)
    block = outs[0].shape[1]
    result = (
        dot(columns_ref[0], grad_ref[0])
        + dot(columns_ref[0], grad_ref[1])
        + dot(columns_ref[1], grad_ref[0])
    )
    for pair in range(len(outs) // 2):
        @pl.when(step == pair)
        def _():
            outs[2 * pair][...] = result[:, :block]
            outs[2 * pair + 1][...] = result[:, block:]


def table_grads(columns, grad, block, first, count):
    _, features, edges = columns.shape
    return kernel_call(
        table_grad_kernel, [shape((features, block))] * count,
        6 * features * count * block * edges, 4 * edges * (features + count * block),
        grid=(count // 2,),
        in_specs=[
            held((2, features, edges)),
            pl.BlockSpec((2, edges, 2 * block), lambda i: (0, 0, first // 2 + i)),
        ],
        out_specs=[held((features, block))] * count,
    )(columns, grad)


def relation_grad_kernel(
    steps, me_ref, table_ref, grad_ref, heads_ref, rels_ref, edge_rel_ref, source_ref, *refs
):
    outs, lines, total = refs[:-2], refs[-2], refs[-1]
    groups = len(outs) // 2
    half, width = outs[0].shape
    step = pl.program_id(0)
    features, chunk = heads_ref.shape
    tile = total.shape[2]

    @pl.when(step < steps)
    def _():
        hi, lo = table_ref[:features], table_ref[features:2 * features]
        query_grad = dot_nt(hi, grad_ref[0]) + dot_nt(hi, grad_ref[1]) + dot_nt(lo, grad_ref[0])
        source_ref[0], source_ref[1] = split2(conj_product(query_grad, rels_ref[...]))
        lines[step] = jnp.concatenate(split2(conj_product(query_grad, heads_ref[...])), axis=1)

    @pl.when(step >= steps)
    def _():
        part = None
        for i in range(steps):
            slots = edge_rel_ref[i * chunk:(i + 1) * chunk, :] - (step - steps) * tile
            hot = columns_hot(slots, tile)
            term = dot(lines[i, :, :chunk], hot) + dot(lines[i, :, chunk:], hot)
            part = term if part is None else part + term
        total[step - steps] = part

    @pl.when(step == pl.num_programs(0) - 1)
    def _():
        group, core = me_ref[0], me_ref[1]
        for j in range(groups):
            for at in range(0, width, LANES):
                start = (group ^ j) * width + at
                rows = total.at[start // tile, :, pl.ds(pl.multiple_of(start % tile, LANES), LANES)]
                outs[j][:, at:at + LANES] = rows[pl.ds(pl.multiple_of(core * half, 8), half), :]
                outs[groups + j][:, at:at + LANES] = rows[
                    pl.ds(pl.multiple_of((1 - core) * half, 8), half), :
                ]


def relation_grads(me, table, grad, heads, rels, edge_relation, groups, width):
    features, edges = heads.shape
    table_rows = table.shape[1]
    chunk = CHUNK
    steps = edges // chunk
    tile = math.gcd(groups * width, WIDE)
    tiles = groups * width // tile

    def now(i):
        return jnp.minimum(i, steps - 1)

    return kernel_call(
        functools.partial(relation_grad_kernel, steps),
        [shape((2, features, edges), BF16)] + [shape((features // 2, width))] * (2 * groups),
        10 * features * table_rows * edges, 30 * features * edges,
        grid=(steps + tiles,),
        in_specs=[
            SMEM,
            held((3 * features, table_rows)),
            pl.BlockSpec((2, chunk, table_rows), lambda i: (0, now(i), 0)),
            pl.BlockSpec((features, chunk), lambda i: (0, now(i))),
            pl.BlockSpec((features, chunk), lambda i: (0, now(i))),
            held((edges, 1)),
        ],
        out_specs=[pl.BlockSpec((2, features, chunk), lambda i: (0, 0, now(i)))]
        + [held((features // 2, width))] * (2 * groups),
        scratch_shapes=[
            pltpu.VMEM((steps, features, 2 * chunk), BF16),
            pltpu.VMEM((tiles, features, tile), F32),
        ],
    )(me, table, grad, heads, rels, edge_relation)


def source_grad_kernel(first, rows_ref, edge_source_ref, *outs):
    step = pl.program_id(0)
    block = outs[0].shape[1]
    hot = columns_hot(edge_source_ref[...] - (first * block + step * 2 * block), 2 * block)
    result = dot(rows_ref[0], hot) + dot(rows_ref[1], hot)
    for pair in range(len(outs) // 2):
        @pl.when(step == pair)
        def _():
            outs[2 * pair][...] = result[:, :block]
            outs[2 * pair + 1][...] = result[:, block:]


def source_grads(rows, edge_source, block, first, count):
    _, features, edges = rows.shape
    return kernel_call(
        functools.partial(source_grad_kernel, first), [shape((features, block))] * count,
        4 * features * count * block * edges, 4 * features * (edges + count * block),
        grid=(count // 2,),
        in_specs=[held((2, features, edges)), held((edges, 1))],
        out_specs=[held((features, block))] * count,
    )(rows, edge_source)


def put_back(blocks, hot_ref):
    hi, lo = split2(jnp.concatenate([ref[...] for ref in blocks], axis=1))
    return dot(hi, hot_ref[...]) + dot(lo, hot_ref[...])


def target_home_kernel(hot_ref, *refs):
    refs[-1][...] = put_back(refs[:-1], hot_ref)


def target_home(hots, blocks):
    features = blocks[0].shape[0]
    rows = hots.shape[1]
    return kernel_call(
        target_home_kernel, shape((features, rows)),
        4 * features * rows * hots.shape[0], 8 * features * hots.shape[0],
        in_specs=[VMEM] * (1 + len(blocks)), out_specs=VMEM,
    )(hots, *blocks)


def adagrad(params, state, gradient):
    new_state = state + jnp.mean(gradient * gradient, axis=0, keepdims=True)
    return params - gradient * (learn_rate / jnp.sqrt(new_state))


def entity_kernel(other_ref, entity_ref, state_ref, hot_ref, *refs):
    gradient = other_ref[...] + put_back(refs[:-1], hot_ref)
    refs[-1][...] = adagrad(entity_ref[...], state_ref[...], gradient)


def entity_update(hots, blocks, other, entity, state):
    features, rows = entity.shape
    return kernel_call(
        entity_kernel, shape((features, rows)),
        4 * features * rows * hots.shape[0], 8 * features * hots.shape[0],
        in_specs=[VMEM] * (4 + len(blocks)), out_specs=VMEM,
    )(other, entity, state, hots, *blocks)


def cut_kernel(me_ref, *refs):
    chips = me_ref.shape[0]
    terms, outs, whole = refs[:-1 - chips], refs[-1 - chips:-1], refs[-1]
    rows, width = outs[0].shape
    have = terms[0].shape[0]
    total = terms[0][...]
    for term in terms[1:]:
        total = total + term[...]
    whole[:have, :] = total
    if have < chips * rows:
        whole[have:, :] = jnp.zeros((chips * rows - have, width), F32)
    for k, out in enumerate(outs):
        out[...] = whole[pl.ds(pl.multiple_of(me_ref[k] * rows, 8), rows), :]


def cut_pieces(order, terms):
    chips = order.shape[0]
    half, width = terms[0].shape
    rows = pl.cdiv(half, 8 * chips) * 8
    return kernel_call(
        cut_kernel, [shape((rows, width))] * chips,
        len(terms) * half * width, 4 * (len(terms) + 1) * half * width,
        in_specs=[SMEM] + [VMEM] * len(terms), out_specs=[VMEM] * chips,
        scratch_shapes=[pltpu.VMEM((chips * rows, width), F32)],
    )(order, *terms)


def sum_kernel(*refs):
    total = refs[0][...]
    for ref in refs[1:-1]:
        total = total + ref[...]
    refs[-1][...] = total


def sum_pieces(pieces):
    rows, width = pieces[0].shape
    return kernel_call(
        sum_kernel, shape((rows, width)),
        len(pieces) * rows * width, 4 * (len(pieces) + 1) * rows * width,
        in_specs=[VMEM] * len(pieces), out_specs=VMEM,
    )(*pieces)


def join_kernel(me_ref, *refs):
    pieces, out_ref, whole = refs[:-2], refs[-2], refs[-1]
    rows = pieces[0].shape[0]
    for k, piece in enumerate(pieces):
        whole[pl.ds(pl.multiple_of(me_ref[k] * rows, 8), rows), :] = piece[...]
    out_ref[...] = whole[:out_ref.shape[0], :]


def join_pieces(order, pieces, half):
    rows, width = pieces[0].shape
    return kernel_call(
        join_kernel, shape((half, width)),
        half * width, 8 * half * width,
        in_specs=[SMEM] + [VMEM] * len(pieces), out_specs=VMEM,
        scratch_shapes=[pltpu.VMEM((len(pieces) * rows, width), F32)],
    )(order, *pieces)


def relation_update_kernel(me_ref, relation_ref, state_ref, *refs):
    parts, out_ref, total = refs[:-2], refs[-2], refs[-1]
    groups = len(parts) // 2
    half, width = parts[0].shape
    group, core = me_ref[0], me_ref[1]
    for j in range(groups):
        at = pl.ds(pl.multiple_of((group ^ j) * width, LANES), width)
        total[pl.ds(pl.multiple_of(core * half, 8), half), at] = parts[j][...]
        total[pl.ds(pl.multiple_of((1 - core) * half, 8), half), at] = parts[groups + j][...]
    gradient = total[:, :out_ref.shape[1]]
    out_ref[...] = adagrad(relation_ref[...], state_ref[...], gradient)


def relation_update(me, relation, state, parts):
    features, count = relation.shape
    _, width = parts[0].shape
    groups = len(parts) // 2
    return kernel_call(
        relation_update_kernel, shape((features, count)),
        8 * features * count, 12 * features * count,
        in_specs=[SMEM] + [VMEM] * (2 + len(parts)), out_specs=VMEM,
        scratch_shapes=[pltpu.VMEM((features, groups * width), F32)],
    )(me, relation, state, *parts)


def sent_on(value, hop, peers):
    return lax.ppermute(value, "shard", [(i, partner(i, hop, peers, 1)) for i in range(peers)])


def sent_across(value, hop, peers, groups, by):
    pairs = [
        (g * peers + i, (g + by) % groups * peers + partner(i, hop, peers, 1))
        for g in range(groups)
        for i in range(peers)
    ]
    return lax.ppermute(value, ("group", "shard"), pairs)


def sent_group(value, bit, groups):
    return lax.ppermute(value, "group", [(g, g ^ bit) for g in range(groups)])


def relation_sum(kept, sent, peers, groups, chip):
    chips = peers // 2
    half = kept[0].shape[0]
    other_core = (0, 1)
    sent = [sent_on(b, other_core, peers) for b in sent]
    mine = [a + b for a, b in zip(kept, sent)]
    terms = [mine[0]] + [sent_group(mine[j], j, groups) for j in range(1, groups)]
    ahead = (chip + jnp.arange(chips, dtype=I32)) % chips
    behind = (chip - jnp.arange(chips, dtype=I32)) % chips
    pieces = cut_pieces(ahead, terms)
    pieces = [pieces[0]] + [sent_on(pieces[k], (k, 0), peers) for k in range(1, chips)]
    piece = sum_pieces(pieces)
    pieces = [piece] + [sent_on(piece, (k, 0), peers) for k in range(1, chips)]
    block = join_pieces(behind, pieces, half)
    blocks = [block] + [sent_group(block, j, groups) for j in range(1, groups)]
    return blocks + [sent_on(b, other_core, peers) for b in blocks]


def on_device(
    entity, entity_state, relation, relation_state, src_send, dst_send,
    edge_source, edge_relation, edge_target, neg_slots, edge_count,
):
    rows, _ = entity.shape
    relations = relation.shape[0]
    peers, block = src_send.shape[1:]
    groups = lax.axis_size("group")
    group = lax.axis_index("group").astype(I32)
    me = lax.axis_index("shard").astype(I32)
    width = pl.cdiv(relations, groups * LANES) * LANES
    entity_t, relation_t = entity.T, relation.T
    ways = hops(peers)
    order = jnp.stack([partner(me, hop, peers, 1) for hop in ways])
    here = jnp.stack([group, me % 2])

    def placed(slots):
        return places_of(me, slots // block, peers) * block + slots % block

    edge_source, edge_target = placed(edge_source), placed(edge_target)
    early = peers // 2
    sources = pick_blocks(order[:2], entity_t, src_send[0])
    sources += pick_blocks(order[2:], entity_t, src_send[0])
    sources = [
        sent_on(value, hop, peers) if hop != (0, 0) else value
        for value, hop in zip(sources, ways)
    ]
    targets = pick_blocks(order, entity_t, dst_send[0])
    targets = [sent_across(value, hop, peers, groups, -1) for value, hop in zip(targets, ways)]
    rels = relation_rows(relation_t, edge_relation.reshape(1, -1))
    counts = slot_counts(placed(neg_slots), peers * block)
    source_hots = home_hots(order, src_send[0], rows)
    target_hots = home_hots(order, dst_send[0], rows)
    heads, query_columns, query_lines = query_rows(sources, edge_source.reshape(1, -1), rels)
    loss, grad, table = score_spans(
        edge_count, targets, query_lines, counts, edge_target.reshape(-1, 1)
    )
    table_parts = table_grads(query_columns, grad, block, 0, early)
    table_parts += table_grads(query_columns, grad, block, early, peers - early)
    back = [(-hop[0], hop[1]) for hop in ways]
    home = [
        sent_across(value, hop, peers, groups, 1)
        for value, hop in zip(table_parts[:early], back[:early])
    ]
    home += [
        sent_across(value, hop, peers, groups, 1)
        for value, hop in zip(table_parts[early:], back[early:])
    ]
    source_lines, *halves = relation_grads(
        here, table, grad, heads, rels, edge_relation.reshape(-1, 1), groups, width
    )
    edge_source = edge_source.reshape(-1, 1)
    source_parts = source_grads(source_lines, edge_source, block, 0, 2)
    source_parts += source_grads(source_lines, edge_source, block, 2, peers - 2)
    returned = []
    for value, hop, way in zip(source_parts, back, ways):
        returned.append(sent_on(value, hop, peers) if way != (0, 0) else value)
    parts = relation_sum(halves[:groups], halves[groups:], peers, groups, me // 2)
    relation_new = relation_update(here, relation_t, relation_state.reshape(1, -1), parts)
    target_part = target_home(target_hots, home)
    entity_new = entity_update(
        source_hots, returned, target_part, entity_t, entity_state.reshape(1, -1)
    )
    return entity_new.T, relation_new.T, loss.reshape(-1)


def solution(mesh):
    both = ("group", "shard")
    return jax.shard_map(
        on_device,
        mesh=mesh,
        in_specs=(
            P(both, None), P(both), P(), P(), P(both, None, None), P(both, None, None),
            P(both), P(both), P(both), P(both, None), P(both),
        ),
        out_specs=(P(both, None), P(), P(both)),
        check_vma=False,
    )
```

```python
import functools
import math

import jax
import jax.numpy as jnp
from jax import lax
from jax.experimental import pallas as pl
from jax.experimental.pallas import tpu as pltpu
from jax.sharding import PartitionSpec as P


SPAN = 512
LANES = 128
CHUNK = 256
WIDE = 512


learn_rate = 0.5

F32, BF16, I32 = jnp.float32, jnp.bfloat16, jnp.int32
VMEM = pl.BlockSpec(memory_space=pltpu.VMEM)
SMEM = pl.BlockSpec(memory_space=pltpu.SMEM)
VMEM_LIMIT = 24 << 20


def kernel_call(kernel, outs, flops, moved, **kw):
    semantics = ("arbitrary",) if "grid" in kw else None
    return pl.pallas_call(
        kernel,
        out_shape=outs,
        compiler_params=pltpu.CompilerParams(
            vmem_limit_bytes=VMEM_LIMIT, dimension_semantics=semantics
        ),
        cost_estimate=pl.CostEstimate(flops=flops, bytes_accessed=moved, transcendentals=0),
        **kw,
    )


def shape(dims, dtype=F32):
    return jax.ShapeDtypeStruct(dims, dtype)


def held(dims):
    return pl.BlockSpec(dims, lambda i: (0,) * len(dims))


def split2(x):
    hi = x.astype(BF16)
    return hi, (x - hi.astype(F32)).astype(BF16)


def split3(x):
    hi = x.astype(BF16)
    rest = x - hi.astype(F32)
    mid = rest.astype(BF16)
    return hi, mid, (rest - mid.astype(F32)).astype(BF16)


def dot(a, b):
    return jnp.dot(a, b, preferred_element_type=F32)


def dot_nt(a, b):
    return lax.dot_general(a, b, (((1,), (1,)), ((), ())), preferred_element_type=F32)


def one_hot(mask):
    return jnp.where(mask, 1.0, 0.0).astype(BF16)


def rows_hot(length, slots):
    return one_hot(lax.broadcasted_iota(I32, (length, slots.shape[1]), 0) == slots)


def columns_hot(slots, length):
    return one_hot(lax.broadcasted_iota(I32, (slots.shape[0], length), 1) == slots)


def complex_product(a, b):
    half = a.shape[0] // 2
    ar, ai, br, bi = a[:half], a[half:], b[:half], b[half:]
    return jnp.concatenate([ar * br - ai * bi, ar * bi + ai * br], axis=0)


def conj_product(a, b):
    half = a.shape[0] // 2
    ar, ai, br, bi = a[:half], a[half:], b[:half], b[half:]
    return jnp.concatenate([ar * br + ai * bi, ai * br - ar * bi], axis=0)


def hops(peers):
    chips = peers // 2
    ahead = [(k, b) for k in range(1, chips) for b in (0, 1)]
    return ahead + [(0, 1), (0, 0)]


def partner(me, hop, peers, sign):
    chips = peers // 2
    return (me // 2 + sign * hop[0]) % chips * 2 + (me % 2 + hop[1]) % 2


def places_of(me, owner, peers):
    chips = peers // 2
    k = (me // 2 - owner // 2) % chips
    b = (me + owner) % 2
    return (k - 1) % chips * 2 + jnp.where(k == 0, 1 - b, b)


def pick_kernel(order_ref, rows_ref, slots_ref, *outs):
    hi, mid, lo = split3(rows_ref[...])
    block = slots_ref.shape[1]
    together = max(1, CHUNK // block)
    for first in range(0, len(outs), together):
        group = outs[first:first + together]
        slots = [slots_ref[pl.ds(order_ref[first + i], 1), :] for i in range(len(group))]
        hot = rows_hot(rows_ref.shape[1], jnp.concatenate(slots, axis=1))
        picked = dot(hi, hot) + dot(mid, hot) + dot(lo, hot)
        for i, out in enumerate(group):
            out[...] = picked[:, i * block:(i + 1) * block]


def pick_blocks(order, rows, slots):
    features, length = rows.shape
    block = slots.shape[1]
    count = order.shape[0]
    return kernel_call(
        pick_kernel, [shape((features, block))] * count,
        6 * features * length * count * block, 8 * features * count * block,
        in_specs=[SMEM, VMEM, VMEM], out_specs=[VMEM] * count,
    )(order, rows, slots)


def relation_kernel(rel_ref, edge_rel_ref, out_ref, pieces):
    count = rel_ref.shape[1]
    padded = pieces.shape[2]

    @pl.when(pl.program_id(0) == 0)
    def _():
        features = rel_ref.shape[0]
        tail = padded - count // LANES * LANES
        for piece, value in enumerate(split3(rel_ref[...])):
            pieces[piece, :, padded - tail:] = jnp.zeros((features, tail), BF16)
            pieces[piece, :, :count] = value

    hot = rows_hot(padded, edge_rel_ref[...])
    out_ref[...] = dot(pieces[0], hot) + dot(pieces[1], hot) + dot(pieces[2], hot)


def relation_rows(relation, edge_relation):
    features, count = relation.shape
    edges = edge_relation.shape[1]
    padded = pl.cdiv(count, LANES) * LANES
    return kernel_call(
        relation_kernel, shape((features, edges)),
        6 * features * padded * edges, 8 * features * edges,
        grid=(edges // CHUNK,),
        in_specs=[held((features, count)), pl.BlockSpec((1, CHUNK), lambda i: (0, i))],
        out_specs=pl.BlockSpec((features, CHUNK), lambda i: (0, i)),
        scratch_shapes=[pltpu.VMEM((3, features, padded), BF16)],
    )(relation, edge_relation)


def count_kernel(slots_ref, out_ref):
    table_rows = out_ref.shape[2]
    hits = lax.broadcasted_iota(I32, (slots_ref.shape[1], table_rows), 1) == slots_ref[0]
    counts = jnp.sum(jnp.where(hits, 1.0, 0.0), axis=0, keepdims=True)
    out_ref[0] = jnp.where(counts > 0.0, jnp.log(jnp.maximum(counts, 1.0)), -jnp.inf)


def slot_counts(neg_slots, table_rows):
    spans, negatives = neg_slots.shape
    return kernel_call(
        count_kernel, shape((spans, 1, table_rows)),
        2 * spans * negatives * table_rows, 512 * spans * negatives,
        grid=(spans,),
        in_specs=[pl.BlockSpec((1, negatives, 1), lambda i: (i, 0, 0))],
        out_specs=pl.BlockSpec((1, 1, table_rows), lambda i: (i, 0, 0)),
    )(neg_slots[:, :, None])


def hot_kernel(order_ref, slots_ref, out_ref):
    peers, block, _ = slots_ref.shape
    for j in range(peers):
        out_ref[j * block:(j + 1) * block, :] = columns_hot(slots_ref[order_ref[j]], out_ref.shape[1])


def home_hots(order, slots, rows):
    peers, block = slots.shape
    return kernel_call(
        hot_kernel, shape((peers * block, rows), BF16),
        2 * peers * block * rows, 2 * peers * block * rows,
        in_specs=[SMEM, VMEM], out_specs=VMEM,
    )(order, slots[:, :, None])


def query_kernel(*refs):
    edge_source_ref, rels_ref, *blocks = refs[:-4]
    heads_ref, columns_ref, rows_ref, pieces = refs[-4:]
    block = blocks[0].shape[1]

    @pl.when(pl.program_id(0) == 0)
    def _():
        for p, ref in enumerate(blocks):
            for piece, value in enumerate(split3(ref[...])):
                pieces[piece, :, p * block:(p + 1) * block] = value

    hot = rows_hot(pieces.shape[2], edge_source_ref[...])
    heads = dot(pieces[0], hot) + dot(pieces[1], hot) + dot(pieces[2], hot)
    heads_ref[...] = heads
    queries = complex_product(heads, rels_ref[...])
    hi, lo = split2(queries)
    columns_ref[0], columns_ref[1] = hi, lo
    hi, lo = split2(queries.T)
    rows_ref[...] = jnp.concatenate([hi, hi, lo], axis=1)


def query_rows(blocks, edge_source, rels):
    peers = len(blocks)
    features, block = blocks[0].shape
    edges = edge_source.shape[1]
    return kernel_call(
        query_kernel,
        [shape((features, edges)), shape((2, features, edges), BF16), shape((edges, 3 * features), BF16)],
        6 * features * peers * block * edges, 20 * features * edges,
        grid=(edges // CHUNK,),
        in_specs=[
            pl.BlockSpec((1, CHUNK), lambda i: (0, i)),
            pl.BlockSpec((features, CHUNK), lambda i: (0, i)),
        ] + [held((features, block))] * peers,
        out_specs=[
            pl.BlockSpec((features, CHUNK), lambda i: (0, i)),
            pl.BlockSpec((2, features, CHUNK), lambda i: (0, 0, i)),
            pl.BlockSpec((CHUNK, 3 * features), lambda i: (i, 0)),
        ],
        scratch_shapes=[pltpu.VMEM((3, features, peers * block), BF16)],
    )(edge_source, rels, *blocks)


def softmax_step(step, live, score, log_counts, edge_target, loss_ref, grad_ref):
    own = lax.broadcasted_iota(I32, score.shape, 1) == edge_target
    pos = jnp.sum(jnp.where(own, score, 0.0), axis=1, keepdims=True)
    score = score + log_counts
    peak = jnp.maximum(pos, jnp.max(score, axis=1, keepdims=True))
    weight = jnp.exp(score - peak)
    pos_weight = jnp.exp(pos - peak)
    sum_all = pos_weight + jnp.sum(weight, axis=1, keepdims=True)
    edge = step * score.shape[0] + lax.broadcasted_iota(I32, pos.shape, 0)
    is_live = jnp.where(edge < live, 1.0, 0.0)
    loss = (peak - pos + jnp.log(sum_all)) * is_live
    loss_ref[...] = jnp.broadcast_to(loss, (loss.shape[0], LANES)).T[:1]
    scale = is_live / sum_all
    pos_grad = pos_weight * scale - is_live
    grad = weight * scale + jnp.where(own, pos_grad, 0.0)
    grad_ref[0], grad_ref[1] = split2(grad)


def score_kernel(peers, *refs):
    live_ref, rows_ref, counts_ref, edge_target_ref = refs[:4]
    blocks = refs[4:4 + peers]
    loss_ref, grad_ref, table_ref, scores = refs[4 + peers:]
    features, block = blocks[0].shape
    step = pl.program_id(0)
    last = pl.num_programs(0) - 1

    @pl.when(step == 0)
    def _():
        for p, ref in enumerate(blocks):
            hi, lo = split2(ref[...])
            at = pl.ds(p * block, block)
            table_ref[:features, at] = hi
            table_ref[features:2 * features, at] = lo
            table_ref[2 * features:, at] = hi

    def multiply():
        scores[step % 2] = dot(rows_ref[...], table_ref[...])

    def finish():
        softmax_step(
            step - 1, live_ref[0], scores[(step + 1) % 2], counts_ref[0], edge_target_ref[...],
            loss_ref, grad_ref,
        )

    @pl.when(step == 0)
    def _():
        multiply()

    @pl.when((step > 0) & (step < last))
    def _():
        multiply()
        finish()

    @pl.when(step == last)
    def _():
        finish()


def score_spans(live, blocks, rows, counts, edge_target):
    peers = len(blocks)
    features, block = blocks[0].shape
    edges = edge_target.shape[0]
    table_rows = peers * block
    chunk = CHUNK
    per_span = SPAN // chunk
    steps = edges // chunk

    def now(i):
        return jnp.minimum(i, steps - 1)

    def before(i):
        return jnp.maximum(i - 1, 0)

    return kernel_call(
        functools.partial(score_kernel, peers),
        [
            shape((1, edges)),
            shape((2, edges, table_rows), BF16),
            shape((3 * features, table_rows), BF16),
        ],
        6 * features * table_rows * edges, 30 * features * edges,
        grid=(steps + 1,),
        in_specs=[
            SMEM,
            pl.BlockSpec((chunk, 3 * features), lambda i: (now(i), 0)),
            pl.BlockSpec((1, 1, table_rows), lambda i: (before(i) // per_span, 0, 0)),
            pl.BlockSpec((chunk, 1), lambda i: (before(i), 0)),
        ] + [held((features, block))] * peers,
        out_specs=[
            pl.BlockSpec((1, chunk), lambda i: (0, before(i))),
            pl.BlockSpec((2, chunk, table_rows), lambda i: (0, before(i), 0)),
            held((3 * features, table_rows)),
        ],
        scratch_shapes=[pltpu.VMEM((2, chunk, table_rows), F32)],
    )(live, rows, counts, edge_target, *blocks)


def table_grad_kernel(columns_ref, grad_ref, *outs):
    step = pl.program_id(0)
    block = outs[0].shape[1]
    result = (
        dot(columns_ref[0], grad_ref[0])
        + dot(columns_ref[0], grad_ref[1])
        + dot(columns_ref[1], grad_ref[0])
    )
    for pair in range(len(outs) // 2):
        @pl.when(step == pair)
        def _():
            outs[2 * pair][...] = result[:, :block]
            outs[2 * pair + 1][...] = result[:, block:]


def table_grads(columns, grad, block, first, count):
    _, features, edges = columns.shape
    return kernel_call(
        table_grad_kernel, [shape((features, block))] * count,
        6 * features * count * block * edges, 4 * edges * (features + count * block),
        grid=(count // 2,),
        in_specs=[
            held((2, features, edges)),
            pl.BlockSpec((2, edges, 2 * block), lambda i: (0, 0, first // 2 + i)),
        ],
        out_specs=[held((features, block))] * count,
    )(columns, grad)


def relation_grad_kernel(
    steps, me_ref, table_ref, grad_ref, heads_ref, rels_ref, edge_rel_ref, source_ref, *refs
):
    outs, lines, total = refs[:-2], refs[-2], refs[-1]
    groups = len(outs) // 2
    half, width = outs[0].shape
    step = pl.program_id(0)
    features, chunk = heads_ref.shape
    tile = total.shape[2]

    @pl.when(step < steps)
    def _():
        hi, lo = table_ref[:features], table_ref[features:2 * features]
        query_grad = dot_nt(hi, grad_ref[0]) + dot_nt(hi, grad_ref[1]) + dot_nt(lo, grad_ref[0])
        source_ref[0], source_ref[1] = split2(conj_product(query_grad, rels_ref[...]))
        lines[step] = jnp.concatenate(split2(conj_product(query_grad, heads_ref[...])), axis=1)

    @pl.when(step >= steps)
    def _():
        part = None
        for i in range(steps):
            slots = edge_rel_ref[i * chunk:(i + 1) * chunk, :] - (step - steps) * tile
            hot = columns_hot(slots, tile)
            term = dot(lines[i, :, :chunk], hot) + dot(lines[i, :, chunk:], hot)
            part = term if part is None else part + term
        total[step - steps] = part

    @pl.when(step == pl.num_programs(0) - 1)
    def _():
        group, core = me_ref[0], me_ref[1]
        for j in range(groups):
            for at in range(0, width, LANES):
                start = (group ^ j) * width + at
                rows = total.at[start // tile, :, pl.ds(pl.multiple_of(start % tile, LANES), LANES)]
                outs[j][:, at:at + LANES] = rows[pl.ds(pl.multiple_of(core * half, 8), half), :]
                outs[groups + j][:, at:at + LANES] = rows[
                    pl.ds(pl.multiple_of((1 - core) * half, 8), half), :
                ]


def relation_grads(me, table, grad, heads, rels, edge_relation, groups, width):
    features, edges = heads.shape
    table_rows = table.shape[1]
    chunk = CHUNK
    steps = edges // chunk
    tile = math.gcd(groups * width, WIDE)
    tiles = groups * width // tile

    def now(i):
        return jnp.minimum(i, steps - 1)

    return kernel_call(
        functools.partial(relation_grad_kernel, steps),
        [shape((2, features, edges), BF16)] + [shape((features // 2, width))] * (2 * groups),
        10 * features * table_rows * edges, 30 * features * edges,
        grid=(steps + tiles,),
        in_specs=[
            SMEM,
            held((3 * features, table_rows)),
            pl.BlockSpec((2, chunk, table_rows), lambda i: (0, now(i), 0)),
            pl.BlockSpec((features, chunk), lambda i: (0, now(i))),
            pl.BlockSpec((features, chunk), lambda i: (0, now(i))),
            held((edges, 1)),
        ],
        out_specs=[pl.BlockSpec((2, features, chunk), lambda i: (0, 0, now(i)))]
        + [held((features // 2, width))] * (2 * groups),
        scratch_shapes=[
            pltpu.VMEM((steps, features, 2 * chunk), BF16),
            pltpu.VMEM((tiles, features, tile), F32),
        ],
    )(me, table, grad, heads, rels, edge_relation)


def source_grad_kernel(first, rows_ref, edge_source_ref, *outs):
    step = pl.program_id(0)
    block = outs[0].shape[1]
    hot = columns_hot(edge_source_ref[...] - (first * block + step * 2 * block), 2 * block)
    result = dot(rows_ref[0], hot) + dot(rows_ref[1], hot)
    for pair in range(len(outs) // 2):
        @pl.when(step == pair)
        def _():
            outs[2 * pair][...] = result[:, :block]
            outs[2 * pair + 1][...] = result[:, block:]


def source_grads(rows, edge_source, block, first, count):
    _, features, edges = rows.shape
    return kernel_call(
        functools.partial(source_grad_kernel, first), [shape((features, block))] * count,
        4 * features * count * block * edges, 4 * features * (edges + count * block),
        grid=(count // 2,),
        in_specs=[held((2, features, edges)), held((edges, 1))],
        out_specs=[held((features, block))] * count,
    )(rows, edge_source)


def put_back(blocks, hot):
    hi, lo = split2(jnp.concatenate([ref[...] for ref in blocks], axis=1))
    return dot(hi, hot) + dot(lo, hot)


def target_home_kernel(hot_ref, source_hot_ref, own_ref, entity_ref, *refs):
    blocks, out_ref, entity_out_ref = refs[:-2], refs[-2], refs[-1]
    block = own_ref.shape[1]
    own_hot = source_hot_ref[source_hot_ref.shape[0] - block:, :]
    out_ref[...] = put_back(blocks, hot_ref[...]) + put_back([own_ref], own_hot)
    entity_out_ref[...] = entity_ref[...]


def target_home(hots, source_hots, own, entity, blocks):
    features, rows = entity.shape
    return kernel_call(
        target_home_kernel, [shape((features, rows))] * 2,
        4 * features * rows * hots.shape[0], 8 * features * hots.shape[0],
        in_specs=[VMEM] * (4 + len(blocks)), out_specs=[VMEM] * 2,
    )(hots, source_hots, own, entity, *blocks)


def adagrad(params, state, gradient):
    new_state = state + jnp.mean(gradient * gradient, axis=0, keepdims=True)
    return params - gradient * (learn_rate / jnp.sqrt(new_state))


def entity_kernel(other_ref, entity_ref, state_ref, hot_ref, *refs):
    blocks = refs[:-1]
    here = len(blocks) * blocks[0].shape[1]
    gradient = other_ref[...] + put_back(blocks, hot_ref[:here, :])
    refs[-1][...] = adagrad(entity_ref[...], state_ref[...], gradient)


def entity_update(hots, blocks, other, entity, state):
    features, rows = entity.shape
    return kernel_call(
        entity_kernel, shape((features, rows)),
        4 * features * rows * hots.shape[0], 8 * features * hots.shape[0],
        in_specs=[VMEM] * (4 + len(blocks)), out_specs=VMEM,
    )(other, entity, state, hots, *blocks)


def add_kernel(*refs):
    count = len(refs) // 3
    for i in range(count):
        refs[2 * count + i][...] = refs[i][...] + refs[count + i][...]


def added(ours, theirs):
    count = len(ours)
    dims = ours[0].shape
    return kernel_call(
        add_kernel, [shape(dims)] * count,
        count * dims[0] * dims[1], 12 * count * dims[0] * dims[1],
        in_specs=[VMEM] * (2 * count), out_specs=[VMEM] * count,
    )(*ours, *theirs)


def cut_kernel(me_ref, *refs):
    chips = me_ref.shape[0]
    terms, outs, whole = refs[:-1 - chips], refs[-1 - chips:-1], refs[-1]
    rows, width = outs[0].shape
    have = terms[0].shape[0]
    total = terms[0][...]
    for term in terms[1:]:
        total = total + term[...]
    whole[:have, :] = total
    if have < chips * rows:
        whole[have:, :] = jnp.zeros((chips * rows - have, width), F32)
    for k, out in enumerate(outs):
        out[...] = whole[pl.ds(pl.multiple_of(me_ref[k] * rows, 8), rows), :]


def cut_pieces(order, terms):
    chips = order.shape[0]
    half, width = terms[0].shape
    rows = pl.cdiv(half, 8 * chips) * 8
    return kernel_call(
        cut_kernel, [shape((rows, width))] * chips,
        len(terms) * half * width, 4 * (len(terms) + 1) * half * width,
        in_specs=[SMEM] + [VMEM] * len(terms), out_specs=[VMEM] * chips,
        scratch_shapes=[pltpu.VMEM((chips * rows, width), F32)],
    )(order, *terms)


def sum_kernel(*refs):
    total = refs[0][...]
    for ref in refs[1:-1]:
        total = total + ref[...]
    refs[-1][...] = total


def sum_pieces(pieces):
    rows, width = pieces[0].shape
    return kernel_call(
        sum_kernel, shape((rows, width)),
        len(pieces) * rows * width, 4 * (len(pieces) + 1) * rows * width,
        in_specs=[VMEM] * len(pieces), out_specs=VMEM,
    )(*pieces)


def join_kernel(me_ref, *refs):
    pieces, out_ref, whole = refs[:-2], refs[-2], refs[-1]
    rows = pieces[0].shape[0]
    for k, piece in enumerate(pieces):
        whole[pl.ds(pl.multiple_of(me_ref[k] * rows, 8), rows), :] = piece[...]
    out_ref[...] = whole[:out_ref.shape[0], :]


def join_pieces(order, pieces, half):
    rows, width = pieces[0].shape
    return kernel_call(
        join_kernel, shape((half, width)),
        half * width, 8 * half * width,
        in_specs=[SMEM] + [VMEM] * len(pieces), out_specs=VMEM,
        scratch_shapes=[pltpu.VMEM((len(pieces) * rows, width), F32)],
    )(order, *pieces)


def relation_update_kernel(me_ref, relation_ref, state_ref, *refs):
    parts, out_ref, total = refs[:-2], refs[-2], refs[-1]
    groups = len(parts) // 2
    half, width = parts[0].shape
    group, core = me_ref[0], me_ref[1]
    for j in range(groups):
        at = pl.ds(pl.multiple_of((group ^ j) * width, LANES), width)
        total[pl.ds(pl.multiple_of(core * half, 8), half), at] = parts[j][...]
        total[pl.ds(pl.multiple_of((1 - core) * half, 8), half), at] = parts[groups + j][...]
    gradient = total[:, :out_ref.shape[1]]
    out_ref[...] = adagrad(relation_ref[...], state_ref[...], gradient)


def relation_update(me, relation, state, parts):
    features, count = relation.shape
    _, width = parts[0].shape
    groups = len(parts) // 2
    return kernel_call(
        relation_update_kernel, shape((features, count)),
        8 * features * count, 12 * features * count,
        in_specs=[SMEM] + [VMEM] * (2 + len(parts)), out_specs=VMEM,
        scratch_shapes=[pltpu.VMEM((features, groups * width), F32)],
    )(me, relation, state, *parts)


def sent_on(value, hop, peers):
    return lax.ppermute(value, "shard", [(i, partner(i, hop, peers, 1)) for i in range(peers)])


def sent_across(value, hop, peers, groups, by):
    pairs = [
        (g * peers + i, (g + by) % groups * peers + partner(i, hop, peers, 1))
        for g in range(groups)
        for i in range(peers)
    ]
    return lax.ppermute(value, ("group", "shard"), pairs)


def sent_group(value, bit, groups):
    return lax.ppermute(value, "group", [(g, g ^ bit) for g in range(groups)])


def relation_sum(kept, sent, peers, groups, chip):
    chips = peers // 2
    half = kept[0].shape[0]
    other_core = (0, 1)
    sent = [sent_on(b, other_core, peers) for b in sent]
    mine = added(kept, sent)
    terms = [mine[0]] + [sent_group(mine[j], j, groups) for j in range(1, groups)]
    ahead = (chip + jnp.arange(chips, dtype=I32)) % chips
    behind = (chip - jnp.arange(chips, dtype=I32)) % chips
    pieces = cut_pieces(ahead, terms)
    pieces = [pieces[0]] + [sent_on(pieces[k], (k, 0), peers) for k in range(1, chips)]
    piece = sum_pieces(pieces)
    pieces = [piece] + [sent_on(piece, (k, 0), peers) for k in range(1, chips)]
    block = join_pieces(behind, pieces, half)
    blocks = [block] + [sent_group(block, j, groups) for j in range(1, groups)]
    return blocks + [sent_on(b, other_core, peers) for b in blocks]


def on_device(
    entity, entity_state, relation, relation_state, src_send, dst_send,
    edge_source, edge_relation, edge_target, neg_slots, edge_count,
):
    rows, _ = entity.shape
    relations = relation.shape[0]
    peers, block = src_send.shape[1:]
    groups = lax.axis_size("group")
    group = lax.axis_index("group").astype(I32)
    me = lax.axis_index("shard").astype(I32)
    width = pl.cdiv(relations, groups * LANES) * LANES
    entity_t, relation_t = entity.T, relation.T
    ways = hops(peers)
    order = jnp.stack([partner(me, hop, peers, 1) for hop in ways])
    here = jnp.stack([group, me % 2])

    def placed(slots):
        return places_of(me, slots // block, peers) * block + slots % block

    edge_source, edge_target = placed(edge_source), placed(edge_target)
    early = peers // 2
    sources = pick_blocks(order[:2], entity_t, src_send[0])
    sources += pick_blocks(order[2:], entity_t, src_send[0])
    sources = [
        sent_on(value, hop, peers) if hop != (0, 0) else value
        for value, hop in zip(sources, ways)
    ]
    targets = pick_blocks(order, entity_t, dst_send[0])
    targets = [sent_across(value, hop, peers, groups, -1) for value, hop in zip(targets, ways)]
    rels = relation_rows(relation_t, edge_relation.reshape(1, -1))
    counts = slot_counts(placed(neg_slots), peers * block)
    source_hots = home_hots(order, src_send[0], rows)
    target_hots = home_hots(order, dst_send[0], rows)
    heads, query_columns, query_lines = query_rows(sources, edge_source.reshape(1, -1), rels)
    loss, grad, table = score_spans(
        edge_count, targets, query_lines, counts, edge_target.reshape(-1, 1)
    )
    table_parts = table_grads(query_columns, grad, block, 0, early)
    table_parts += table_grads(query_columns, grad, block, early, peers - early)
    back = [(-hop[0], hop[1]) for hop in ways]
    home = [
        sent_across(value, hop, peers, groups, 1)
        for value, hop in zip(table_parts[:early], back[:early])
    ]
    home += [
        sent_across(value, hop, peers, groups, 1)
        for value, hop in zip(table_parts[early:], back[early:])
    ]
    source_lines, *halves = relation_grads(
        here, table, grad, heads, rels, edge_relation.reshape(-1, 1), groups, width
    )
    edge_source = edge_source.reshape(-1, 1)
    source_parts = source_grads(source_lines, edge_source, block, 0, 2)
    source_parts += source_grads(source_lines, edge_source, block, 2, peers - 2)
    returned = []
    for value, hop, way in zip(source_parts, back, ways):
        returned.append(sent_on(value, hop, peers) if way != (0, 0) else value)
    parts = relation_sum(halves[:groups], halves[groups:], peers, groups, me // 2)
    relation_new = relation_update(here, relation_t, relation_state.reshape(1, -1), parts)
    target_part, entity_t = target_home(target_hots, source_hots, returned[-1], entity_t, home)
    entity_new = entity_update(
        source_hots, returned[:-1], target_part, entity_t, entity_state.reshape(1, -1)
    )
    return entity_new.T, relation_new.T, loss.reshape(-1)


def solution(mesh):
    both = ("group", "shard")
    return jax.shard_map(
        on_device,
        mesh=mesh,
        in_specs=(
            P(both, None), P(both), P(), P(), P(both, None, None), P(both, None, None),
            P(both), P(both), P(both), P(both, None), P(both),
        ),
        out_specs=(P(both, None), P(), P(both)),
        check_vma=False,
    )
```

```python
import functools
import math

import jax
import jax.numpy as jnp
from jax import lax
from jax.experimental import pallas as pl
from jax.experimental.pallas import tpu as pltpu
from jax.sharding import PartitionSpec as P


SPAN = 512
LANES = 128
CHUNK = 256
WIDE = 512


learn_rate = 0.5

F32, BF16, I32 = jnp.float32, jnp.bfloat16, jnp.int32
VMEM = pl.BlockSpec(memory_space=pltpu.VMEM)
SMEM = pl.BlockSpec(memory_space=pltpu.SMEM)
VMEM_LIMIT = 24 << 20


def kernel_call(kernel, outs, flops, moved, **kw):
    semantics = ("arbitrary",) if "grid" in kw else None
    return pl.pallas_call(
        kernel,
        out_shape=outs,
        compiler_params=pltpu.CompilerParams(
            vmem_limit_bytes=VMEM_LIMIT, dimension_semantics=semantics
        ),
        cost_estimate=pl.CostEstimate(flops=flops, bytes_accessed=moved, transcendentals=0),
        **kw,
    )


def shape(dims, dtype=F32):
    return jax.ShapeDtypeStruct(dims, dtype)


def held(dims):
    return pl.BlockSpec(dims, lambda i: (0,) * len(dims))


def split2(x):
    hi = x.astype(BF16)
    return hi, (x - hi.astype(F32)).astype(BF16)


def split3(x):
    hi = x.astype(BF16)
    rest = x - hi.astype(F32)
    mid = rest.astype(BF16)
    return hi, mid, (rest - mid.astype(F32)).astype(BF16)


def dot(a, b):
    return jnp.dot(a, b, preferred_element_type=F32)


def dot_nt(a, b):
    return lax.dot_general(a, b, (((1,), (1,)), ((), ())), preferred_element_type=F32)


def one_hot(mask):
    return jnp.where(mask, 1.0, 0.0).astype(BF16)


def rows_hot(length, slots):
    return one_hot(lax.broadcasted_iota(I32, (length, slots.shape[1]), 0) == slots)


def columns_hot(slots, length):
    return one_hot(lax.broadcasted_iota(I32, (slots.shape[0], length), 1) == slots)


def complex_product(a, b):
    half = a.shape[0] // 2
    ar, ai, br, bi = a[:half], a[half:], b[:half], b[half:]
    return jnp.concatenate([ar * br - ai * bi, ar * bi + ai * br], axis=0)


def conj_product(a, b):
    half = a.shape[0] // 2
    ar, ai, br, bi = a[:half], a[half:], b[:half], b[half:]
    return jnp.concatenate([ar * br + ai * bi, ai * br - ar * bi], axis=0)


def hops(peers):
    chips = peers // 2
    ahead = [(k, b) for k in range(1, chips) for b in (0, 1)]
    return ahead + [(0, 1), (0, 0)]


def partner(me, hop, peers, sign):
    chips = peers // 2
    return (me // 2 + sign * hop[0]) % chips * 2 + (me % 2 + hop[1]) % 2


def places_of(me, owner, peers):
    chips = peers // 2
    k = (me // 2 - owner // 2) % chips
    b = (me + owner) % 2
    return (k - 1) % chips * 2 + jnp.where(k == 0, 1 - b, b)


def pick_kernel(order_ref, rows_ref, slots_ref, *outs):
    hi, mid, lo = split3(rows_ref[...])
    block = slots_ref.shape[1]
    together = max(1, CHUNK // block)
    for first in range(0, len(outs), together):
        group = outs[first:first + together]
        slots = [slots_ref[pl.ds(order_ref[first + i], 1), :] for i in range(len(group))]
        hot = rows_hot(rows_ref.shape[1], jnp.concatenate(slots, axis=1))
        picked = dot(hi, hot) + dot(mid, hot) + dot(lo, hot)
        for i, out in enumerate(group):
            out[...] = picked[:, i * block:(i + 1) * block]


def pick_blocks(order, rows, slots):
    features, length = rows.shape
    block = slots.shape[1]
    count = order.shape[0]
    return kernel_call(
        pick_kernel, [shape((features, block))] * count,
        6 * features * length * count * block, 8 * features * count * block,
        in_specs=[SMEM, VMEM, VMEM], out_specs=[VMEM] * count,
    )(order, rows, slots)


def relation_kernel(rel_ref, edge_rel_ref, out_ref, pieces):
    count = rel_ref.shape[1]
    padded = pieces.shape[2]

    @pl.when(pl.program_id(0) == 0)
    def _():
        features = rel_ref.shape[0]
        tail = padded - count // LANES * LANES
        for piece, value in enumerate(split3(rel_ref[...])):
            pieces[piece, :, padded - tail:] = jnp.zeros((features, tail), BF16)
            pieces[piece, :, :count] = value

    hot = rows_hot(padded, edge_rel_ref[...])
    out_ref[...] = dot(pieces[0], hot) + dot(pieces[1], hot) + dot(pieces[2], hot)


def relation_rows(relation, edge_relation):
    features, count = relation.shape
    edges = edge_relation.shape[1]
    padded = pl.cdiv(count, LANES) * LANES
    return kernel_call(
        relation_kernel, shape((features, edges)),
        6 * features * padded * edges, 8 * features * edges,
        grid=(edges // CHUNK,),
        in_specs=[held((features, count)), pl.BlockSpec((1, CHUNK), lambda i: (0, i))],
        out_specs=pl.BlockSpec((features, CHUNK), lambda i: (0, i)),
        scratch_shapes=[pltpu.VMEM((3, features, padded), BF16)],
    )(relation, edge_relation)


def count_kernel(slots_ref, out_ref):
    table_rows = out_ref.shape[2]
    hits = lax.broadcasted_iota(I32, (slots_ref.shape[1], table_rows), 1) == slots_ref[0]
    counts = jnp.sum(jnp.where(hits, 1.0, 0.0), axis=0, keepdims=True)
    out_ref[0] = jnp.where(counts > 0.0, jnp.log(jnp.maximum(counts, 1.0)), -jnp.inf)


def slot_counts(neg_slots, table_rows):
    spans, negatives = neg_slots.shape
    return kernel_call(
        count_kernel, shape((spans, 1, table_rows)),
        2 * spans * negatives * table_rows, 512 * spans * negatives,
        grid=(spans,),
        in_specs=[pl.BlockSpec((1, negatives, 1), lambda i: (i, 0, 0))],
        out_specs=pl.BlockSpec((1, 1, table_rows), lambda i: (i, 0, 0)),
    )(neg_slots[:, :, None])


def hot_kernel(order_ref, slots_ref, out_ref):
    peers, block, _ = slots_ref.shape
    for j in range(peers):
        out_ref[j * block:(j + 1) * block, :] = columns_hot(slots_ref[order_ref[j]], out_ref.shape[1])


def home_hots(order, slots, rows):
    peers, block = slots.shape
    return kernel_call(
        hot_kernel, shape((peers * block, rows), BF16),
        2 * peers * block * rows, 2 * peers * block * rows,
        in_specs=[SMEM, VMEM], out_specs=VMEM,
    )(order, slots[:, :, None])


def query_kernel(*refs):
    edge_source_ref, rels_ref, *blocks = refs[:-4]
    heads_ref, columns_ref, rows_ref, pieces = refs[-4:]
    block = blocks[0].shape[1]

    @pl.when(pl.program_id(0) == 0)
    def _():
        for p, ref in enumerate(blocks):
            for piece, value in enumerate(split3(ref[...])):
                pieces[piece, :, p * block:(p + 1) * block] = value

    hot = rows_hot(pieces.shape[2], edge_source_ref[...])
    heads = dot(pieces[0], hot) + dot(pieces[1], hot) + dot(pieces[2], hot)
    heads_ref[...] = heads
    queries = complex_product(heads, rels_ref[...])
    hi, lo = split2(queries)
    columns_ref[0], columns_ref[1] = hi, lo
    hi, lo = split2(queries.T)
    rows_ref[...] = jnp.concatenate([hi, hi, lo], axis=1)


def query_rows(blocks, edge_source, rels):
    peers = len(blocks)
    features, block = blocks[0].shape
    edges = edge_source.shape[1]
    return kernel_call(
        query_kernel,
        [shape((features, edges)), shape((2, features, edges), BF16), shape((edges, 3 * features), BF16)],
        6 * features * peers * block * edges, 20 * features * edges,
        grid=(edges // CHUNK,),
        in_specs=[
            pl.BlockSpec((1, CHUNK), lambda i: (0, i)),
            pl.BlockSpec((features, CHUNK), lambda i: (0, i)),
        ] + [held((features, block))] * peers,
        out_specs=[
            pl.BlockSpec((features, CHUNK), lambda i: (0, i)),
            pl.BlockSpec((2, features, CHUNK), lambda i: (0, 0, i)),
            pl.BlockSpec((CHUNK, 3 * features), lambda i: (i, 0)),
        ],
        scratch_shapes=[pltpu.VMEM((3, features, peers * block), BF16)],
    )(edge_source, rels, *blocks)


def softmax_step(step, live, score, log_counts, edge_target, loss_ref, grad_ref):
    own = lax.broadcasted_iota(I32, score.shape, 1) == edge_target
    pos = jnp.sum(jnp.where(own, score, 0.0), axis=1, keepdims=True)
    score = score + log_counts
    peak = jnp.maximum(pos, jnp.max(score, axis=1, keepdims=True))
    weight = jnp.exp(score - peak)
    pos_weight = jnp.exp(pos - peak)
    sum_all = pos_weight + jnp.sum(weight, axis=1, keepdims=True)
    edge = step * score.shape[0] + lax.broadcasted_iota(I32, pos.shape, 0)
    is_live = jnp.where(edge < live, 1.0, 0.0)
    loss = (peak - pos + jnp.log(sum_all)) * is_live
    loss_ref[...] = jnp.broadcast_to(loss, (loss.shape[0], LANES)).T[:1]
    scale = is_live / sum_all
    pos_grad = pos_weight * scale - is_live
    grad = weight * scale + jnp.where(own, pos_grad, 0.0)
    grad_ref[0], grad_ref[1] = split2(grad)


def score_kernel(peers, *refs):
    live_ref, rows_ref, counts_ref, edge_target_ref = refs[:4]
    blocks = refs[4:4 + peers]
    loss_ref, grad_ref, table_ref, scores = refs[4 + peers:]
    features, block = blocks[0].shape
    step = pl.program_id(0)
    last = pl.num_programs(0) - 1

    @pl.when(step == 0)
    def _():
        for p, ref in enumerate(blocks):
            hi, lo = split2(ref[...])
            at = pl.ds(p * block, block)
            table_ref[:features, at] = hi
            table_ref[features:2 * features, at] = lo
            table_ref[2 * features:, at] = hi

    def multiply():
        scores[step % 2] = dot(rows_ref[...], table_ref[...])

    def finish():
        softmax_step(
            step - 1, live_ref[0], scores[(step + 1) % 2], counts_ref[0], edge_target_ref[...],
            loss_ref, grad_ref,
        )

    @pl.when(step == 0)
    def _():
        multiply()

    @pl.when((step > 0) & (step < last))
    def _():
        multiply()
        finish()

    @pl.when(step == last)
    def _():
        finish()


def score_spans(live, blocks, rows, counts, edge_target):
    peers = len(blocks)
    features, block = blocks[0].shape
    edges = edge_target.shape[0]
    table_rows = peers * block
    chunk = CHUNK
    per_span = SPAN // chunk
    steps = edges // chunk

    def now(i):
        return jnp.minimum(i, steps - 1)

    def before(i):
        return jnp.maximum(i - 1, 0)

    return kernel_call(
        functools.partial(score_kernel, peers),
        [
            shape((1, edges)),
            shape((2, edges, table_rows), BF16),
            shape((3 * features, table_rows), BF16),
        ],
        6 * features * table_rows * edges, 30 * features * edges,
        grid=(steps + 1,),
        in_specs=[
            SMEM,
            pl.BlockSpec((chunk, 3 * features), lambda i: (now(i), 0)),
            pl.BlockSpec((1, 1, table_rows), lambda i: (before(i) // per_span, 0, 0)),
            pl.BlockSpec((chunk, 1), lambda i: (before(i), 0)),
        ] + [held((features, block))] * peers,
        out_specs=[
            pl.BlockSpec((1, chunk), lambda i: (0, before(i))),
            pl.BlockSpec((2, chunk, table_rows), lambda i: (0, before(i), 0)),
            held((3 * features, table_rows)),
        ],
        scratch_shapes=[pltpu.VMEM((2, chunk, table_rows), F32)],
    )(live, rows, counts, edge_target, *blocks)


def table_grad_kernel(columns_ref, grad_ref, *outs):
    step = pl.program_id(0)
    block = outs[0].shape[1]
    result = (
        dot(columns_ref[0], grad_ref[0])
        + dot(columns_ref[0], grad_ref[1])
        + dot(columns_ref[1], grad_ref[0])
    )
    for pair in range(len(outs) // 2):
        @pl.when(step == pair)
        def _():
            outs[2 * pair][...] = result[:, :block]
            outs[2 * pair + 1][...] = result[:, block:]


def table_grads(columns, grad, block, first, count):
    _, features, edges = columns.shape
    return kernel_call(
        table_grad_kernel, [shape((features, block))] * count,
        6 * features * count * block * edges, 4 * edges * (features + count * block),
        grid=(count // 2,),
        in_specs=[
            held((2, features, edges)),
            pl.BlockSpec((2, edges, 2 * block), lambda i: (0, 0, first // 2 + i)),
        ],
        out_specs=[held((features, block))] * count,
    )(columns, grad)


def edge_grad_kernel(table_ref, grad_ref, heads_ref, rels_ref, source_ref, relation_ref):
    features = heads_ref.shape[0]
    hi, lo = table_ref[:features], table_ref[features:2 * features]
    query_grad = dot_nt(hi, grad_ref[0]) + dot_nt(hi, grad_ref[1]) + dot_nt(lo, grad_ref[0])
    source_ref[0], source_ref[1] = split2(conj_product(query_grad, rels_ref[...]))
    relation_ref[0], relation_ref[1] = split2(conj_product(query_grad, heads_ref[...]))


def edge_grads(table, grad, heads, rels):
    features, edges = heads.shape
    table_rows = table.shape[1]
    chunk = CHUNK
    columns = pl.BlockSpec((features, chunk), lambda i: (0, i))
    pieces = pl.BlockSpec((2, features, chunk), lambda i: (0, 0, i))
    return kernel_call(
        edge_grad_kernel, [shape((2, features, edges), BF16)] * 2,
        6 * features * table_rows * edges, 20 * features * edges,
        grid=(edges // chunk,),
        in_specs=[
            held((3 * features, table_rows)),
            pl.BlockSpec((2, chunk, table_rows), lambda i: (0, i, 0)),
            columns,
            columns,
        ],
        out_specs=[pieces, pieces],
    )(table, grad, heads, rels)


def relation_grad_kernel(me_ref, lines_ref, edge_rel_ref, *refs):
    outs, total = refs[:-1], refs[-1]
    groups = len(outs) // 2
    half, width = outs[0].shape
    tile = total.shape[2]
    step = pl.program_id(0)
    hot = columns_hot(edge_rel_ref[...] - step * tile, tile)
    total[step] = dot(lines_ref[0], hot) + dot(lines_ref[1], hot)

    @pl.when(step == pl.num_programs(0) - 1)
    def _():
        group, core = me_ref[0], me_ref[1]
        for j in range(groups):
            for at in range(0, width, LANES):
                start = (group ^ j) * width + at
                rows = total.at[start // tile, :, pl.ds(pl.multiple_of(start % tile, LANES), LANES)]
                outs[j][:, at:at + LANES] = rows[pl.ds(pl.multiple_of(core * half, 8), half), :]
                outs[groups + j][:, at:at + LANES] = rows[
                    pl.ds(pl.multiple_of((1 - core) * half, 8), half), :
                ]


def relation_grads(me, lines, edge_relation, groups, width):
    _, features, edges = lines.shape
    tile = math.gcd(groups * width, WIDE)
    tiles = groups * width // tile
    return kernel_call(
        relation_grad_kernel, [shape((features // 2, width))] * (2 * groups),
        4 * features * groups * width * edges, 4 * features * (edges + groups * width),
        grid=(tiles,),
        in_specs=[SMEM, held((2, features, edges)), held((edges, 1))],
        out_specs=[held((features // 2, width))] * (2 * groups),
        scratch_shapes=[pltpu.VMEM((tiles, features, tile), F32)],
    )(me, lines, edge_relation)


def source_grad_kernel(first, rows_ref, edge_source_ref, *outs):
    step = pl.program_id(0)
    block = outs[0].shape[1]
    hot = columns_hot(edge_source_ref[...] - (first * block + step * 2 * block), 2 * block)
    result = dot(rows_ref[0], hot) + dot(rows_ref[1], hot)
    for pair in range(len(outs) // 2):
        @pl.when(step == pair)
        def _():
            outs[2 * pair][...] = result[:, :block]
            outs[2 * pair + 1][...] = result[:, block:]


def source_grads(rows, edge_source, block, first, count):
    _, features, edges = rows.shape
    return kernel_call(
        functools.partial(source_grad_kernel, first), [shape((features, block))] * count,
        4 * features * count * block * edges, 4 * features * (edges + count * block),
        grid=(count // 2,),
        in_specs=[held((2, features, edges)), held((edges, 1))],
        out_specs=[held((features, block))] * count,
    )(rows, edge_source)


def put_back(blocks, hot):
    hi, lo = split2(jnp.concatenate([ref[...] for ref in blocks], axis=1))
    return dot(hi, hot) + dot(lo, hot)


def source_home_kernel(hot_ref, entity_ref, *refs):
    blocks, out_ref, entity_out_ref = refs[:-2], refs[-2], refs[-1]
    out_ref[...] = put_back(blocks, hot_ref[...])
    entity_out_ref[...] = entity_ref[...]


def source_home(hots, entity, blocks):
    features, rows = entity.shape
    return kernel_call(
        source_home_kernel, [shape((features, rows))] * 2,
        4 * features * rows * hots.shape[0], 8 * features * hots.shape[0],
        in_specs=[VMEM] * (2 + len(blocks)), out_specs=[VMEM] * 2,
    )(hots, entity, *blocks)


def adagrad(params, state, gradient):
    new_state = state + jnp.mean(gradient * gradient, axis=0, keepdims=True)
    return params - gradient * (learn_rate / jnp.sqrt(new_state))


def entity_kernel(other_ref, entity_ref, state_ref, hot_ref, *refs):
    gradient = other_ref[...] + put_back(refs[:-1], hot_ref[...])
    refs[-1][...] = adagrad(entity_ref[...], state_ref[...], gradient)


def entity_update(hots, blocks, other, entity, state):
    features, rows = entity.shape
    return kernel_call(
        entity_kernel, shape((features, rows)),
        4 * features * rows * hots.shape[0], 8 * features * hots.shape[0],
        in_specs=[VMEM] * (4 + len(blocks)), out_specs=VMEM,
    )(other, entity, state, hots, *blocks)


def add_kernel(*refs):
    count = len(refs) // 3
    for i in range(count):
        refs[2 * count + i][...] = refs[i][...] + refs[count + i][...]


def added(ours, theirs):
    count = len(ours)
    dims = ours[0].shape
    return kernel_call(
        add_kernel, [shape(dims)] * count,
        count * dims[0] * dims[1], 12 * count * dims[0] * dims[1],
        in_specs=[VMEM] * (2 * count), out_specs=[VMEM] * count,
    )(*ours, *theirs)


def cut_kernel(me_ref, *refs):
    chips = me_ref.shape[0]
    terms, outs, whole = refs[:-1 - chips], refs[-1 - chips:-1], refs[-1]
    rows, width = outs[0].shape
    have = terms[0].shape[0]
    total = terms[0][...]
    for term in terms[1:]:
        total = total + term[...]
    whole[:have, :] = total
    if have < chips * rows:
        whole[have:, :] = jnp.zeros((chips * rows - have, width), F32)
    for k, out in enumerate(outs):
        out[...] = whole[pl.ds(pl.multiple_of(me_ref[k] * rows, 8), rows), :]


def cut_pieces(order, terms):
    chips = order.shape[0]
    half, width = terms[0].shape
    rows = pl.cdiv(half, 8 * chips) * 8
    return kernel_call(
        cut_kernel, [shape((rows, width))] * chips,
        len(terms) * half * width, 4 * (len(terms) + 1) * half * width,
        in_specs=[SMEM] + [VMEM] * len(terms), out_specs=[VMEM] * chips,
        scratch_shapes=[pltpu.VMEM((chips * rows, width), F32)],
    )(order, *terms)


def sum_kernel(*refs):
    total = refs[0][...]
    for ref in refs[1:-1]:
        total = total + ref[...]
    refs[-1][...] = total


def sum_pieces(pieces):
    rows, width = pieces[0].shape
    return kernel_call(
        sum_kernel, shape((rows, width)),
        len(pieces) * rows * width, 4 * (len(pieces) + 1) * rows * width,
        in_specs=[VMEM] * len(pieces), out_specs=VMEM,
    )(*pieces)


def join_kernel(me_ref, *refs):
    pieces, out_ref, whole = refs[:-2], refs[-2], refs[-1]
    rows = pieces[0].shape[0]
    for k, piece in enumerate(pieces):
        whole[pl.ds(pl.multiple_of(me_ref[k] * rows, 8), rows), :] = piece[...]
    out_ref[...] = whole[:out_ref.shape[0], :]


def join_pieces(order, pieces, half):
    rows, width = pieces[0].shape
    return kernel_call(
        join_kernel, shape((half, width)),
        half * width, 8 * half * width,
        in_specs=[SMEM] + [VMEM] * len(pieces), out_specs=VMEM,
        scratch_shapes=[pltpu.VMEM((len(pieces) * rows, width), F32)],
    )(order, *pieces)


def relation_update_kernel(me_ref, relation_ref, state_ref, *refs):
    parts, out_ref, total = refs[:-2], refs[-2], refs[-1]
    groups = len(parts) // 2
    half, width = parts[0].shape
    group, core = me_ref[0], me_ref[1]
    for j in range(groups):
        at = pl.ds(pl.multiple_of((group ^ j) * width, LANES), width)
        total[pl.ds(pl.multiple_of(core * half, 8), half), at] = parts[j][...]
        total[pl.ds(pl.multiple_of((1 - core) * half, 8), half), at] = parts[groups + j][...]
    gradient = total[:, :out_ref.shape[1]]
    out_ref[...] = adagrad(relation_ref[...], state_ref[...], gradient)


def relation_update(me, relation, state, parts):
    features, count = relation.shape
    _, width = parts[0].shape
    groups = len(parts) // 2
    return kernel_call(
        relation_update_kernel, shape((features, count)),
        8 * features * count, 12 * features * count,
        in_specs=[SMEM] + [VMEM] * (2 + len(parts)), out_specs=VMEM,
        scratch_shapes=[pltpu.VMEM((features, groups * width), F32)],
    )(me, relation, state, *parts)


def sent_on(value, hop, peers):
    return lax.ppermute(value, "shard", [(i, partner(i, hop, peers, 1)) for i in range(peers)])


def sent_across(value, hop, peers, groups, by):
    pairs = [
        (g * peers + i, (g + by) % groups * peers + partner(i, hop, peers, 1))
        for g in range(groups)
        for i in range(peers)
    ]
    return lax.ppermute(value, ("group", "shard"), pairs)


def sent_group(value, bit, groups):
    return lax.ppermute(value, "group", [(g, g ^ bit) for g in range(groups)])


def relation_sum(kept, sent, peers, groups, chip):
    chips = peers // 2
    half = kept[0].shape[0]
    other_core = (0, 1)
    sent = [sent_on(b, other_core, peers) for b in sent]
    mine = added(kept, sent)
    terms = [mine[0]] + [sent_group(mine[j], j, groups) for j in range(1, groups)]
    ahead = (chip + jnp.arange(chips, dtype=I32)) % chips
    behind = (chip - jnp.arange(chips, dtype=I32)) % chips
    pieces = cut_pieces(ahead, terms)
    pieces = [pieces[0]] + [sent_on(pieces[k], (k, 0), peers) for k in range(1, chips)]
    piece = sum_pieces(pieces)
    pieces = [piece] + [sent_on(piece, (k, 0), peers) for k in range(1, chips)]
    block = join_pieces(behind, pieces, half)
    blocks = [block] + [sent_group(block, j, groups) for j in range(1, groups)]
    return blocks + [sent_on(b, other_core, peers) for b in blocks]


def on_device(
    entity, entity_state, relation, relation_state, src_send, dst_send,
    edge_source, edge_relation, edge_target, neg_slots, edge_count,
):
    rows, _ = entity.shape
    relations = relation.shape[0]
    peers, block = src_send.shape[1:]
    groups = lax.axis_size("group")
    group = lax.axis_index("group").astype(I32)
    me = lax.axis_index("shard").astype(I32)
    width = pl.cdiv(relations, groups * LANES) * LANES
    entity_t, relation_t = entity.T, relation.T
    ways = hops(peers)
    order = jnp.stack([partner(me, hop, peers, 1) for hop in ways])
    here = jnp.stack([group, me % 2])

    def placed(slots):
        return places_of(me, slots // block, peers) * block + slots % block

    edge_source, edge_target = placed(edge_source), placed(edge_target)
    early = peers // 2
    sources = pick_blocks(order[:2], entity_t, src_send[0])
    sources += pick_blocks(order[2:], entity_t, src_send[0])
    sources = [
        sent_on(value, hop, peers) if hop != (0, 0) else value
        for value, hop in zip(sources, ways)
    ]
    targets = pick_blocks(order, entity_t, dst_send[0])
    targets = [sent_across(value, hop, peers, groups, -1) for value, hop in zip(targets, ways)]
    rels = relation_rows(relation_t, edge_relation.reshape(1, -1))
    counts = slot_counts(placed(neg_slots), peers * block)
    source_hots = home_hots(order, src_send[0], rows)
    target_hots = home_hots(order, dst_send[0], rows)
    heads, query_columns, query_lines = query_rows(sources, edge_source.reshape(1, -1), rels)
    loss, grad, table = score_spans(
        edge_count, targets, query_lines, counts, edge_target.reshape(-1, 1)
    )
    back = [(-hop[0], hop[1]) for hop in ways]
    source_lines, relation_lines = edge_grads(table, grad, heads, rels)
    edge_source = edge_source.reshape(-1, 1)
    source_parts = source_grads(source_lines, edge_source, block, 0, early)
    source_parts += source_grads(source_lines, edge_source, block, early, peers - early)
    returned = []
    for value, hop, way in zip(source_parts, back, ways):
        returned.append(sent_on(value, hop, peers) if way != (0, 0) else value)
    halves = relation_grads(here, relation_lines, edge_relation.reshape(-1, 1), groups, width)
    parts = relation_sum(halves[:groups], halves[groups:], peers, groups, me // 2)
    relation_new = relation_update(here, relation_t, relation_state.reshape(1, -1), parts)
    table_parts = table_grads(query_columns, grad, block, 0, peers)
    home = []
    for value, hop, way in zip(table_parts, back, ways):
        home.append(sent_across(value, hop, peers, groups, 1))
    source_part, entity_t = source_home(source_hots, entity_t, returned)
    entity_new = entity_update(
        target_hots, home, source_part, entity_t, entity_state.reshape(1, -1)
    )
    return entity_new.T, relation_new.T, loss.reshape(-1)


def solution(mesh):
    both = ("group", "shard")
    return jax.shard_map(
        on_device,
        mesh=mesh,
        in_specs=(
            P(both, None), P(both), P(), P(), P(both, None, None), P(both, None, None),
            P(both), P(both), P(both), P(both, None), P(both),
        ),
        out_specs=(P(both, None), P(), P(both)),
        check_vma=False,
    )
```

```python
import functools
import math

import jax
import jax.numpy as jnp
from jax import lax
from jax.experimental import pallas as pl
from jax.experimental.pallas import tpu as pltpu
from jax.sharding import PartitionSpec as P


SPAN = 512
LANES = 128
CHUNK = 256
WIDE = 512


learn_rate = 0.5

F32, BF16, I32 = jnp.float32, jnp.bfloat16, jnp.int32
VMEM = pl.BlockSpec(memory_space=pltpu.VMEM)
SMEM = pl.BlockSpec(memory_space=pltpu.SMEM)
VMEM_LIMIT = 24 << 20


def kernel_call(kernel, outs, flops, moved, **kw):
    semantics = ("arbitrary",) if "grid" in kw else None
    return pl.pallas_call(
        kernel,
        out_shape=outs,
        compiler_params=pltpu.CompilerParams(
            vmem_limit_bytes=VMEM_LIMIT, dimension_semantics=semantics
        ),
        cost_estimate=pl.CostEstimate(flops=flops, bytes_accessed=moved, transcendentals=0),
        **kw,
    )


def shape(dims, dtype=F32):
    return jax.ShapeDtypeStruct(dims, dtype)


def held(dims):
    return pl.BlockSpec(dims, lambda i: (0,) * len(dims))


def split2(x):
    hi = x.astype(BF16)
    return hi, (x - hi.astype(F32)).astype(BF16)


def split3(x):
    hi = x.astype(BF16)
    rest = x - hi.astype(F32)
    mid = rest.astype(BF16)
    return hi, mid, (rest - mid.astype(F32)).astype(BF16)


def dot(a, b):
    return jnp.dot(a, b, preferred_element_type=F32)


def dot_nt(a, b):
    return lax.dot_general(a, b, (((1,), (1,)), ((), ())), preferred_element_type=F32)


def one_hot(mask):
    return jnp.where(mask, 1.0, 0.0).astype(BF16)


def rows_hot(length, slots):
    return one_hot(lax.broadcasted_iota(I32, (length, slots.shape[1]), 0) == slots)


def columns_hot(slots, length):
    return one_hot(lax.broadcasted_iota(I32, (slots.shape[0], length), 1) == slots)


def complex_product(a, b):
    half = a.shape[0] // 2
    ar, ai, br, bi = a[:half], a[half:], b[:half], b[half:]
    return jnp.concatenate([ar * br - ai * bi, ar * bi + ai * br], axis=0)


def conj_product(a, b):
    half = a.shape[0] // 2
    ar, ai, br, bi = a[:half], a[half:], b[:half], b[half:]
    return jnp.concatenate([ar * br + ai * bi, ai * br - ar * bi], axis=0)


def hops(peers):
    chips = peers // 2
    ahead = [(k, b) for k in range(1, chips) for b in (0, 1)]
    return ahead + [(0, 1), (0, 0)]


def partner(me, hop, peers, sign):
    chips = peers // 2
    return (me // 2 + sign * hop[0]) % chips * 2 + (me % 2 + hop[1]) % 2


def places_of(me, owner, peers):
    chips = peers // 2
    k = (me // 2 - owner // 2) % chips
    b = (me + owner) % 2
    return (k - 1) % chips * 2 + jnp.where(k == 0, 1 - b, b)


def pick_kernel(order_ref, rows_ref, slots_ref, *outs):
    hi, mid, lo = split3(rows_ref[...])
    block = slots_ref.shape[1]
    together = max(1, CHUNK // block)
    for first in range(0, len(outs), together):
        group = outs[first:first + together]
        slots = [slots_ref[pl.ds(order_ref[first + i], 1), :] for i in range(len(group))]
        hot = rows_hot(rows_ref.shape[1], jnp.concatenate(slots, axis=1))
        picked = dot(hi, hot) + dot(mid, hot) + dot(lo, hot)
        for i, out in enumerate(group):
            out[...] = picked[:, i * block:(i + 1) * block]


def pick_blocks(order, rows, slots):
    features, length = rows.shape
    block = slots.shape[1]
    count = order.shape[0]
    return kernel_call(
        pick_kernel, [shape((features, block))] * count,
        6 * features * length * count * block, 8 * features * count * block,
        in_specs=[SMEM, VMEM, VMEM], out_specs=[VMEM] * count,
    )(order, rows, slots)


def relation_kernel(rel_ref, edge_rel_ref, out_ref, pieces):
    count = rel_ref.shape[1]
    padded = pieces.shape[2]

    @pl.when(pl.program_id(0) == 0)
    def _():
        features = rel_ref.shape[0]
        tail = padded - count // LANES * LANES
        for piece, value in enumerate(split3(rel_ref[...])):
            pieces[piece, :, padded - tail:] = jnp.zeros((features, tail), BF16)
            pieces[piece, :, :count] = value

    hot = rows_hot(padded, edge_rel_ref[...])
    out_ref[...] = dot(pieces[0], hot) + dot(pieces[1], hot) + dot(pieces[2], hot)


def relation_rows(relation, edge_relation):
    features, count = relation.shape
    edges = edge_relation.shape[1]
    padded = pl.cdiv(count, LANES) * LANES
    return kernel_call(
        relation_kernel, shape((features, edges)),
        6 * features * padded * edges, 8 * features * edges,
        grid=(edges // CHUNK,),
        in_specs=[held((features, count)), pl.BlockSpec((1, CHUNK), lambda i: (0, i))],
        out_specs=pl.BlockSpec((features, CHUNK), lambda i: (0, i)),
        scratch_shapes=[pltpu.VMEM((3, features, padded), BF16)],
    )(relation, edge_relation)


def count_kernel(slots_ref, out_ref):
    table_rows = out_ref.shape[2]
    hits = lax.broadcasted_iota(I32, (slots_ref.shape[1], table_rows), 1) == slots_ref[0]
    counts = jnp.sum(jnp.where(hits, 1.0, 0.0), axis=0, keepdims=True)
    out_ref[0] = jnp.where(counts > 0.0, jnp.log(jnp.maximum(counts, 1.0)), -jnp.inf)


def slot_counts(neg_slots, table_rows):
    spans, negatives = neg_slots.shape
    return kernel_call(
        count_kernel, shape((spans, 1, table_rows)),
        2 * spans * negatives * table_rows, 512 * spans * negatives,
        grid=(spans,),
        in_specs=[pl.BlockSpec((1, negatives, 1), lambda i: (i, 0, 0))],
        out_specs=pl.BlockSpec((1, 1, table_rows), lambda i: (i, 0, 0)),
    )(neg_slots[:, :, None])


def hot_kernel(order_ref, slots_ref, out_ref):
    peers, block, _ = slots_ref.shape
    for j in range(peers):
        out_ref[j * block:(j + 1) * block, :] = columns_hot(slots_ref[order_ref[j]], out_ref.shape[1])


def home_hots(order, slots, rows):
    peers, block = slots.shape
    return kernel_call(
        hot_kernel, shape((peers * block, rows), BF16),
        2 * peers * block * rows, 2 * peers * block * rows,
        in_specs=[SMEM, VMEM], out_specs=VMEM,
    )(order, slots[:, :, None])


def query_kernel(*refs):
    edge_source_ref, rels_ref, *blocks = refs[:-4]
    heads_ref, columns_ref, rows_ref, pieces = refs[-4:]
    block = blocks[0].shape[1]

    @pl.when(pl.program_id(0) == 0)
    def _():
        for p, ref in enumerate(blocks):
            for piece, value in enumerate(split3(ref[...])):
                pieces[piece, :, p * block:(p + 1) * block] = value

    hot = rows_hot(pieces.shape[2], edge_source_ref[...])
    heads = dot(pieces[0], hot) + dot(pieces[1], hot) + dot(pieces[2], hot)
    heads_ref[...] = heads
    queries = complex_product(heads, rels_ref[...])
    hi, lo = split2(queries)
    columns_ref[0], columns_ref[1] = hi, lo
    hi, lo = split2(queries.T)
    rows_ref[...] = jnp.concatenate([hi, hi, lo], axis=1)


def query_rows(blocks, edge_source, rels):
    peers = len(blocks)
    features, block = blocks[0].shape
    edges = edge_source.shape[1]
    return kernel_call(
        query_kernel,
        [shape((features, edges)), shape((2, features, edges), BF16), shape((edges, 3 * features), BF16)],
        6 * features * peers * block * edges, 20 * features * edges,
        grid=(edges // CHUNK,),
        in_specs=[
            pl.BlockSpec((1, CHUNK), lambda i: (0, i)),
            pl.BlockSpec((features, CHUNK), lambda i: (0, i)),
        ] + [held((features, block))] * peers,
        out_specs=[
            pl.BlockSpec((features, CHUNK), lambda i: (0, i)),
            pl.BlockSpec((2, features, CHUNK), lambda i: (0, 0, i)),
            pl.BlockSpec((CHUNK, 3 * features), lambda i: (i, 0)),
        ],
        scratch_shapes=[pltpu.VMEM((3, features, peers * block), BF16)],
    )(edge_source, rels, *blocks)


def softmax_step(step, live, score, log_counts, edge_target, loss_ref, grad_ref):
    own = lax.broadcasted_iota(I32, score.shape, 1) == edge_target
    pos = jnp.sum(jnp.where(own, score, 0.0), axis=1, keepdims=True)
    score = score + log_counts
    peak = jnp.maximum(pos, jnp.max(score, axis=1, keepdims=True))
    weight = jnp.exp(score - peak)
    pos_weight = jnp.exp(pos - peak)
    sum_all = pos_weight + jnp.sum(weight, axis=1, keepdims=True)
    edge = step * score.shape[0] + lax.broadcasted_iota(I32, pos.shape, 0)
    is_live = jnp.where(edge < live, 1.0, 0.0)
    loss = (peak - pos + jnp.log(sum_all)) * is_live
    loss_ref[...] = jnp.broadcast_to(loss, (loss.shape[0], LANES)).T[:1]
    scale = is_live / sum_all
    pos_grad = pos_weight * scale - is_live
    grad = weight * scale + jnp.where(own, pos_grad, 0.0)
    grad_ref[0], grad_ref[1] = split2(grad)


def score_kernel(peers, *refs):
    live_ref, rows_ref, counts_ref, edge_target_ref = refs[:4]
    blocks = refs[4:4 + peers]
    loss_ref, grad_ref, table_ref, scores = refs[4 + peers:]
    features, block = blocks[0].shape
    step = pl.program_id(0)
    last = pl.num_programs(0) - 1

    @pl.when(step == 0)
    def _():
        for p, ref in enumerate(blocks):
            hi, lo = split2(ref[...])
            at = pl.ds(p * block, block)
            table_ref[:features, at] = hi
            table_ref[features:2 * features, at] = lo
            table_ref[2 * features:, at] = hi

    def multiply():
        scores[step % 2] = dot(rows_ref[...], table_ref[...])

    def finish():
        softmax_step(
            step - 1, live_ref[0], scores[(step + 1) % 2], counts_ref[0], edge_target_ref[...],
            loss_ref, grad_ref,
        )

    @pl.when(step == 0)
    def _():
        multiply()

    @pl.when((step > 0) & (step < last))
    def _():
        multiply()
        finish()

    @pl.when(step == last)
    def _():
        finish()


def score_spans(live, blocks, rows, counts, edge_target):
    peers = len(blocks)
    features, block = blocks[0].shape
    edges = edge_target.shape[0]
    table_rows = peers * block
    chunk = CHUNK
    per_span = SPAN // chunk
    steps = edges // chunk

    def now(i):
        return jnp.minimum(i, steps - 1)

    def before(i):
        return jnp.maximum(i - 1, 0)

    return kernel_call(
        functools.partial(score_kernel, peers),
        [
            shape((1, edges)),
            shape((2, edges, table_rows), BF16),
            shape((3 * features, table_rows), BF16),
        ],
        6 * features * table_rows * edges, 30 * features * edges,
        grid=(steps + 1,),
        in_specs=[
            SMEM,
            pl.BlockSpec((chunk, 3 * features), lambda i: (now(i), 0)),
            pl.BlockSpec((1, 1, table_rows), lambda i: (before(i) // per_span, 0, 0)),
            pl.BlockSpec((chunk, 1), lambda i: (before(i), 0)),
        ] + [held((features, block))] * peers,
        out_specs=[
            pl.BlockSpec((1, chunk), lambda i: (0, before(i))),
            pl.BlockSpec((2, chunk, table_rows), lambda i: (0, before(i), 0)),
            held((3 * features, table_rows)),
        ],
        scratch_shapes=[pltpu.VMEM((2, chunk, table_rows), F32)],
    )(live, rows, counts, edge_target, *blocks)


def table_grad_kernel(columns_ref, grad_ref, *outs):
    step = pl.program_id(0)
    block = outs[0].shape[1]
    result = (
        dot(columns_ref[0], grad_ref[0])
        + dot(columns_ref[0], grad_ref[1])
        + dot(columns_ref[1], grad_ref[0])
    )
    for pair in range(len(outs) // 2):
        @pl.when(step == pair)
        def _():
            outs[2 * pair][...] = result[:, :block]
            outs[2 * pair + 1][...] = result[:, block:]


def table_grads(columns, grad, block, first, count):
    _, features, edges = columns.shape
    return kernel_call(
        table_grad_kernel, [shape((features, block))] * count,
        6 * features * count * block * edges, 4 * edges * (features + count * block),
        grid=(count // 2,),
        in_specs=[
            held((2, features, edges)),
            pl.BlockSpec((2, edges, 2 * block), lambda i: (0, 0, first // 2 + i)),
        ],
        out_specs=[held((features, block))] * count,
    )(columns, grad)


def relation_grad_kernel(
    steps, me_ref, table_ref, grad_ref, heads_ref, rels_ref, edge_rel_ref, source_ref, *refs
):
    outs, lines, total = refs[:-2], refs[-2], refs[-1]
    groups = len(outs) // 2
    half, width = outs[0].shape
    step = pl.program_id(0)
    features, chunk = heads_ref.shape
    tile = total.shape[2]

    @pl.when(step < steps)
    def _():
        hi, lo = table_ref[:features], table_ref[features:2 * features]
        query_grad = dot_nt(hi, grad_ref[0]) + dot_nt(hi, grad_ref[1]) + dot_nt(lo, grad_ref[0])
        source_ref[0], source_ref[1] = split2(conj_product(query_grad, rels_ref[...]))
        lines[step] = jnp.concatenate(split2(conj_product(query_grad, heads_ref[...])), axis=1)

    @pl.when(step >= steps)
    def _():
        part = None
        for i in range(steps):
            slots = edge_rel_ref[i * chunk:(i + 1) * chunk, :] - (step - steps) * tile
            hot = columns_hot(slots, tile)
            term = dot(lines[i, :, :chunk], hot) + dot(lines[i, :, chunk:], hot)
            part = term if part is None else part + term
        total[step - steps] = part

    @pl.when(step == pl.num_programs(0) - 1)
    def _():
        group, core = me_ref[0], me_ref[1]
        for j in range(groups):
            for at in range(0, width, LANES):
                start = (group ^ j) * width + at
                rows = total.at[start // tile, :, pl.ds(pl.multiple_of(start % tile, LANES), LANES)]
                outs[j][:, at:at + LANES] = rows[pl.ds(pl.multiple_of(core * half, 8), half), :]
                outs[groups + j][:, at:at + LANES] = rows[
                    pl.ds(pl.multiple_of((1 - core) * half, 8), half), :
                ]


def relation_grads(me, table, grad, heads, rels, edge_relation, groups, width):
    features, edges = heads.shape
    table_rows = table.shape[1]
    chunk = CHUNK
    steps = edges // chunk
    tile = math.gcd(groups * width, WIDE)
    tiles = groups * width // tile

    def now(i):
        return jnp.minimum(i, steps - 1)

    return kernel_call(
        functools.partial(relation_grad_kernel, steps),
        [shape((2, features, edges), BF16)] + [shape((features // 2, width))] * (2 * groups),
        10 * features * table_rows * edges, 30 * features * edges,
        grid=(steps + tiles,),
        in_specs=[
            SMEM,
            held((3 * features, table_rows)),
            pl.BlockSpec((2, chunk, table_rows), lambda i: (0, now(i), 0)),
            pl.BlockSpec((features, chunk), lambda i: (0, now(i))),
            pl.BlockSpec((features, chunk), lambda i: (0, now(i))),
            held((edges, 1)),
        ],
        out_specs=[pl.BlockSpec((2, features, chunk), lambda i: (0, 0, now(i)))]
        + [held((features // 2, width))] * (2 * groups),
        scratch_shapes=[
            pltpu.VMEM((steps, features, 2 * chunk), BF16),
            pltpu.VMEM((tiles, features, tile), F32),
        ],
    )(me, table, grad, heads, rels, edge_relation)


def source_grad_kernel(first, rows_ref, edge_source_ref, *outs):
    step = pl.program_id(0)
    block = outs[0].shape[1]
    hot = columns_hot(edge_source_ref[...] - (first * block + step * 2 * block), 2 * block)
    result = dot(rows_ref[0], hot) + dot(rows_ref[1], hot)
    for pair in range(len(outs) // 2):
        @pl.when(step == pair)
        def _():
            outs[2 * pair][...] = result[:, :block]
            outs[2 * pair + 1][...] = result[:, block:]


def source_grads(rows, edge_source, block, first, count):
    _, features, edges = rows.shape
    return kernel_call(
        functools.partial(source_grad_kernel, first), [shape((features, block))] * count,
        4 * features * count * block * edges, 4 * features * (edges + count * block),
        grid=(count // 2,),
        in_specs=[held((2, features, edges)), held((edges, 1))],
        out_specs=[held((features, block))] * count,
    )(rows, edge_source)


def put_back(blocks, hot):
    hi, lo = split2(jnp.concatenate([ref[...] for ref in blocks], axis=1))
    return dot(hi, hot) + dot(lo, hot)


def target_home_kernel(hot_ref, source_hot_ref, own_ref, entity_ref, *refs):
    blocks, out_ref, entity_out_ref = refs[:-2], refs[-2], refs[-1]
    block = own_ref.shape[1]
    own_hot = source_hot_ref[source_hot_ref.shape[0] - block:, :]
    out_ref[...] = put_back(blocks, hot_ref[...]) + put_back([own_ref], own_hot)
    entity_out_ref[...] = entity_ref[...]


def target_home(hots, source_hots, own, entity, blocks):
    features, rows = entity.shape
    return kernel_call(
        target_home_kernel, [shape((features, rows))] * 2,
        4 * features * rows * hots.shape[0], 8 * features * hots.shape[0],
        in_specs=[VMEM] * (4 + len(blocks)), out_specs=[VMEM] * 2,
    )(hots, source_hots, own, entity, *blocks)


def adagrad(params, state, gradient):
    new_state = state + jnp.mean(gradient * gradient, axis=0, keepdims=True)
    return params - gradient * (learn_rate / jnp.sqrt(new_state))


def entity_kernel(other_ref, entity_ref, state_ref, hot_ref, *refs):
    blocks = refs[:-1]
    here = len(blocks) * blocks[0].shape[1]
    gradient = other_ref[...] + put_back(blocks, hot_ref[:here, :])
    refs[-1][...] = adagrad(entity_ref[...], state_ref[...], gradient)


def entity_update(hots, blocks, other, entity, state):
    features, rows = entity.shape
    return kernel_call(
        entity_kernel, shape((features, rows)),
        4 * features * rows * hots.shape[0], 8 * features * hots.shape[0],
        in_specs=[VMEM] * (4 + len(blocks)), out_specs=VMEM,
    )(other, entity, state, hots, *blocks)


def add_kernel(*refs):
    count = len(refs) // 3
    for i in range(count):
        refs[2 * count + i][...] = refs[i][...] + refs[count + i][...]


def added(ours, theirs):
    count = len(ours)
    dims = ours[0].shape
    return kernel_call(
        add_kernel, [shape(dims)] * count,
        count * dims[0] * dims[1], 12 * count * dims[0] * dims[1],
        in_specs=[VMEM] * (2 * count), out_specs=[VMEM] * count,
    )(*ours, *theirs)


def cut_kernel(me_ref, *refs):
    chips = me_ref.shape[0]
    terms, outs, whole = refs[:-1 - chips], refs[-1 - chips:-1], refs[-1]
    rows, width = outs[0].shape
    have = terms[0].shape[0]
    total = terms[0][...]
    for term in terms[1:]:
        total = total + term[...]
    whole[:have, :] = total
    if have < chips * rows:
        whole[have:, :] = jnp.zeros((chips * rows - have, width), F32)
    for k, out in enumerate(outs):
        out[...] = whole[pl.ds(pl.multiple_of(me_ref[k] * rows, 8), rows), :]


def cut_pieces(order, terms):
    chips = order.shape[0]
    half, width = terms[0].shape
    rows = pl.cdiv(half, 8 * chips) * 8
    return kernel_call(
        cut_kernel, [shape((rows, width))] * chips,
        len(terms) * half * width, 4 * (len(terms) + 1) * half * width,
        in_specs=[SMEM] + [VMEM] * len(terms), out_specs=[VMEM] * chips,
        scratch_shapes=[pltpu.VMEM((chips * rows, width), F32)],
    )(order, *terms)


def sum_kernel(*refs):
    total = refs[0][...]
    for ref in refs[1:-1]:
        total = total + ref[...]
    refs[-1][...] = total


def sum_pieces(pieces):
    rows, width = pieces[0].shape
    return kernel_call(
        sum_kernel, shape((rows, width)),
        len(pieces) * rows * width, 4 * (len(pieces) + 1) * rows * width,
        in_specs=[VMEM] * len(pieces), out_specs=VMEM,
    )(*pieces)


def join_kernel(me_ref, *refs):
    pieces, out_ref, whole = refs[:-2], refs[-2], refs[-1]
    rows = pieces[0].shape[0]
    for k, piece in enumerate(pieces):
        whole[pl.ds(pl.multiple_of(me_ref[k] * rows, 8), rows), :] = piece[...]
    out_ref[...] = whole[:out_ref.shape[0], :]


def join_pieces(order, pieces, half):
    rows, width = pieces[0].shape
    return kernel_call(
        join_kernel, shape((half, width)),
        half * width, 8 * half * width,
        in_specs=[SMEM] + [VMEM] * len(pieces), out_specs=VMEM,
        scratch_shapes=[pltpu.VMEM((len(pieces) * rows, width), F32)],
    )(order, *pieces)


def relation_update_kernel(me_ref, relation_ref, state_ref, *refs):
    parts, out_ref, total = refs[:-2], refs[-2], refs[-1]
    groups = len(parts) // 2
    half, width = parts[0].shape
    group, core = me_ref[0], me_ref[1]
    for j in range(groups):
        at = pl.ds(pl.multiple_of((group ^ j) * width, LANES), width)
        total[pl.ds(pl.multiple_of(core * half, 8), half), at] = parts[j][...]
        total[pl.ds(pl.multiple_of((1 - core) * half, 8), half), at] = parts[groups + j][...]
    gradient = total[:, :out_ref.shape[1]]
    out_ref[...] = adagrad(relation_ref[...], state_ref[...], gradient)


def relation_update(me, relation, state, parts):
    features, count = relation.shape
    _, width = parts[0].shape
    groups = len(parts) // 2
    return kernel_call(
        relation_update_kernel, shape((features, count)),
        8 * features * count, 12 * features * count,
        in_specs=[SMEM] + [VMEM] * (2 + len(parts)), out_specs=VMEM,
        scratch_shapes=[pltpu.VMEM((features, groups * width), F32)],
    )(me, relation, state, *parts)


def sent_on(value, hop, peers):
    return lax.ppermute(value, "shard", [(i, partner(i, hop, peers, 1)) for i in range(peers)])


def sent_across(value, hop, peers, groups, by):
    pairs = [
        (g * peers + i, (g + by) % groups * peers + partner(i, hop, peers, 1))
        for g in range(groups)
        for i in range(peers)
    ]
    return lax.ppermute(value, ("group", "shard"), pairs)


def sent_group(value, bit, groups):
    return lax.ppermute(value, "group", [(g, g ^ bit) for g in range(groups)])


def relation_sum(kept, sent, peers, groups, chip):
    chips = peers // 2
    half = kept[0].shape[0]
    other_core = (0, 1)
    sent = [sent_on(b, other_core, peers) for b in sent]
    mine = added(kept, sent)
    terms = [mine[0]] + [sent_group(mine[j], j, groups) for j in range(1, groups)]
    ahead = (chip + jnp.arange(chips, dtype=I32)) % chips
    behind = (chip - jnp.arange(chips, dtype=I32)) % chips
    pieces = cut_pieces(ahead, terms)
    pieces = [pieces[0]] + [sent_on(pieces[k], (k, 0), peers) for k in range(1, chips)]
    piece = sum_pieces(pieces)
    pieces = [piece] + [sent_on(piece, (k, 0), peers) for k in range(1, chips)]
    block = join_pieces(behind, pieces, half)
    blocks = [block] + [sent_group(block, j, groups) for j in range(1, groups)]
    return blocks + [sent_on(b, other_core, peers) for b in blocks]


def on_device(
    entity, entity_state, relation, relation_state, src_send, dst_send,
    edge_source, edge_relation, edge_target, neg_slots, edge_count,
):
    rows, _ = entity.shape
    relations = relation.shape[0]
    peers, block = src_send.shape[1:]
    groups = lax.axis_size("group")
    group = lax.axis_index("group").astype(I32)
    me = lax.axis_index("shard").astype(I32)
    width = pl.cdiv(relations, groups * LANES) * LANES
    entity_t, relation_t = entity.T, relation.T
    ways = hops(peers)
    order = jnp.stack([partner(me, hop, peers, 1) for hop in ways])
    here = jnp.stack([group, me % 2])

    def placed(slots):
        return places_of(me, slots // block, peers) * block + slots % block

    edge_source, edge_target = placed(edge_source), placed(edge_target)
    early = peers // 2
    sources = pick_blocks(order[:2], entity_t, src_send[0])
    sources += pick_blocks(order[2:], entity_t, src_send[0])
    sources = [
        sent_on(value, hop, peers) if hop != (0, 0) else value
        for value, hop in zip(sources, ways)
    ]
    targets = pick_blocks(order, entity_t, dst_send[0])
    targets = [sent_across(value, hop, peers, groups, -1) for value, hop in zip(targets, ways)]
    rels = relation_rows(relation_t, edge_relation.reshape(1, -1))
    counts = slot_counts(placed(neg_slots), peers * block)
    source_hots = home_hots(order, src_send[0], rows)
    target_hots = home_hots(order, dst_send[0], rows)
    heads, query_columns, query_lines = query_rows(sources, edge_source.reshape(1, -1), rels)
    loss, grad, table = score_spans(
        edge_count, targets, query_lines, counts, edge_target.reshape(-1, 1)
    )
    table_parts = table_grads(query_columns, grad, block, 0, early)
    table_parts += table_grads(query_columns, grad, block, early, peers - early)
    back = [(-hop[0], hop[1]) for hop in ways]
    home = []
    for value, hop in zip(table_parts, back):
        home.append(sent_across(value, hop, peers, groups, 1))
    source_lines, *halves = relation_grads(
        here, table, grad, heads, rels, edge_relation.reshape(-1, 1), groups, width
    )
    edge_source = edge_source.reshape(-1, 1)
    source_parts = source_grads(source_lines, edge_source, block, 0, 2)
    source_parts += source_grads(source_lines, edge_source, block, 2, peers - 2)
    returned = []
    for value, hop, way in zip(source_parts, back, ways):
        returned.append(sent_on(value, hop, peers) if way != (0, 0) else value)
    parts = relation_sum(halves[:groups], halves[groups:], peers, groups, me // 2)
    relation_new = relation_update(here, relation_t, relation_state.reshape(1, -1), parts)
    target_part, entity_t = target_home(target_hots, source_hots, returned[-1], entity_t, home)
    entity_new = entity_update(
        source_hots, returned[:-1], target_part, entity_t, entity_state.reshape(1, -1)
    )
    return entity_new.T, relation_new.T, loss.reshape(-1)


def solution(mesh):
    both = ("group", "shard")
    return jax.shard_map(
        on_device,
        mesh=mesh,
        in_specs=(
            P(both, None), P(both), P(), P(), P(both, None, None), P(both, None, None),
            P(both), P(both), P(both), P(both, None), P(both),
        ),
        out_specs=(P(both, None), P(), P(both)),
        check_vma=False,
    )
```

```python
import functools
import math

import jax
import jax.numpy as jnp
from jax import lax
from jax.experimental import pallas as pl
from jax.experimental.pallas import tpu as pltpu
from jax.sharding import PartitionSpec as P


SPAN = 512
LANES = 128
CHUNK = 256
WIDE = 512


learn_rate = 0.5

F32, BF16, I32 = jnp.float32, jnp.bfloat16, jnp.int32
VMEM = pl.BlockSpec(memory_space=pltpu.VMEM)
SMEM = pl.BlockSpec(memory_space=pltpu.SMEM)
VMEM_LIMIT = 24 << 20


def kernel_call(kernel, outs, flops, moved, **kw):
    semantics = ("arbitrary",) if "grid" in kw else None
    return pl.pallas_call(
        kernel,
        out_shape=outs,
        compiler_params=pltpu.CompilerParams(
            vmem_limit_bytes=VMEM_LIMIT, dimension_semantics=semantics
        ),
        cost_estimate=pl.CostEstimate(flops=flops, bytes_accessed=moved, transcendentals=0),
        **kw,
    )


def shape(dims, dtype=F32):
    return jax.ShapeDtypeStruct(dims, dtype)


def held(dims):
    return pl.BlockSpec(dims, lambda i: (0,) * len(dims))


def split2(x):
    hi = x.astype(BF16)
    return hi, (x - hi.astype(F32)).astype(BF16)


def split3(x):
    hi = x.astype(BF16)
    rest = x - hi.astype(F32)
    mid = rest.astype(BF16)
    return hi, mid, (rest - mid.astype(F32)).astype(BF16)


def dot(a, b):
    return jnp.dot(a, b, preferred_element_type=F32)


def dot_nt(a, b):
    return lax.dot_general(a, b, (((1,), (1,)), ((), ())), preferred_element_type=F32)


def one_hot(mask):
    return jnp.where(mask, 1.0, 0.0).astype(BF16)


def rows_hot(length, slots):
    return one_hot(lax.broadcasted_iota(I32, (length, slots.shape[1]), 0) == slots)


def columns_hot(slots, length):
    return one_hot(lax.broadcasted_iota(I32, (slots.shape[0], length), 1) == slots)


def complex_product(a, b):
    half = a.shape[0] // 2
    ar, ai, br, bi = a[:half], a[half:], b[:half], b[half:]
    return jnp.concatenate([ar * br - ai * bi, ar * bi + ai * br], axis=0)


def conj_product(a, b):
    half = a.shape[0] // 2
    ar, ai, br, bi = a[:half], a[half:], b[:half], b[half:]
    return jnp.concatenate([ar * br + ai * bi, ai * br - ar * bi], axis=0)


def hops(peers):
    chips = peers // 2
    ahead = [(k, b) for k in range(1, chips) for b in (0, 1)]
    return ahead + [(0, 1), (0, 0)]


def partner(me, hop, peers, sign):
    chips = peers // 2
    return (me // 2 + sign * hop[0]) % chips * 2 + (me % 2 + hop[1]) % 2


def places_of(me, owner, peers):
    chips = peers // 2
    k = (me // 2 - owner // 2) % chips
    b = (me + owner) % 2
    return (k - 1) % chips * 2 + jnp.where(k == 0, 1 - b, b)


def pick_kernel(order_ref, rows_ref, slots_ref, *outs):
    hi, mid, lo = split3(rows_ref[...])
    block = slots_ref.shape[1]
    together = max(1, CHUNK // block)
    for first in range(0, len(outs), together):
        group = outs[first:first + together]
        slots = [slots_ref[pl.ds(order_ref[first + i], 1), :] for i in range(len(group))]
        hot = rows_hot(rows_ref.shape[1], jnp.concatenate(slots, axis=1))
        picked = dot(hi, hot) + dot(mid, hot) + dot(lo, hot)
        for i, out in enumerate(group):
            out[...] = picked[:, i * block:(i + 1) * block]


def pick_blocks(order, rows, slots):
    features, length = rows.shape
    block = slots.shape[1]
    count = order.shape[0]
    return kernel_call(
        pick_kernel, [shape((features, block))] * count,
        6 * features * length * count * block, 8 * features * count * block,
        in_specs=[SMEM, VMEM, VMEM], out_specs=[VMEM] * count,
    )(order, rows, slots)


def relation_kernel(rel_ref, edge_rel_ref, out_ref, pieces):
    count = rel_ref.shape[1]
    padded = pieces.shape[2]

    @pl.when(pl.program_id(0) == 0)
    def _():
        features = rel_ref.shape[0]
        tail = padded - count // LANES * LANES
        for piece, value in enumerate(split3(rel_ref[...])):
            pieces[piece, :, padded - tail:] = jnp.zeros((features, tail), BF16)
            pieces[piece, :, :count] = value

    hot = rows_hot(padded, edge_rel_ref[...])
    out_ref[...] = dot(pieces[0], hot) + dot(pieces[1], hot) + dot(pieces[2], hot)


def relation_rows(relation, edge_relation):
    features, count = relation.shape
    edges = edge_relation.shape[1]
    padded = pl.cdiv(count, LANES) * LANES
    return kernel_call(
        relation_kernel, shape((features, edges)),
        6 * features * padded * edges, 8 * features * edges,
        grid=(edges // CHUNK,),
        in_specs=[held((features, count)), pl.BlockSpec((1, CHUNK), lambda i: (0, i))],
        out_specs=pl.BlockSpec((features, CHUNK), lambda i: (0, i)),
        scratch_shapes=[pltpu.VMEM((3, features, padded), BF16)],
    )(relation, edge_relation)


def count_kernel(slots_ref, out_ref):
    table_rows = out_ref.shape[2]
    hits = lax.broadcasted_iota(I32, (slots_ref.shape[1], table_rows), 1) == slots_ref[0]
    counts = jnp.sum(jnp.where(hits, 1.0, 0.0), axis=0, keepdims=True)
    out_ref[0] = jnp.where(counts > 0.0, jnp.log(jnp.maximum(counts, 1.0)), -jnp.inf)


def slot_counts(neg_slots, table_rows):
    spans, negatives = neg_slots.shape
    return kernel_call(
        count_kernel, shape((spans, 1, table_rows)),
        2 * spans * negatives * table_rows, 512 * spans * negatives,
        grid=(spans,),
        in_specs=[pl.BlockSpec((1, negatives, 1), lambda i: (i, 0, 0))],
        out_specs=pl.BlockSpec((1, 1, table_rows), lambda i: (i, 0, 0)),
    )(neg_slots[:, :, None])


def hot_kernel(order_ref, slots_ref, out_ref):
    peers, block, _ = slots_ref.shape
    for j in range(peers):
        out_ref[j * block:(j + 1) * block, :] = columns_hot(slots_ref[order_ref[j]], out_ref.shape[1])


def home_hots(order, slots, rows):
    peers, block = slots.shape
    return kernel_call(
        hot_kernel, shape((peers * block, rows), BF16),
        2 * peers * block * rows, 2 * peers * block * rows,
        in_specs=[SMEM, VMEM], out_specs=VMEM,
    )(order, slots[:, :, None])


def query_kernel(*refs):
    edge_source_ref, rels_ref, *blocks = refs[:-4]
    heads_ref, columns_ref, rows_ref, pieces = refs[-4:]
    block = blocks[0].shape[1]

    @pl.when(pl.program_id(0) == 0)
    def _():
        for p, ref in enumerate(blocks):
            for piece, value in enumerate(split3(ref[...])):
                pieces[piece, :, p * block:(p + 1) * block] = value

    hot = rows_hot(pieces.shape[2], edge_source_ref[...])
    heads = dot(pieces[0], hot) + dot(pieces[1], hot) + dot(pieces[2], hot)
    heads_ref[...] = heads
    queries = complex_product(heads, rels_ref[...])
    hi, lo = split2(queries)
    columns_ref[0], columns_ref[1] = hi, lo
    hi, lo = split2(queries.T)
    rows_ref[...] = jnp.concatenate([hi, hi, lo], axis=1)


def query_rows(blocks, edge_source, rels):
    peers = len(blocks)
    features, block = blocks[0].shape
    edges = edge_source.shape[1]
    return kernel_call(
        query_kernel,
        [shape((features, edges)), shape((2, features, edges), BF16), shape((edges, 3 * features), BF16)],
        6 * features * peers * block * edges, 20 * features * edges,
        grid=(edges // CHUNK,),
        in_specs=[
            pl.BlockSpec((1, CHUNK), lambda i: (0, i)),
            pl.BlockSpec((features, CHUNK), lambda i: (0, i)),
        ] + [held((features, block))] * peers,
        out_specs=[
            pl.BlockSpec((features, CHUNK), lambda i: (0, i)),
            pl.BlockSpec((2, features, CHUNK), lambda i: (0, 0, i)),
            pl.BlockSpec((CHUNK, 3 * features), lambda i: (i, 0)),
        ],
        scratch_shapes=[pltpu.VMEM((3, features, peers * block), BF16)],
    )(edge_source, rels, *blocks)


def softmax_step(step, live, score, log_counts, edge_target, loss_ref, grad_ref):
    own = lax.broadcasted_iota(I32, score.shape, 1) == edge_target
    pos = jnp.sum(jnp.where(own, score, 0.0), axis=1, keepdims=True)
    score = score + log_counts
    peak = jnp.maximum(pos, jnp.max(score, axis=1, keepdims=True))
    weight = jnp.exp(score - peak)
    pos_weight = jnp.exp(pos - peak)
    sum_all = pos_weight + jnp.sum(weight, axis=1, keepdims=True)
    edge = step * score.shape[0] + lax.broadcasted_iota(I32, pos.shape, 0)
    is_live = jnp.where(edge < live, 1.0, 0.0)
    loss_ref[...] = (peak - pos + jnp.log(sum_all)) * is_live
    scale = is_live / sum_all
    pos_grad = pos_weight * scale - is_live
    grad = weight * scale + jnp.where(own, pos_grad, 0.0)
    grad_ref[0], grad_ref[1] = split2(grad)


def score_kernel(peers, *refs):
    live_ref, rows_ref, counts_ref, edge_target_ref = refs[:4]
    blocks = refs[4:4 + peers]
    loss_ref, grad_ref, table_ref, scores = refs[4 + peers:]
    features, block = blocks[0].shape
    step = pl.program_id(0)
    last = pl.num_programs(0) - 1

    @pl.when(step == 0)
    def _():
        for p, ref in enumerate(blocks):
            hi, lo = split2(ref[...])
            at = pl.ds(p * block, block)
            table_ref[:features, at] = hi
            table_ref[features:2 * features, at] = lo
            table_ref[2 * features:, at] = hi

    def multiply():
        scores[step % 2] = dot(rows_ref[...], table_ref[...])

    def finish():
        softmax_step(
            step - 1, live_ref[0], scores[(step + 1) % 2], counts_ref[0], edge_target_ref[...],
            loss_ref, grad_ref,
        )

    @pl.when(step == 0)
    def _():
        multiply()

    @pl.when((step > 0) & (step < last))
    def _():
        multiply()
        finish()

    @pl.when(step == last)
    def _():
        finish()


def score_spans(live, blocks, rows, counts, edge_target):
    peers = len(blocks)
    features, block = blocks[0].shape
    edges = edge_target.shape[0]
    table_rows = peers * block
    chunk = CHUNK
    per_span = SPAN // chunk
    steps = edges // chunk

    def now(i):
        return jnp.minimum(i, steps - 1)

    def before(i):
        return jnp.maximum(i - 1, 0)

    return kernel_call(
        functools.partial(score_kernel, peers),
        [
            shape((edges, 1)),
            shape((2, edges, table_rows), BF16),
            shape((3 * features, table_rows), BF16),
        ],
        6 * features * table_rows * edges, 30 * features * edges,
        grid=(steps + 1,),
        in_specs=[
            SMEM,
            pl.BlockSpec((chunk, 3 * features), lambda i: (now(i), 0)),
            pl.BlockSpec((1, 1, table_rows), lambda i: (before(i) // per_span, 0, 0)),
            pl.BlockSpec((chunk, 1), lambda i: (before(i), 0)),
        ] + [held((features, block))] * peers,
        out_specs=[
            pl.BlockSpec((chunk, 1), lambda i: (before(i), 0)),
            pl.BlockSpec((2, chunk, table_rows), lambda i: (0, before(i), 0)),
            held((3 * features, table_rows)),
        ],
        scratch_shapes=[pltpu.VMEM((2, chunk, table_rows), F32)],
    )(live, rows, counts, edge_target, *blocks)


def loss_row_kernel(loss_ref, out_ref):
    edges = loss_ref.shape[0]
    out_ref[...] = jnp.broadcast_to(loss_ref[...], (edges, LANES)).T[:1]


def loss_row(loss):
    edges = loss.shape[0]
    return kernel_call(
        loss_row_kernel, shape((1, edges)), edges * LANES, 4 * edges * LANES,
        in_specs=[VMEM], out_specs=VMEM,
    )(loss)


def table_grad_kernel(columns_ref, grad_ref, *outs):
    step = pl.program_id(0)
    block = outs[0].shape[1]
    result = (
        dot(columns_ref[0], grad_ref[0])
        + dot(columns_ref[0], grad_ref[1])
        + dot(columns_ref[1], grad_ref[0])
    )
    for pair in range(len(outs) // 2):
        @pl.when(step == pair)
        def _():
            outs[2 * pair][...] = result[:, :block]
            outs[2 * pair + 1][...] = result[:, block:]


def table_grads(columns, grad, block, first, count):
    _, features, edges = columns.shape
    return kernel_call(
        table_grad_kernel, [shape((features, block))] * count,
        6 * features * count * block * edges, 4 * edges * (features + count * block),
        grid=(count // 2,),
        in_specs=[
            held((2, features, edges)),
            pl.BlockSpec((2, edges, 2 * block), lambda i: (0, 0, first // 2 + i)),
        ],
        out_specs=[held((features, block))] * count,
    )(columns, grad)


def relation_grad_kernel(
    steps, me_ref, table_ref, grad_ref, heads_ref, rels_ref, edge_rel_ref, source_ref, *refs
):
    outs, lines, total = refs[:-2], refs[-2], refs[-1]
    groups = len(outs) // 2
    half, width = outs[0].shape
    step = pl.program_id(0)
    features, chunk = heads_ref.shape
    tile = total.shape[2]

    @pl.when(step < steps)
    def _():
        hi, lo = table_ref[:features], table_ref[features:2 * features]
        query_grad = dot_nt(hi, grad_ref[0]) + dot_nt(hi, grad_ref[1]) + dot_nt(lo, grad_ref[0])
        source_ref[0], source_ref[1] = split2(conj_product(query_grad, rels_ref[...]))
        lines[step] = jnp.concatenate(split2(conj_product(query_grad, heads_ref[...])), axis=1)

    @pl.when(step >= steps)
    def _():
        part = None
        for i in range(steps):
            slots = edge_rel_ref[i * chunk:(i + 1) * chunk, :] - (step - steps) * tile
            hot = columns_hot(slots, tile)
            term = dot(lines[i, :, :chunk], hot) + dot(lines[i, :, chunk:], hot)
            part = term if part is None else part + term
        total[step - steps] = part

    @pl.when(step == pl.num_programs(0) - 1)
    def _():
        group, core = me_ref[0], me_ref[1]
        for j in range(groups):
            for at in range(0, width, LANES):
                start = (group ^ j) * width + at
                rows = total.at[start // tile, :, pl.ds(pl.multiple_of(start % tile, LANES), LANES)]
                outs[j][:, at:at + LANES] = rows[pl.ds(pl.multiple_of(core * half, 8), half), :]
                outs[groups + j][:, at:at + LANES] = rows[
                    pl.ds(pl.multiple_of((1 - core) * half, 8), half), :
                ]


def relation_grads(me, table, grad, heads, rels, edge_relation, groups, width):
    features, edges = heads.shape
    table_rows = table.shape[1]
    chunk = CHUNK
    steps = edges // chunk
    tile = math.gcd(groups * width, WIDE)
    tiles = groups * width // tile

    def now(i):
        return jnp.minimum(i, steps - 1)

    return kernel_call(
        functools.partial(relation_grad_kernel, steps),
        [shape((2, features, edges), BF16)] + [shape((features // 2, width))] * (2 * groups),
        10 * features * table_rows * edges, 30 * features * edges,
        grid=(steps + tiles,),
        in_specs=[
            SMEM,
            held((3 * features, table_rows)),
            pl.BlockSpec((2, chunk, table_rows), lambda i: (0, now(i), 0)),
            pl.BlockSpec((features, chunk), lambda i: (0, now(i))),
            pl.BlockSpec((features, chunk), lambda i: (0, now(i))),
            held((edges, 1)),
        ],
        out_specs=[pl.BlockSpec((2, features, chunk), lambda i: (0, 0, now(i)))]
        + [held((features // 2, width))] * (2 * groups),
        scratch_shapes=[
            pltpu.VMEM((steps, features, 2 * chunk), BF16),
            pltpu.VMEM((tiles, features, tile), F32),
        ],
    )(me, table, grad, heads, rels, edge_relation)


def source_grad_kernel(first, rows_ref, edge_source_ref, *outs):
    step = pl.program_id(0)
    block = outs[0].shape[1]
    hot = columns_hot(edge_source_ref[...] - (first * block + step * 2 * block), 2 * block)
    result = dot(rows_ref[0], hot) + dot(rows_ref[1], hot)
    for pair in range(len(outs) // 2):
        @pl.when(step == pair)
        def _():
            outs[2 * pair][...] = result[:, :block]
            outs[2 * pair + 1][...] = result[:, block:]


def source_grads(rows, edge_source, block, first, count):
    _, features, edges = rows.shape
    return kernel_call(
        functools.partial(source_grad_kernel, first), [shape((features, block))] * count,
        4 * features * count * block * edges, 4 * features * (edges + count * block),
        grid=(count // 2,),
        in_specs=[held((2, features, edges)), held((edges, 1))],
        out_specs=[held((features, block))] * count,
    )(rows, edge_source)


def put_back(blocks, hot):
    hi, lo = split2(jnp.concatenate([ref[...] for ref in blocks], axis=1))
    return dot(hi, hot) + dot(lo, hot)


def target_home_kernel(hot_ref, source_hot_ref, own_ref, entity_ref, *refs):
    blocks, out_ref, entity_out_ref = refs[:-2], refs[-2], refs[-1]
    block = own_ref.shape[1]
    own_hot = source_hot_ref[source_hot_ref.shape[0] - block:, :]
    out_ref[...] = put_back(blocks, hot_ref[...]) + put_back([own_ref], own_hot)
    entity_out_ref[...] = entity_ref[...]


def target_home(hots, source_hots, own, entity, blocks):
    features, rows = entity.shape
    return kernel_call(
        target_home_kernel, [shape((features, rows))] * 2,
        4 * features * rows * hots.shape[0], 8 * features * hots.shape[0],
        in_specs=[VMEM] * (4 + len(blocks)), out_specs=[VMEM] * 2,
    )(hots, source_hots, own, entity, *blocks)


def adagrad(params, state, gradient):
    new_state = state + jnp.mean(gradient * gradient, axis=0, keepdims=True)
    return params - gradient * (learn_rate / jnp.sqrt(new_state))


def entity_kernel(other_ref, entity_ref, state_ref, hot_ref, *refs):
    blocks = refs[:-1]
    here = len(blocks) * blocks[0].shape[1]
    gradient = other_ref[...] + put_back(blocks, hot_ref[:here, :])
    refs[-1][...] = adagrad(entity_ref[...], state_ref[...], gradient)


def entity_update(hots, blocks, other, entity, state):
    features, rows = entity.shape
    return kernel_call(
        entity_kernel, shape((features, rows)),
        4 * features * rows * hots.shape[0], 8 * features * hots.shape[0],
        in_specs=[VMEM] * (4 + len(blocks)), out_specs=VMEM,
    )(other, entity, state, hots, *blocks)


def add_kernel(*refs):
    count = len(refs) // 3
    for i in range(count):
        refs[2 * count + i][...] = refs[i][...] + refs[count + i][...]


def added(ours, theirs):
    count = len(ours)
    dims = ours[0].shape
    return kernel_call(
        add_kernel, [shape(dims)] * count,
        count * dims[0] * dims[1], 12 * count * dims[0] * dims[1],
        in_specs=[VMEM] * (2 * count), out_specs=[VMEM] * count,
    )(*ours, *theirs)


def cut_kernel(me_ref, *refs):
    chips = me_ref.shape[0]
    terms, outs, whole = refs[:-1 - chips], refs[-1 - chips:-1], refs[-1]
    rows, width = outs[0].shape
    have = terms[0].shape[0]
    total = terms[0][...]
    for term in terms[1:]:
        total = total + term[...]
    whole[:have, :] = total
    if have < chips * rows:
        whole[have:, :] = jnp.zeros((chips * rows - have, width), F32)
    for k, out in enumerate(outs):
        out[...] = whole[pl.ds(pl.multiple_of(me_ref[k] * rows, 8), rows), :]


def cut_pieces(order, terms):
    chips = order.shape[0]
    half, width = terms[0].shape
    rows = pl.cdiv(half, 8 * chips) * 8
    return kernel_call(
        cut_kernel, [shape((rows, width))] * chips,
        len(terms) * half * width, 4 * (len(terms) + 1) * half * width,
        in_specs=[SMEM] + [VMEM] * len(terms), out_specs=[VMEM] * chips,
        scratch_shapes=[pltpu.VMEM((chips * rows, width), F32)],
    )(order, *terms)


def sum_kernel(*refs):
    total = refs[0][...]
    for ref in refs[1:-1]:
        total = total + ref[...]
    refs[-1][...] = total


def sum_pieces(pieces):
    rows, width = pieces[0].shape
    return kernel_call(
        sum_kernel, shape((rows, width)),
        len(pieces) * rows * width, 4 * (len(pieces) + 1) * rows * width,
        in_specs=[VMEM] * len(pieces), out_specs=VMEM,
    )(*pieces)


def join_kernel(me_ref, *refs):
    pieces, out_ref, whole = refs[:-2], refs[-2], refs[-1]
    rows = pieces[0].shape[0]
    for k, piece in enumerate(pieces):
        whole[pl.ds(pl.multiple_of(me_ref[k] * rows, 8), rows), :] = piece[...]
    out_ref[...] = whole[:out_ref.shape[0], :]


def join_pieces(order, pieces, half):
    rows, width = pieces[0].shape
    return kernel_call(
        join_kernel, shape((half, width)),
        half * width, 8 * half * width,
        in_specs=[SMEM] + [VMEM] * len(pieces), out_specs=VMEM,
        scratch_shapes=[pltpu.VMEM((len(pieces) * rows, width), F32)],
    )(order, *pieces)


def relation_update_kernel(me_ref, relation_ref, state_ref, *refs):
    parts, out_ref, total = refs[:-2], refs[-2], refs[-1]
    groups = len(parts) // 2
    half, width = parts[0].shape
    group, core = me_ref[0], me_ref[1]
    for j in range(groups):
        at = pl.ds(pl.multiple_of((group ^ j) * width, LANES), width)
        total[pl.ds(pl.multiple_of(core * half, 8), half), at] = parts[j][...]
        total[pl.ds(pl.multiple_of((1 - core) * half, 8), half), at] = parts[groups + j][...]
    gradient = total[:, :out_ref.shape[1]]
    out_ref[...] = adagrad(relation_ref[...], state_ref[...], gradient)


def relation_update(me, relation, state, parts):
    features, count = relation.shape
    _, width = parts[0].shape
    groups = len(parts) // 2
    return kernel_call(
        relation_update_kernel, shape((features, count)),
        8 * features * count, 12 * features * count,
        in_specs=[SMEM] + [VMEM] * (2 + len(parts)), out_specs=VMEM,
        scratch_shapes=[pltpu.VMEM((features, groups * width), F32)],
    )(me, relation, state, *parts)


def sent_on(value, hop, peers):
    return lax.ppermute(value, "shard", [(i, partner(i, hop, peers, 1)) for i in range(peers)])


def sent_across(value, hop, peers, groups, by):
    pairs = [
        (g * peers + i, (g + by) % groups * peers + partner(i, hop, peers, 1))
        for g in range(groups)
        for i in range(peers)
    ]
    return lax.ppermute(value, ("group", "shard"), pairs)


def sent_group(value, bit, groups):
    return lax.ppermute(value, "group", [(g, g ^ bit) for g in range(groups)])


def relation_sum(kept, sent, peers, groups, chip):
    chips = peers // 2
    half = kept[0].shape[0]
    other_core = (0, 1)
    sent = [sent_on(b, other_core, peers) for b in sent]
    mine = added(kept, sent)
    terms = [mine[0]] + [sent_group(mine[j], j, groups) for j in range(1, groups)]
    ahead = (chip + jnp.arange(chips, dtype=I32)) % chips
    behind = (chip - jnp.arange(chips, dtype=I32)) % chips
    pieces = cut_pieces(ahead, terms)
    pieces = [pieces[0]] + [sent_on(pieces[k], (k, 0), peers) for k in range(1, chips)]
    piece = sum_pieces(pieces)
    pieces = [piece] + [sent_on(piece, (k, 0), peers) for k in range(1, chips)]
    block = join_pieces(behind, pieces, half)
    blocks = [block] + [sent_group(block, j, groups) for j in range(1, groups)]
    return blocks + [sent_on(b, other_core, peers) for b in blocks]


def on_device(
    entity, entity_state, relation, relation_state, src_send, dst_send,
    edge_source, edge_relation, edge_target, neg_slots, edge_count,
):
    rows, _ = entity.shape
    relations = relation.shape[0]
    peers, block = src_send.shape[1:]
    groups = lax.axis_size("group")
    group = lax.axis_index("group").astype(I32)
    me = lax.axis_index("shard").astype(I32)
    width = pl.cdiv(relations, groups * LANES) * LANES
    entity_t, relation_t = entity.T, relation.T
    ways = hops(peers)
    order = jnp.stack([partner(me, hop, peers, 1) for hop in ways])
    here = jnp.stack([group, me % 2])

    def placed(slots):
        return places_of(me, slots // block, peers) * block + slots % block

    edge_source, edge_target = placed(edge_source), placed(edge_target)
    early = peers // 2
    sources = pick_blocks(order[:2], entity_t, src_send[0])
    sources += pick_blocks(order[2:], entity_t, src_send[0])
    sources = [
        sent_on(value, hop, peers) if hop != (0, 0) else value
        for value, hop in zip(sources, ways)
    ]
    targets = pick_blocks(order, entity_t, dst_send[0])
    targets = [sent_across(value, hop, peers, groups, -1) for value, hop in zip(targets, ways)]
    rels = relation_rows(relation_t, edge_relation.reshape(1, -1))
    counts = slot_counts(placed(neg_slots), peers * block)
    source_hots = home_hots(order, src_send[0], rows)
    target_hots = home_hots(order, dst_send[0], rows)
    heads, query_columns, query_lines = query_rows(sources, edge_source.reshape(1, -1), rels)
    loss, grad, table = score_spans(
        edge_count, targets, query_lines, counts, edge_target.reshape(-1, 1)
    )
    far = early - 2
    far_parts = table_grads(query_columns, grad, block, far, 2)
    table_parts = table_grads(query_columns, grad, block, 0, far)
    table_parts += far_parts
    table_parts += table_grads(query_columns, grad, block, early, peers - early)
    back = [(-hop[0], hop[1]) for hop in ways]
    home = []
    for value, hop in zip(table_parts, back):
        home.append(sent_across(value, hop, peers, groups, 1))
    source_lines, *halves = relation_grads(
        here, table, grad, heads, rels, edge_relation.reshape(-1, 1), groups, width
    )
    edge_source = edge_source.reshape(-1, 1)
    source_parts = source_grads(source_lines, edge_source, block, 0, 2)
    source_parts += source_grads(source_lines, edge_source, block, 2, peers - 2)
    returned = []
    for value, hop, way in zip(source_parts, back, ways):
        returned.append(sent_on(value, hop, peers) if way != (0, 0) else value)
    parts = relation_sum(halves[:groups], halves[groups:], peers, groups, me // 2)
    relation_new = relation_update(here, relation_t, relation_state.reshape(1, -1), parts)
    target_part, entity_t = target_home(target_hots, source_hots, returned[-1], entity_t, home)
    entity_new = entity_update(
        source_hots, returned[:-1], target_part, entity_t, entity_state.reshape(1, -1)
    )
    return entity_new.T, relation_new.T, loss_row(loss).reshape(-1)


def solution(mesh):
    both = ("group", "shard")
    return jax.shard_map(
        on_device,
        mesh=mesh,
        in_specs=(
            P(both, None), P(both), P(), P(), P(both, None, None), P(both, None, None),
            P(both), P(both), P(both), P(both, None), P(both),
        ),
        out_specs=(P(both, None), P(), P(both)),
        check_vma=False,
    )
```

```python
import functools
import math

import jax
import jax.numpy as jnp
from jax import lax
from jax.experimental import pallas as pl
from jax.experimental.pallas import tpu as pltpu
from jax.sharding import PartitionSpec as P


SPAN = 512
LANES = 128
CHUNK = 256
WIDE = 512


learn_rate = 0.5

F32, BF16, I32 = jnp.float32, jnp.bfloat16, jnp.int32
VMEM = pl.BlockSpec(memory_space=pltpu.VMEM)
SMEM = pl.BlockSpec(memory_space=pltpu.SMEM)
VMEM_LIMIT = 24 << 20


def kernel_call(kernel, outs, flops, moved, **kw):
    semantics = ("arbitrary",) if "grid" in kw else None
    return pl.pallas_call(
        kernel,
        out_shape=outs,
        compiler_params=pltpu.CompilerParams(
            vmem_limit_bytes=VMEM_LIMIT, dimension_semantics=semantics
        ),
        cost_estimate=pl.CostEstimate(flops=flops, bytes_accessed=moved, transcendentals=0),
        **kw,
    )


def shape(dims, dtype=F32):
    return jax.ShapeDtypeStruct(dims, dtype)


def held(dims):
    return pl.BlockSpec(dims, lambda i: (0,) * len(dims))


def split2(x):
    hi = x.astype(BF16)
    return hi, (x - hi.astype(F32)).astype(BF16)


def split3(x):
    hi = x.astype(BF16)
    rest = x - hi.astype(F32)
    mid = rest.astype(BF16)
    return hi, mid, (rest - mid.astype(F32)).astype(BF16)


def dot(a, b):
    return jnp.dot(a, b, preferred_element_type=F32)


def dot_nt(a, b):
    return lax.dot_general(a, b, (((1,), (1,)), ((), ())), preferred_element_type=F32)


def one_hot(mask):
    return jnp.where(mask, 1.0, 0.0).astype(BF16)


def rows_hot(length, slots):
    return one_hot(lax.broadcasted_iota(I32, (length, slots.shape[1]), 0) == slots)


def columns_hot(slots, length):
    return one_hot(lax.broadcasted_iota(I32, (slots.shape[0], length), 1) == slots)


def complex_product(a, b):
    half = a.shape[0] // 2
    ar, ai, br, bi = a[:half], a[half:], b[:half], b[half:]
    return jnp.concatenate([ar * br - ai * bi, ar * bi + ai * br], axis=0)


def conj_product(a, b):
    half = a.shape[0] // 2
    ar, ai, br, bi = a[:half], a[half:], b[:half], b[half:]
    return jnp.concatenate([ar * br + ai * bi, ai * br - ar * bi], axis=0)


def hops(peers):
    chips = peers // 2
    ahead = [(k, b) for k in range(1, chips) for b in (0, 1)]
    return ahead + [(0, 1), (0, 0)]


def partner(me, hop, peers, sign):
    chips = peers // 2
    return (me // 2 + sign * hop[0]) % chips * 2 + (me % 2 + hop[1]) % 2


def places_of(me, owner, peers):
    chips = peers // 2
    k = (me // 2 - owner // 2) % chips
    b = (me + owner) % 2
    return (k - 1) % chips * 2 + jnp.where(k == 0, 1 - b, b)


def pick_kernel(order_ref, rows_ref, slots_ref, *outs):
    hi, mid, lo = split3(rows_ref[...])
    block = slots_ref.shape[1]
    together = max(1, CHUNK // block)
    for first in range(0, len(outs), together):
        group = outs[first:first + together]
        slots = [slots_ref[pl.ds(order_ref[first + i], 1), :] for i in range(len(group))]
        hot = rows_hot(rows_ref.shape[1], jnp.concatenate(slots, axis=1))
        picked = dot(hi, hot) + dot(mid, hot) + dot(lo, hot)
        for i, out in enumerate(group):
            out[...] = picked[:, i * block:(i + 1) * block]


def pick_blocks(order, rows, slots):
    features, length = rows.shape
    block = slots.shape[1]
    count = order.shape[0]
    return kernel_call(
        pick_kernel, [shape((features, block))] * count,
        6 * features * length * count * block, 8 * features * count * block,
        in_specs=[SMEM, VMEM, VMEM], out_specs=[VMEM] * count,
    )(order, rows, slots)


def relation_kernel(rel_ref, edge_rel_ref, out_ref, pieces):
    count = rel_ref.shape[1]
    padded = pieces.shape[2]

    @pl.when(pl.program_id(0) == 0)
    def _():
        features = rel_ref.shape[0]
        tail = padded - count // LANES * LANES
        for piece, value in enumerate(split3(rel_ref[...])):
            pieces[piece, :, padded - tail:] = jnp.zeros((features, tail), BF16)
            pieces[piece, :, :count] = value

    hot = rows_hot(padded, edge_rel_ref[...])
    out_ref[...] = dot(pieces[0], hot) + dot(pieces[1], hot) + dot(pieces[2], hot)


def relation_rows(relation, edge_relation):
    features, count = relation.shape
    edges = edge_relation.shape[1]
    padded = pl.cdiv(count, LANES) * LANES
    return kernel_call(
        relation_kernel, shape((features, edges)),
        6 * features * padded * edges, 8 * features * edges,
        grid=(edges // CHUNK,),
        in_specs=[held((features, count)), pl.BlockSpec((1, CHUNK), lambda i: (0, i))],
        out_specs=pl.BlockSpec((features, CHUNK), lambda i: (0, i)),
        scratch_shapes=[pltpu.VMEM((3, features, padded), BF16)],
    )(relation, edge_relation)


def count_kernel(slots_ref, out_ref):
    table_rows = out_ref.shape[2]
    hits = lax.broadcasted_iota(I32, (slots_ref.shape[1], table_rows), 1) == slots_ref[0]
    counts = jnp.sum(jnp.where(hits, 1.0, 0.0), axis=0, keepdims=True)
    out_ref[0] = jnp.where(counts > 0.0, jnp.log(jnp.maximum(counts, 1.0)), -jnp.inf)


def slot_counts(neg_slots, table_rows):
    spans, negatives = neg_slots.shape
    return kernel_call(
        count_kernel, shape((spans, 1, table_rows)),
        2 * spans * negatives * table_rows, 512 * spans * negatives,
        grid=(spans,),
        in_specs=[pl.BlockSpec((1, negatives, 1), lambda i: (i, 0, 0))],
        out_specs=pl.BlockSpec((1, 1, table_rows), lambda i: (i, 0, 0)),
    )(neg_slots[:, :, None])


def hot_kernel(order_ref, slots_ref, out_ref):
    peers, block, _ = slots_ref.shape
    for j in range(peers):
        out_ref[j * block:(j + 1) * block, :] = columns_hot(slots_ref[order_ref[j]], out_ref.shape[1])


def home_hots(order, slots, rows):
    peers, block = slots.shape
    return kernel_call(
        hot_kernel, shape((peers * block, rows), BF16),
        2 * peers * block * rows, 2 * peers * block * rows,
        in_specs=[SMEM, VMEM], out_specs=VMEM,
    )(order, slots[:, :, None])


def query_kernel(*refs):
    edge_source_ref, rels_ref, *blocks = refs[:-4]
    heads_ref, columns_ref, rows_ref, pieces = refs[-4:]
    block = blocks[0].shape[1]

    @pl.when(pl.program_id(0) == 0)
    def _():
        for p, ref in enumerate(blocks):
            for piece, value in enumerate(split3(ref[...])):
                pieces[piece, :, p * block:(p + 1) * block] = value

    hot = rows_hot(pieces.shape[2], edge_source_ref[...])
    heads = dot(pieces[0], hot) + dot(pieces[1], hot) + dot(pieces[2], hot)
    heads_ref[...] = heads
    queries = complex_product(heads, rels_ref[...])
    hi, lo = split2(queries)
    columns_ref[0], columns_ref[1] = hi, lo
    hi, lo = split2(queries.T)
    rows_ref[...] = jnp.concatenate([hi, hi, lo], axis=1)


def query_rows(blocks, edge_source, rels):
    peers = len(blocks)
    features, block = blocks[0].shape
    edges = edge_source.shape[1]
    return kernel_call(
        query_kernel,
        [shape((features, edges)), shape((2, features, edges), BF16), shape((edges, 3 * features), BF16)],
        6 * features * peers * block * edges, 20 * features * edges,
        grid=(edges // CHUNK,),
        in_specs=[
            pl.BlockSpec((1, CHUNK), lambda i: (0, i)),
            pl.BlockSpec((features, CHUNK), lambda i: (0, i)),
        ] + [held((features, block))] * peers,
        out_specs=[
            pl.BlockSpec((features, CHUNK), lambda i: (0, i)),
            pl.BlockSpec((2, features, CHUNK), lambda i: (0, 0, i)),
            pl.BlockSpec((CHUNK, 3 * features), lambda i: (i, 0)),
        ],
        scratch_shapes=[pltpu.VMEM((3, features, peers * block), BF16)],
    )(edge_source, rels, *blocks)


def softmax_step(step, live, score, log_counts, edge_target, loss_ref, grad_ref):
    own = lax.broadcasted_iota(I32, score.shape, 1) == edge_target
    pos = jnp.sum(jnp.where(own, score, 0.0), axis=1, keepdims=True)
    score = score + log_counts
    peak = jnp.maximum(pos, jnp.max(score, axis=1, keepdims=True))
    weight = jnp.exp(score - peak)
    pos_weight = jnp.exp(pos - peak)
    sum_all = pos_weight + jnp.sum(weight, axis=1, keepdims=True)
    edge = step * score.shape[0] + lax.broadcasted_iota(I32, pos.shape, 0)
    is_live = jnp.where(edge < live, 1.0, 0.0)
    loss_ref[...] = (peak - pos + jnp.log(sum_all)) * is_live
    scale = is_live / sum_all
    pos_grad = pos_weight * scale - is_live
    grad = weight * scale + jnp.where(own, pos_grad, 0.0)
    grad_ref[0], grad_ref[1] = split2(grad)


def score_kernel(peers, *refs):
    live_ref, rows_ref, counts_ref, edge_target_ref = refs[:4]
    blocks = refs[4:4 + peers]
    loss_ref, grad_ref, table_ref, scores = refs[4 + peers:]
    features, block = blocks[0].shape
    step = pl.program_id(0)
    last = pl.num_programs(0) - 1

    @pl.when(step == 0)
    def _():
        for p, ref in enumerate(blocks):
            hi, lo = split2(ref[...])
            at = pl.ds(p * block, block)
            table_ref[:features, at] = hi
            table_ref[features:2 * features, at] = lo
            table_ref[2 * features:, at] = hi

    def multiply():
        scores[step % 2] = dot(rows_ref[...], table_ref[...])

    def finish():
        softmax_step(
            step - 1, live_ref[0], scores[(step + 1) % 2], counts_ref[0], edge_target_ref[...],
            loss_ref, grad_ref,
        )

    @pl.when(step == 0)
    def _():
        multiply()

    @pl.when((step > 0) & (step < last))
    def _():
        multiply()
        finish()

    @pl.when(step == last)
    def _():
        finish()


def score_spans(live, blocks, rows, counts, edge_target):
    peers = len(blocks)
    features, block = blocks[0].shape
    edges = edge_target.shape[0]
    table_rows = peers * block
    chunk = CHUNK
    per_span = SPAN // chunk
    steps = edges // chunk

    def now(i):
        return jnp.minimum(i, steps - 1)

    def before(i):
        return jnp.maximum(i - 1, 0)

    return kernel_call(
        functools.partial(score_kernel, peers),
        [
            shape((edges, 1)),
            shape((2, edges, table_rows), BF16),
            shape((3 * features, table_rows), BF16),
        ],
        6 * features * table_rows * edges, 30 * features * edges,
        grid=(steps + 1,),
        in_specs=[
            SMEM,
            pl.BlockSpec((chunk, 3 * features), lambda i: (now(i), 0)),
            pl.BlockSpec((1, 1, table_rows), lambda i: (before(i) // per_span, 0, 0)),
            pl.BlockSpec((chunk, 1), lambda i: (before(i), 0)),
        ] + [held((features, block))] * peers,
        out_specs=[
            pl.BlockSpec((chunk, 1), lambda i: (before(i), 0)),
            pl.BlockSpec((2, chunk, table_rows), lambda i: (0, before(i), 0)),
            held((3 * features, table_rows)),
        ],
        scratch_shapes=[pltpu.VMEM((2, chunk, table_rows), F32)],
    )(live, rows, counts, edge_target, *blocks)


def loss_row_kernel(loss_ref, out_ref):
    edges = loss_ref.shape[0]
    out_ref[...] = jnp.broadcast_to(loss_ref[...], (edges, LANES)).T[:1]


def loss_row(loss):
    edges = loss.shape[0]
    return kernel_call(
        loss_row_kernel, shape((1, edges)), edges * LANES, 4 * edges * LANES,
        in_specs=[VMEM], out_specs=VMEM,
    )(loss)


def table_grad_kernel(columns_ref, grad_ref, *outs):
    step = pl.program_id(0)
    block = outs[0].shape[1]
    result = (
        dot(columns_ref[0], grad_ref[0])
        + dot(columns_ref[0], grad_ref[1])
        + dot(columns_ref[1], grad_ref[0])
    )
    for pair in range(len(outs) // 2):
        @pl.when(step == pair)
        def _():
            outs[2 * pair][...] = result[:, :block]
            outs[2 * pair + 1][...] = result[:, block:]


def table_grads(columns, grad, block, first, count):
    _, features, edges = columns.shape
    return kernel_call(
        table_grad_kernel, [shape((features, block))] * count,
        6 * features * count * block * edges, 4 * edges * (features + count * block),
        grid=(count // 2,),
        in_specs=[
            held((2, features, edges)),
            pl.BlockSpec((2, edges, 2 * block), lambda i: (0, 0, first // 2 + i)),
        ],
        out_specs=[held((features, block))] * count,
    )(columns, grad)


def relation_grad_kernel(
    steps, me_ref, table_ref, grad_ref, heads_ref, rels_ref, edge_rel_ref, source_ref, *refs
):
    outs, lines, total = refs[:-2], refs[-2], refs[-1]
    groups = len(outs) // 2
    half, width = outs[0].shape
    step = pl.program_id(0)
    features, chunk = heads_ref.shape
    tile = total.shape[2]

    @pl.when(step < steps)
    def _():
        hi, lo = table_ref[:features], table_ref[features:2 * features]
        query_grad = dot_nt(hi, grad_ref[0]) + dot_nt(hi, grad_ref[1]) + dot_nt(lo, grad_ref[0])
        source_ref[0], source_ref[1] = split2(conj_product(query_grad, rels_ref[...]))
        lines[step] = jnp.concatenate(split2(conj_product(query_grad, heads_ref[...])), axis=1)

    @pl.when(step >= steps)
    def _():
        part = None
        for i in range(steps):
            slots = edge_rel_ref[i * chunk:(i + 1) * chunk, :] - (step - steps) * tile
            hot = columns_hot(slots, tile)
            term = dot(lines[i, :, :chunk], hot) + dot(lines[i, :, chunk:], hot)
            part = term if part is None else part + term
        total[step - steps] = part

    @pl.when(step == pl.num_programs(0) - 1)
    def _():
        group, core = me_ref[0], me_ref[1]
        for j in range(groups):
            for at in range(0, width, LANES):
                start = (group ^ j) * width + at
                rows = total.at[start // tile, :, pl.ds(pl.multiple_of(start % tile, LANES), LANES)]
                outs[j][:, at:at + LANES] = rows[pl.ds(pl.multiple_of(core * half, 8), half), :]
                outs[groups + j][:, at:at + LANES] = rows[
                    pl.ds(pl.multiple_of((1 - core) * half, 8), half), :
                ]


def relation_grads(me, table, grad, heads, rels, edge_relation, groups, width):
    features, edges = heads.shape
    table_rows = table.shape[1]
    chunk = CHUNK
    steps = edges // chunk
    tile = math.gcd(groups * width, WIDE)
    tiles = groups * width // tile

    def now(i):
        return jnp.minimum(i, steps - 1)

    return kernel_call(
        functools.partial(relation_grad_kernel, steps),
        [shape((2, features, edges), BF16)] + [shape((features // 2, width))] * (2 * groups),
        10 * features * table_rows * edges, 30 * features * edges,
        grid=(steps + tiles,),
        in_specs=[
            SMEM,
            held((3 * features, table_rows)),
            pl.BlockSpec((2, chunk, table_rows), lambda i: (0, now(i), 0)),
            pl.BlockSpec((features, chunk), lambda i: (0, now(i))),
            pl.BlockSpec((features, chunk), lambda i: (0, now(i))),
            held((edges, 1)),
        ],
        out_specs=[pl.BlockSpec((2, features, chunk), lambda i: (0, 0, now(i)))]
        + [held((features // 2, width))] * (2 * groups),
        scratch_shapes=[
            pltpu.VMEM((steps, features, 2 * chunk), BF16),
            pltpu.VMEM((tiles, features, tile), F32),
        ],
    )(me, table, grad, heads, rels, edge_relation)


def source_grad_kernel(first, rows_ref, edge_source_ref, *outs):
    step = pl.program_id(0)
    block = outs[0].shape[1]
    hot = columns_hot(edge_source_ref[...] - (first * block + step * 2 * block), 2 * block)
    result = dot(rows_ref[0], hot) + dot(rows_ref[1], hot)
    for pair in range(len(outs) // 2):
        @pl.when(step == pair)
        def _():
            outs[2 * pair][...] = result[:, :block]
            outs[2 * pair + 1][...] = result[:, block:]


def source_grads(rows, edge_source, block, first, count):
    _, features, edges = rows.shape
    return kernel_call(
        functools.partial(source_grad_kernel, first), [shape((features, block))] * count,
        4 * features * count * block * edges, 4 * features * (edges + count * block),
        grid=(count // 2,),
        in_specs=[held((2, features, edges)), held((edges, 1))],
        out_specs=[held((features, block))] * count,
    )(rows, edge_source)


def put_back(blocks, hot):
    hi, lo = split2(jnp.concatenate([ref[...] for ref in blocks], axis=1))
    return dot(hi, hot) + dot(lo, hot)


def target_home_kernel(hot_ref, source_hot_ref, own_ref, entity_ref, *refs):
    blocks, out_ref, entity_out_ref = refs[:-2], refs[-2], refs[-1]
    block = own_ref.shape[1]
    own_hot = source_hot_ref[source_hot_ref.shape[0] - block:, :]
    out_ref[...] = put_back(blocks, hot_ref[...]) + put_back([own_ref], own_hot)
    entity_out_ref[...] = entity_ref[...]


def target_home(hots, source_hots, own, entity, blocks):
    features, rows = entity.shape
    return kernel_call(
        target_home_kernel, [shape((features, rows))] * 2,
        4 * features * rows * hots.shape[0], 8 * features * hots.shape[0],
        in_specs=[VMEM] * (4 + len(blocks)), out_specs=[VMEM] * 2,
    )(hots, source_hots, own, entity, *blocks)


def adagrad(params, state, gradient):
    new_state = state + jnp.mean(gradient * gradient, axis=0, keepdims=True)
    return params - gradient * (learn_rate / jnp.sqrt(new_state))


def entity_kernel(other_ref, entity_ref, state_ref, hot_ref, *refs):
    blocks = refs[:-1]
    here = len(blocks) * blocks[0].shape[1]
    gradient = other_ref[...] + put_back(blocks, hot_ref[:here, :])
    refs[-1][...] = adagrad(entity_ref[...], state_ref[...], gradient)


def entity_update(hots, blocks, other, entity, state):
    features, rows = entity.shape
    return kernel_call(
        entity_kernel, shape((features, rows)),
        4 * features * rows * hots.shape[0], 8 * features * hots.shape[0],
        in_specs=[VMEM] * (4 + len(blocks)), out_specs=VMEM,
    )(other, entity, state, hots, *blocks)


def add_kernel(*refs):
    count = len(refs) // 3
    for i in range(count):
        refs[2 * count + i][...] = refs[i][...] + refs[count + i][...]


def added(ours, theirs):
    count = len(ours)
    dims = ours[0].shape
    return kernel_call(
        add_kernel, [shape(dims)] * count,
        count * dims[0] * dims[1], 12 * count * dims[0] * dims[1],
        in_specs=[VMEM] * (2 * count), out_specs=[VMEM] * count,
    )(*ours, *theirs)


def cut_kernel(me_ref, *refs):
    chips = me_ref.shape[0]
    terms, outs, whole = refs[:-1 - chips], refs[-1 - chips:-1], refs[-1]
    rows, width = outs[0].shape
    have = terms[0].shape[0]
    total = terms[0][...]
    for term in terms[1:]:
        total = total + term[...]
    whole[:have, :] = total
    if have < chips * rows:
        whole[have:, :] = jnp.zeros((chips * rows - have, width), F32)
    for k, out in enumerate(outs):
        out[...] = whole[pl.ds(pl.multiple_of(me_ref[k] * rows, 8), rows), :]


def cut_pieces(order, terms):
    chips = order.shape[0]
    half, width = terms[0].shape
    rows = pl.cdiv(half, 8 * chips) * 8
    return kernel_call(
        cut_kernel, [shape((rows, width))] * chips,
        len(terms) * half * width, 4 * (len(terms) + 1) * half * width,
        in_specs=[SMEM] + [VMEM] * len(terms), out_specs=[VMEM] * chips,
        scratch_shapes=[pltpu.VMEM((chips * rows, width), F32)],
    )(order, *terms)


def sum_kernel(*refs):
    total = refs[0][...]
    for ref in refs[1:-1]:
        total = total + ref[...]
    refs[-1][...] = total


def sum_pieces(pieces):
    rows, width = pieces[0].shape
    return kernel_call(
        sum_kernel, shape((rows, width)),
        len(pieces) * rows * width, 4 * (len(pieces) + 1) * rows * width,
        in_specs=[VMEM] * len(pieces), out_specs=VMEM,
    )(*pieces)


def join_kernel(me_ref, *refs):
    pieces, out_ref, whole = refs[:-2], refs[-2], refs[-1]
    rows = pieces[0].shape[0]
    for k, piece in enumerate(pieces):
        whole[pl.ds(pl.multiple_of(me_ref[k] * rows, 8), rows), :] = piece[...]
    out_ref[...] = whole[:out_ref.shape[0], :]


def join_pieces(order, pieces, half):
    rows, width = pieces[0].shape
    return kernel_call(
        join_kernel, shape((half, width)),
        half * width, 8 * half * width,
        in_specs=[SMEM] + [VMEM] * len(pieces), out_specs=VMEM,
        scratch_shapes=[pltpu.VMEM((len(pieces) * rows, width), F32)],
    )(order, *pieces)


def relation_update_kernel(me_ref, relation_ref, state_ref, *refs):
    parts, out_ref, total = refs[:-2], refs[-2], refs[-1]
    groups = len(parts) // 2
    half, width = parts[0].shape
    group, core = me_ref[0], me_ref[1]
    for j in range(groups):
        at = pl.ds(pl.multiple_of((group ^ j) * width, LANES), width)
        total[pl.ds(pl.multiple_of(core * half, 8), half), at] = parts[j][...]
        total[pl.ds(pl.multiple_of((1 - core) * half, 8), half), at] = parts[groups + j][...]
    gradient = total[:, :out_ref.shape[1]]
    out_ref[...] = adagrad(relation_ref[...], state_ref[...], gradient)


def relation_update(me, relation, state, parts):
    features, count = relation.shape
    _, width = parts[0].shape
    groups = len(parts) // 2
    return kernel_call(
        relation_update_kernel, shape((features, count)),
        8 * features * count, 12 * features * count,
        in_specs=[SMEM] + [VMEM] * (2 + len(parts)), out_specs=VMEM,
        scratch_shapes=[pltpu.VMEM((features, groups * width), F32)],
    )(me, relation, state, *parts)


def sent_on(value, hop, peers):
    return lax.ppermute(value, "shard", [(i, partner(i, hop, peers, 1)) for i in range(peers)])


def sent_across(value, hop, peers, groups, by):
    pairs = [
        (g * peers + i, (g + by) % groups * peers + partner(i, hop, peers, 1))
        for g in range(groups)
        for i in range(peers)
    ]
    return lax.ppermute(value, ("group", "shard"), pairs)


def sent_group(value, bit, groups):
    return lax.ppermute(value, "group", [(g, g ^ bit) for g in range(groups)])


def relation_sum(kept, sent, peers, groups, chip):
    chips = peers // 2
    half = kept[0].shape[0]
    other_core = (0, 1)
    sent = [sent_on(b, other_core, peers) for b in sent]
    mine = added(kept, sent)
    terms = [mine[0]] + [sent_group(mine[j], j, groups) for j in range(1, groups)]
    ahead = (chip + jnp.arange(chips, dtype=I32)) % chips
    behind = (chip - jnp.arange(chips, dtype=I32)) % chips
    pieces = cut_pieces(ahead, terms)
    pieces = [pieces[0]] + [sent_on(pieces[k], (k, 0), peers) for k in range(1, chips)]
    piece = sum_pieces(pieces)
    pieces = [piece] + [sent_on(piece, (k, 0), peers) for k in range(1, chips)]
    block = join_pieces(behind, pieces, half)
    blocks = [block] + [sent_group(block, j, groups) for j in range(1, groups)]
    return blocks + [sent_on(b, other_core, peers) for b in blocks]


def on_device(
    entity, entity_state, relation, relation_state, src_send, dst_send,
    edge_source, edge_relation, edge_target, neg_slots, edge_count,
):
    rows, _ = entity.shape
    relations = relation.shape[0]
    peers, block = src_send.shape[1:]
    groups = lax.axis_size("group")
    group = lax.axis_index("group").astype(I32)
    me = lax.axis_index("shard").astype(I32)
    width = pl.cdiv(relations, groups * LANES) * LANES
    entity_t, relation_t = entity.T, relation.T
    ways = hops(peers)
    order = jnp.stack([partner(me, hop, peers, 1) for hop in ways])
    here = jnp.stack([group, me % 2])

    def placed(slots):
        return places_of(me, slots // block, peers) * block + slots % block

    edge_source, edge_target = placed(edge_source), placed(edge_target)
    early = peers // 2
    sources = pick_blocks(order[:2], entity_t, src_send[0])
    sources += pick_blocks(order[2:], entity_t, src_send[0])
    sources = [
        sent_on(value, hop, peers) if hop != (0, 0) else value
        for value, hop in zip(sources, ways)
    ]
    targets = pick_blocks(order, entity_t, dst_send[0])
    targets = [sent_across(value, hop, peers, groups, -1) for value, hop in zip(targets, ways)]
    rels = relation_rows(relation_t, edge_relation.reshape(1, -1))
    counts = slot_counts(placed(neg_slots), peers * block)
    source_hots = home_hots(order, src_send[0], rows)
    target_hots = home_hots(order, dst_send[0], rows)
    heads, query_columns, query_lines = query_rows(sources, edge_source.reshape(1, -1), rels)
    loss, grad, table = score_spans(
        edge_count, targets, query_lines, counts, edge_target.reshape(-1, 1)
    )
    table_parts = table_grads(query_columns, grad, block, 0, early)
    table_parts += table_grads(query_columns, grad, block, early, peers - early)
    back = [(-hop[0], hop[1]) for hop in ways]
    home = []
    for value, hop in zip(table_parts, back):
        home.append(sent_across(value, hop, peers, groups, 1))
    source_lines, *halves = relation_grads(
        here, table, grad, heads, rels, edge_relation.reshape(-1, 1), groups, width
    )
    edge_source = edge_source.reshape(-1, 1)
    source_parts = source_grads(source_lines, edge_source, block, 0, 2)
    source_parts += source_grads(source_lines, edge_source, block, 2, peers - 2)
    returned = []
    for value, hop, way in zip(source_parts, back, ways):
        returned.append(sent_on(value, hop, peers) if way != (0, 0) else value)
    parts = relation_sum(halves[:groups], halves[groups:], peers, groups, me // 2)
    relation_new = relation_update(here, relation_t, relation_state.reshape(1, -1), parts)
    target_part, entity_t = target_home(target_hots, source_hots, returned[-1], entity_t, home)
    entity_new = entity_update(
        source_hots, returned[:-1], target_part, entity_t, entity_state.reshape(1, -1)
    )
    return entity_new.T, relation_new.T, loss_row(loss).reshape(-1)


def solution(mesh):
    both = ("group", "shard")
    return jax.shard_map(
        on_device,
        mesh=mesh,
        in_specs=(
            P(both, None), P(both), P(), P(), P(both, None, None), P(both, None, None),
            P(both), P(both), P(both), P(both, None), P(both),
        ),
        out_specs=(P(both, None), P(), P(both)),
        check_vma=False,
    )
```
